32 devices in a mesh: wide: 8 (over z, y), narrow: 4 (over x, core).
Axes of the slice: x: 2, y: 2, z: 4, core: 2. Of those that a mesh axis runs over, the one named last changes fastest.
Arguments:
- tokens: bfloat16 [32768, 768], P(('wide', 'narrow')), may hold values from -6 to 6
- grad_out: bfloat16 [32768, 768], P(('wide', 'narrow')), may hold values from -6 to 6
- routes: int32 [32768, 1], P(('wide', 'narrow')), may hold values from 0 to 7; in each aligned block of 1024 rows (0 to 1023, 1024 to 2047, ...) at most 256 rows name the same one
- group_counts: int32 [8], replicated, may hold values from 1 to 8, 32 in all
- group_weights: int32 [8], replicated, may hold values from 1 to 4
- norm1_gain: float32 [768], replicated, may hold values from 0.5 to 1.5
- norm1_bias: float32 [768], replicated, may hold values from -1.25 to 1.25
- w_query: bfloat16 [768, 768], replicated, may hold values from -0.4375 to 0.4375
- bias_query: float32 [768], replicated, may hold values from -3 to 3
- w_key: bfloat16 [768, 768], replicated, may hold values from -0.21875 to 0.21875
- w_value: bfloat16 [768, 768], replicated, may hold values from -0.21875 to 0.21875
- bias_value: float32 [768], replicated, may hold values from -1.75 to 1.75
- w_out: bfloat16 [768, 768], replicated, may hold values from -0.875 to 0.875
- bias_out: float32 [768], replicated, may hold values from -1.75 to 1.75
- norm2_gain: float32 [768], replicated, may hold values from 0.5 to 1.5
- norm2_bias: float32 [768], replicated, may hold values from -1.25 to 1.25
- router: bfloat16 [768, 8], replicated, may hold values from -0.21875 to 0.21875
- w_in: bfloat16 [8, 768, 3072], P('wide', None, 'narrow'), may hold values from -0.21875 to 0.21875
- bias_in: bfloat16 [8, 3072], P('wide', 'narrow'), may hold values from -1.75 to 1.75
- w_down: bfloat16 [8, 3072, 768], P('wide', 'narrow'), may hold values from -0.4375 to 0.4375
- bias_down: bfloat16 [8, 768], P('wide'), may hold values from -1.75 to 1.75
Outputs:
- block_out: bfloat16 [32768, 768], P(('wide', 'narrow'))
- balance_loss: float32 [], replicated
- grad_tokens: bfloat16 [32768, 768], P(('wide', 'narrow'))
- grad_norm1_gain: float32 [768], replicated
- grad_norm1_bias: float32 [768], replicated
- grad_w_query: float32 [768, 768], replicated
- grad_bias_query: float32 [768], replicated
- grad_w_key: float32 [768, 768], replicated
- grad_w_value: float32 [768, 768], replicated
- grad_bias_value: float32 [768], replicated
- grad_w_out: float32 [768, 768], replicated
- grad_bias_out: float32 [768], replicated
- grad_norm2_gain: float32 [768], replicated
- grad_norm2_bias: float32 [768], replicated
- grad_router: float32 [768, 8], replicated
- grad_w_in: float32 [8, 768, 3072], P('wide', None, 'narrow')
- grad_bias_in: float32 [8, 3072], P('wide', 'narrow')
- grad_w_down: float32 [8, 3072, 768], P('wide', 'narrow')
- grad_bias_down: float32 [8, 768], P('wide', 'narrow')
The draws below stay inside these ranges and needn't reach their ends.
Inputs may be any that keep to these rules, and one draw needn't show every extreme that they name: `routes`: among the 1024 tokens of one device at most 256 name the same expert, and in every draw some device has an expert named by exactly 256 of its tokens. The counts add up to 32; group g holds the next group_counts[g] sequences in order.
All inputs are finite; a program needn't handle non-finite values.
Results may differ from the reference program's by a relative error of at most 0.015.
Values may be sent and summed in bfloat16 or wider, within the bound.
No kernel may reach another device: no remote copies, remote signals or barrier semaphores. Data moves between devices by JAX's collectives and lax.ppermute only.
A program may use at most 384 MiB of HBM per device.

```python
import math
from functools import partial
import jax
import jax.numpy as jnp
import numpy as np
from jax import lax

D = 768
HEADS = 12
HEAD_DIM = 64
FF = 3072
SEQ_LEN = 1024
GROUPS = 8
EXPERTS = 8
TOK_DEV = 1024
TOKENS = 32768
SEQS = 32
CAP = 256
COUNT_MOST = 8
N_WIDE = 8
N_NARROW = 4


def with_ends(drawn, stream_key, smallest, high):
    longest = drawn.shape.index(max(drawn.shape))
    spots = []
    for shift in (0, 1):
        where = [jax.random.randint(jax.random.fold_in(stream_key, axis), (), 0, length) for axis, length in enumerate(drawn.shape)]
        where[longest] = (where[longest] + shift) % drawn.shape[longest]
        spots.append(tuple(where))
    return drawn.at[spots[0]].set(smallest).at[spots[1]].set(high)


def block_scale(rng, extent, cuts, low, top_value):
    def one(axis_at, blocks):
        heights = jax.random.uniform(jax.random.fold_in(jax.random.fold_in(rng, 6), axis_at), (blocks,), jnp.float32, low / len(cuts), top_value / len(cuts))
        return jnp.repeat(jnp.exp(heights), extent[axis_at] // blocks).reshape((-1,) + (1,) * (len(extent) - axis_at - 1))

    level = one(*cuts[0])
    for cut in cuts[1:]:
        level = level * one(*cut)
    return level


def length_profile(count, total, most, skew):
    loads = [(1 << 20) // math.isqrt(standing ** skew) + 1 for standing in range(2, count + 1)]
    spare, counts = total - most - (count - 1), [1] * (count - 1)
    while spare > 0:
        free = [i for i in range(count - 1) if counts[i] < most]
        mass, remaining = sum([loads[i] for i in free]), spare
        for i in free:
            more = min(most - counts[i], max(1, remaining * loads[i] // mass), spare)
            counts[i] = counts[i] + more
            spare = spare - more
    return np.array([most] + counts)


def uneven(own_key, count, total, reach, slope):
    if count == 2:
        one = jax.random.randint(own_key, (), max(1, total - reach), min(reach, total - 1) + 1)
        return jnp.stack([one, total - one])
    lengths = jnp.asarray(length_profile(count, total, reach, slope), jnp.int32)
    twos = (count - 1) // 2
    giver, sink = lengths[1:1 + 2 * twos:2], lengths[2:2 + 2 * twos:2]
    slack = jnp.minimum(giver - 1, reach - sink)
    moved = jax.random.randint(jax.random.fold_in(own_key, 1), (twos,), 0, 1 << 20) % (slack + 1)
    lengths = lengths.at[1:1 + 2 * twos:2].set(giver - moved).at[2:2 + 2 * twos:2].set(sink + moved)
    return lengths[jax.random.permutation(jax.random.fold_in(own_key, 2), count)]


def assign_block(key, own, number, rows, amount, top, reach, skew):
    order = jax.random.permutation(key, amount)
    crowded, ordinary = load_shares(amount, rows * top, reach, skew, True), load_shares(amount, rows * top, reach, skew, False)
    places = jnp.arange(amount)

    def named(tallies, offset_by):
        used = int((tallies > 0).sum())
        fixed = max(1, used // 4)
        passed = fixed + (places - fixed + offset_by * (used - fixed)) % max(1, amount - fixed)
        return jnp.zeros((amount,), jnp.int32).at[order[jnp.where(places < fixed, places, passed)]].set(jnp.asarray(tallies, jnp.int32))

    tallies = jnp.where(number % 4 == 0, named(crowded, number // 4), named(ordinary, number - number // 4 - 1))
    mixed = jax.random.permutation(jax.random.fold_in(own, 3), amount)
    source_of, receiver = mixed[0:amount // 2 * 2:2], mixed[1:amount // 2 * 2:2]
    margin = jnp.minimum(tallies[source_of] - 1, reach - tallies[receiver]) // 2
    margin = jnp.where((source_of == order[0]) | (receiver == order[0]) | (tallies[receiver] == 0), 0, jnp.maximum(margin, 0))
    passed = jax.random.randint(jax.random.fold_in(own, 4), (amount // 2,), 0, 1 << 20) % (margin + 1)
    tallies = tallies.at[source_of].add(-passed).at[receiver].add(passed)
    labels = jnp.searchsorted(jnp.cumsum(tallies), jnp.arange(rows * top), side="right").astype(jnp.int32)
    listing = labels.reshape(top, rows).T
    listing = listing[jax.random.permutation(jax.random.fold_in(own, 1), rows)]
    offset_by = jax.random.randint(jax.random.fold_in(own, 2), (rows, 1), 0, top)
    return jnp.take_along_axis(listing, (jnp.arange(top)[None, :] + offset_by) % top, axis=1)


def load_shares(count, total, most, skew, full):
    loads = [(1 << 20) // math.isqrt(standing ** skew) + 1 for standing in range(1, count + 1)]
    largest = most if full else min(most, max(-(-total // count), total * loads[0] // sum(loads)))
    least = 1 if total - largest >= count - 1 else 0
    holding, rest = [largest] + [least] * (count - 1), total - largest - least * (count - 1)
    while rest > 0:
        movable = [i for i in range(1, count) if holding[i] < largest] or [i for i in range(1, count) if holding[i] < most]
        mass, remaining = sum([loads[i] for i in movable]), rest
        for i in movable:
            extra = min(most - holding[i], max(1, remaining * loads[i] // mass), rest)
            holding[i] = holding[i] + extra
            rest = rest - extra
    return np.array(holding)


def scatter_about(stream_key, shape, deviation, limit, pieces=(), kind=jnp.bfloat16):
    array = jax.random.normal(stream_key, shape, jnp.float32) * deviation
    if len(pieces) > 0:
        array = block_scale(stream_key, shape, pieces, -0.22, 0.18) * array
    return jnp.clip(array, min=-limit, max=limit).astype(kind)


def setup_inputs(seed: int = 0) -> dict:
    splits = jax.random.split(jax.random.key(seed), 22)
    tokens = scatter_about(splits[0], (TOKENS, D), 1.0, 6.0, ((0, 32),))
    grad_out = scatter_about(splits[1], (TOKENS, D), 1.0, 6.0, ((0, 32),))
    routes_keys = jax.random.split(jax.random.fold_in(splits[2], 1), TOKENS // TOK_DEV)
    routes_turns = jax.random.permutation(jax.random.fold_in(splits[2], 3), TOKENS // TOK_DEV)
    routes = jax.vmap(lambda own, number: assign_block(jax.random.fold_in(splits[2], 2), own, number, TOK_DEV, EXPERTS, 1, CAP, 2))(routes_keys, routes_turns).reshape((TOKENS, 1))
    group_counts = uneven(splits[3], GROUPS, SEQS, COUNT_MOST, 2).astype(jnp.int32)
    group_weights = with_ends(jax.random.randint(splits[4], (GROUPS,), 1, 5), jax.random.fold_in(splits[4], 1), 1, 4).astype(jnp.int32)
    norm1_gain = jnp.clip(1.0 + 0.1 * jax.random.normal(splits[5], (D,), jnp.float32), 0.5, 1.5)
    norm1_bias = scatter_about(splits[6], (D,), 0.2, 1.25, (), jnp.float32)
    w_query = scatter_about(splits[7], (D, D), (D // 4) ** -0.5, 0.4375)
    bias_query = scatter_about(splits[8], (D,), 0.5, 3.0, (), jnp.float32)
    w_key = scatter_about(splits[9], (D, D), D ** -0.5, 0.21875)
    w_value = scatter_about(splits[10], (D, D), D ** -0.5, 0.21875)
    bias_value = scatter_about(splits[11], (D,), 0.3, 1.75, (), jnp.float32)
    w_out = scatter_about(splits[12], (D, D), (D // 16) ** -0.5, 0.875)
    bias_out = scatter_about(splits[13], (D,), 0.3, 1.75, (), jnp.float32)
    norm2_gain = jnp.clip(1.0 + 0.1 * jax.random.normal(splits[14], (D,), jnp.float32), 0.5, 1.5)
    norm2_bias = scatter_about(splits[15], (D,), 0.2, 1.25, (), jnp.float32)
    router = scatter_about(splits[16], (D, EXPERTS), D ** -0.5, 0.21875)
    w_in = scatter_about(splits[17], (EXPERTS, D, FF), D ** -0.5, 0.21875, ((0, 8), (2, 4)))
    bias_in = scatter_about(splits[18], (EXPERTS, FF), 0.3, 1.75, ((0, 8), (1, 4)))
    w_down = scatter_about(splits[19], (EXPERTS, FF, D), (FF // 16) ** -0.5, 0.4375, ((0, 8), (1, 4)))
    bias_down = scatter_about(splits[20], (EXPERTS, D), 0.3, 1.75, ((0, 8),))
    return dict(tokens=tokens, grad_out=grad_out, routes=routes, group_counts=group_counts, group_weights=group_weights, norm1_gain=norm1_gain, norm1_bias=norm1_bias, w_query=w_query, bias_query=bias_query, w_key=w_key, w_value=w_value, bias_value=bias_value, w_out=w_out, bias_out=bias_out, norm2_gain=norm2_gain, norm2_bias=norm2_bias, router=router, w_in=w_in, bias_in=bias_in, w_down=w_down, bias_down=bias_down)


EPS = 1e-05
BALANCE = 48.0
NEGATIVE = -1e+30
HIGHEST = lax.Precision.HIGHEST

@jax.custom_vjp
def low(v):
    return lax.optimization_barrier(v.astype(jnp.bfloat16)).astype(jnp.float32)

@jax.custom_vjp
def low_back(v):
    return v

def low_keep(v):
    return (low(v), None)

def low_pass(kept, grad):
    return (grad,)

def back_keep(v):
    return (v, None)

def back_low(kept, grad):
    return (low(grad),)
low.defvjp(low_keep, low_pass)
low_back.defvjp(back_keep, back_low)

def layer_norm(values, norm_gain, norm_shift):
    centred = values - lax.optimization_barrier(jnp.mean(values, axis=-1, keepdims=True))
    spread = lax.rsqrt(lax.optimization_barrier(jnp.mean(centred * centred, axis=-1, keepdims=True)) + EPS)
    return centred * spread * norm_gain + norm_shift

def project(left_side, right_side):
    return jnp.dot(left_side, right_side, precision=HIGHEST, preferred_element_type=jnp.float32)

def attend_group(params, group_block):
    norm1_gain, norm1_bias, w_query, bias_query, w_key, w_value, bias_value, w_out, bias_out = params
    seqs_here, length, model_width = group_block.shape
    flat_rows = group_block.reshape(seqs_here * length, model_width)
    normed = low(layer_norm(flat_rows, norm1_gain, norm1_bias))
    queries = low(low_back(project(normed, w_query) + bias_query))
    key_heads = low(low_back(project(normed, w_key)))
    values = low(low_back(project(normed, w_value) + bias_value))
    head_shape = (seqs_here, length, HEADS, HEAD_DIM)
    queries = queries.reshape(head_shape)
    key_heads = key_heads.reshape(head_shape)
    values = values.reshape(head_shape)
    scores = low_back(jnp.einsum('sqhe,skhe->shqk', queries, key_heads, precision=HIGHEST) * 0.125)
    row_ids = lax.broadcasted_iota(jnp.int32, (length, length), 0)
    col_ids = lax.broadcasted_iota(jnp.int32, (length, length), 1)
    scores = jnp.where(col_ids <= row_ids, scores, NEGATIVE)
    weights = low(jax.nn.softmax(scores, axis=-1))
    context = jnp.einsum('shqk,skhe->sqhe', weights, values, precision=HIGHEST)
    context = low(low_back(context.reshape(seqs_here * length, model_width)))
    branch = low_back(project(context, w_out) + bias_out)
    return (flat_rows + branch).reshape(group_block.shape)

def expert_block(operands):
    expert_rows, w_in, bias_in, w_down, bias_down = operands
    pre_act = low_back(project(expert_rows, w_in) + bias_in)
    activated = low(jax.nn.gelu(pre_act, approximate=False))
    return low(low_back(project(activated, w_down) + bias_down))

def forward(routes, tokens, norm1_gain, norm1_bias, w_query, bias_query, w_key, w_value, bias_value, w_out, bias_out, norm2_gain, norm2_bias, router, w_in, bias_in, w_down, bias_down):
    token_total = tokens.shape[0]
    groups_here = tokens.reshape(token_total // (4 * SEQ_LEN), 4, SEQ_LEN, D)
    params = (norm1_gain, norm1_bias, w_query, bias_query, w_key, w_value, bias_value, w_out, bias_out)
    checked = jax.checkpoint(attend_group)

    def scan_step(scan_carry, group_block):
        return (scan_carry, checked(params, group_block))
    _, hidden_groups = lax.scan(scan_step, jnp.zeros((), jnp.float32), groups_here)
    hidden = hidden_groups.reshape(token_total, D)
    moe_in = low(layer_norm(hidden, norm2_gain, norm2_bias))
    logits = low_back(project(moe_in, router))
    expert_ids = routes[:, 0].astype(jnp.int32)
    picked = expert_ids[:, None] == jnp.arange(EXPERTS, dtype=jnp.int32)[None, :]
    chosen = picked.astype(jnp.float32)
    gate_value = jax.nn.sigmoid(lax.optimization_barrier(jnp.sum(logits * chosen, axis=-1)))
    router_probs = jax.nn.softmax(logits, axis=-1)
    fraction = lax.optimization_barrier(jnp.sum(chosen, axis=0)) / token_total
    balance_loss = EXPERTS * jnp.sum(fraction * lax.optimization_barrier(jnp.mean(router_probs, axis=0)))
    rank_flags = picked.astype(jnp.int32)
    before = jnp.cumsum(rank_flags, axis=0, dtype=jnp.int32) - rank_flags
    position = lax.optimization_barrier(jnp.sum(before * rank_flags, axis=1)).astype(jnp.int32)
    room_rows = N_WIDE * N_NARROW * CAP
    buffer = jnp.zeros((EXPERTS, room_rows, D), jnp.float32).at[expert_ids, position].set(moe_in)
    buffer = low_back(buffer)
    checked_expert = jax.checkpoint(expert_block)
    outputs = lax.map(checked_expert, (buffer, w_in, bias_in, w_down, bias_down))
    returned = outputs[expert_ids, position]
    block_out = hidden + gate_value[:, None] * returned
    return (block_out, balance_loss)

def reference(tokens, grad_out, routes, group_counts, group_weights, norm1_gain, norm1_bias, w_query, bias_query, w_key, w_value, bias_value, w_out, bias_out, norm2_gain, norm2_bias, router, w_in, bias_in, w_down, bias_down):
    floats = tuple((item.astype(jnp.float32) for item in (tokens, norm1_gain, norm1_bias, w_query, bias_query, w_key, w_value, bias_value, w_out, bias_out, norm2_gain, norm2_bias, router, w_in, bias_in, w_down, bias_down)))
    primal_out, pullback = jax.vjp(partial(forward, routes), *floats)
    block_out, balance_loss = primal_out
    group_ends = jnp.cumsum(group_counts, dtype=jnp.int32)
    starts = group_ends - group_counts
    sequence = jnp.arange(TOKENS, dtype=jnp.int32) // SEQ_LEN
    member = ((sequence[:, None] >= starts[None, :]) & (sequence[:, None] < group_ends[None, :])).astype(jnp.float32)
    factor = group_weights.astype(jnp.float32) * SEQS / (GROUPS * group_counts.astype(jnp.float32))
    token_weight = lax.optimization_barrier(jnp.sum(member * factor[None, :], axis=1))
    upstream = token_weight[:, None] * grad_out.astype(jnp.float32)
    gradients = pullback((upstream, jnp.asarray(BALANCE * TOKENS, jnp.float32)))
    return (block_out.astype(jnp.bfloat16), balance_loss, gradients[0].astype(jnp.bfloat16), gradients[1], gradients[2], gradients[3], gradients[4], gradients[5], gradients[6], gradients[7], gradients[8], gradients[9], gradients[10], gradients[11], gradients[12], gradients[13], gradients[14], gradients[15], gradients[16])
```

```python
import functools
import jax
import jax.numpy as jnp
from jax import lax
from jax.experimental import pallas as pl
from jax.experimental.pallas import tpu as pltpu
from jax.sharding import PartitionSpec as P

HEADS = 12
HEAD_DIM = 64
SEQ_LEN = 1024
EPS = 1e-05
BALANCE = 48.0
NEGATIVE = -1e30
PAIR = 2 * HEAD_DIM
F32 = jnp.float32
BF16 = jnp.bfloat16
VMEM_LIMIT = 56 * 1024 * 1024
EXTRA = 8
ATTEND_CALLS = 2


def mm(left, right):
    return lax.dot_general(left, right, (((1,), (0,)), ((), ())), preferred_element_type=F32)


def mm_nt(left, right):
    return lax.dot_general(left, right, (((1,), (1,)), ((), ())), preferred_element_type=F32)


def mm_tn(left, right):
    return lax.dot_general(left, right, (((0,), (0,)), ((), ())), preferred_element_type=F32)


def cost(flops, nbytes, trans=0):
    return pl.CostEstimate(flops=int(flops), bytes_accessed=int(nbytes), transcendentals=int(trans))


def params(*semantics):
    return pltpu.CompilerParams(dimension_semantics=semantics, vmem_limit_bytes=VMEM_LIMIT)


def head_mask(block, head):
    lanes = lax.broadcasted_iota(jnp.int32, block.shape, 1)
    return jnp.where(lanes // HEAD_DIM == head, block, jnp.zeros_like(block))


def causal(scores, block):
    keys = scores.shape[0]
    first = lax.broadcasted_iota(jnp.int32, (block, block), 0)
    second = lax.broadcasted_iota(jnp.int32, (block, block), 1)
    last = jnp.where(first <= second, scores[keys - block :], NEGATIVE)
    if keys == block:
        return last
    return jnp.concatenate([scores[: keys - block], last], axis=0)


def attend_kernel(block, q_ref, k_ref, v_ref, context_ref, log_ref):
    rows = q_ref.shape[0]
    keys = k_ref[...]
    values_t = jnp.transpose(v_ref[...])
    for first in range(0, rows, block):
        span = first + block
        query = q_ref[first:span, :]
        parts = []
        for head in range(2):
            scores = causal(mm_nt(keys[:span], head_mask(query, head)), block)
            peak = jnp.max(scores, axis=0, keepdims=True)
            powers = jnp.exp(scores - peak)
            total = jnp.sum(powers, axis=0, keepdims=True)
            out = mm(values_t[head * HEAD_DIM : (head + 1) * HEAD_DIM, :span], powers.astype(BF16))
            parts.append(out / total)
            log_ref[0, head : head + 1, first:span] = peak + jnp.log(total)
        context_ref[first:span, :] = jnp.transpose(jnp.concatenate(parts, axis=0)).astype(BF16)


def attend(queries, keys, values, block=256):
    rows, width = queries.shape
    pairs = width // PAIR
    spec = pl.BlockSpec((rows, PAIR), lambda p: (0, p))
    return pl.pallas_call(
        functools.partial(attend_kernel, block),
        grid=(pairs,),
        in_specs=[spec, spec, spec],
        out_specs=[spec, pl.BlockSpec((1, 2, rows), lambda p: (p, 0, 0))],
        out_shape=[
            jax.ShapeDtypeStruct((rows, width), BF16),
            jax.ShapeDtypeStruct((pairs, 2, rows), F32),
        ],
        compiler_params=params("arbitrary"),
        cost_estimate=cost(4 * rows * rows * width * 2, rows * width * 8, pairs * 2 * rows * rows),
        name="attend",
    )(queries, keys, values)


def attend_back_kernel(block, q_ref, k_ref, v_ref, log_ref, g_ref, normed_ref,
                       dq_ref, dk_ref, dv_ref, packed_ref, sums_ref, dq_acc, dk_acc, dv_acc):
    rows = q_ref.shape[0]
    keys = k_ref[...]
    values = v_ref[...]
    keys_t = jnp.transpose(keys)
    for first in reversed(range(0, rows, block)):
        span = first + block
        query = q_ref[first:span, :]
        grad = g_ref[first:span, :]
        grad_query, probs_both, scores_both, query_both, grad_both = [], [], [], [], []
        for head in range(2):
            query_h = head_mask(query, head)
            grad_h = head_mask(grad, head)
            scores = causal(mm_nt(keys[:span], query_h), block)
            probs = jnp.exp(scores - log_ref[0, head : head + 1, first:span])
            grad_probs = mm_nt(values[:span], grad_h)
            inner = jnp.sum(probs * grad_probs, axis=0, keepdims=True)
            grad_scores = (probs * (grad_probs - inner)).astype(BF16)
            grad_query.append(mm(keys_t[head * HEAD_DIM : (head + 1) * HEAD_DIM, :span], grad_scores))
            probs_both.append(probs.astype(BF16))
            scores_both.append(grad_scores)
            query_both.append(query_h)
            grad_both.append(grad_h)
        dv = mm(jnp.concatenate(probs_both, axis=1), jnp.concatenate(grad_both, axis=0))
        dk = mm(jnp.concatenate(scores_both, axis=1), jnp.concatenate(query_both, axis=0))
        if span == rows:
            dv_acc[...] = dv
            dk_acc[...] = dk
        else:
            dv_acc[:span, :] += dv
            dk_acc[:span, :] += dk
        dq = jnp.transpose(jnp.concatenate(grad_query, axis=0)) * 0.125
        dq_acc[first:span, :] = dq.astype(BF16)
    dq = dq_acc[...]
    dk = dk_acc[...].astype(BF16)
    dv = dv_acc[...].astype(BF16)
    dq_ref[...] = dq
    dk_ref[...] = dk
    dv_ref[...] = dv
    normed = normed_ref[...]
    packed_ref[:, : 2 * PAIR] = mm(normed, jnp.concatenate([dq, dk], axis=1)).astype(BF16)
    packed_ref[:, 2 * PAIR :] = mm(normed, dv).astype(BF16)
    sums_ref[...] = jnp.concatenate(
        [
            jnp.sum(dq.astype(F32), axis=0, keepdims=True),
            jnp.sum(dv.astype(F32), axis=0, keepdims=True),
            jnp.zeros((6, PAIR), F32),
        ],
        axis=0,
    )


def attend_back(queries, keys, values, logs, grad_context, normed_t, start, pairs, block=256):
    rows, width = queries.shape
    spec = pl.BlockSpec((rows, PAIR), lambda p: (0, p + start))
    out_spec = pl.BlockSpec((rows, PAIR), lambda p: (0, p))
    return pl.pallas_call(
        functools.partial(attend_back_kernel, block),
        grid=(pairs,),
        in_specs=[
            spec,
            spec,
            spec,
            pl.BlockSpec((1, 2, rows), lambda p: (p + start, 0, 0)),
            spec,
            pl.BlockSpec((width, rows), lambda p: (0, 0)),
        ],
        out_specs=[
            out_spec,
            out_spec,
            out_spec,
            pl.BlockSpec((width, 3 * PAIR), lambda p: (0, p)),
            pl.BlockSpec((8, PAIR), lambda p: (0, p)),
        ],
        out_shape=[jax.ShapeDtypeStruct((rows, pairs * PAIR), BF16)] * 3
        + [
            jax.ShapeDtypeStruct((width, 3 * pairs * PAIR), BF16),
            jax.ShapeDtypeStruct((8, pairs * PAIR), F32),
        ],
        scratch_shapes=[
            pltpu.VMEM((rows, PAIR), BF16),
            pltpu.VMEM((rows, PAIR), F32),
            pltpu.VMEM((rows, PAIR), F32),
        ],
        compiler_params=params("arbitrary"),
        cost_estimate=cost(rows * PAIR, rows * PAIR),
        name="attend_back",
    )(queries, keys, values, logs, grad_context, normed_t)


def normalise(values):
    centred = values - jnp.mean(values, axis=-1, keepdims=True)
    spread = lax.rsqrt(jnp.mean(centred * centred, axis=-1, keepdims=True) + EPS)
    return centred * spread, spread


def normalise_back(grad, unit, spread, gain):
    scaled = grad * gain
    mean = jnp.mean(scaled, axis=-1, keepdims=True)
    tilt = jnp.mean(scaled * unit, axis=-1, keepdims=True)
    return spread * (scaled - mean - unit * tilt)


def pieces(values):
    high = values.astype(BF16)
    rest = values - high.astype(F32)
    middle = rest.astype(BF16)
    low = (rest - middle.astype(F32)).astype(BF16)
    fill = jnp.zeros((5, values.shape[1]), F32)
    stacked = jnp.concatenate(
        [high.astype(F32), middle.astype(F32), low.astype(F32), fill], axis=0
    )
    return stacked.astype(BF16)


def join(parts):
    return parts[0:1] + parts[1:2] + parts[2:3]


def column(row):
    return jnp.transpose(jnp.broadcast_to(row, (8, row.shape[1])))[:, 0:1]


def gate_row(logits, picked):
    return jax.nn.sigmoid(jnp.sum(jnp.where(picked, logits, 0.0), axis=0, keepdims=True))


def picked_rows(ids, experts):
    return lax.broadcasted_iota(jnp.int32, (experts, ids.shape[1]), 0) == ids


def one_hot_rows(slots, first, count):
    places = lax.broadcasted_iota(jnp.int32, (count, slots.shape[1]), 0) + first
    return (places == slots).astype(F32).astype(BF16)


def one_hot_columns(slots, first, count):
    places = lax.broadcasted_iota(jnp.int32, (slots.shape[0], count), 1) + first
    return (places == slots).astype(F32).astype(BF16)


def route_kernel(experts, capacity, row_ref, col_ref, grad_ref, slots_ref, columns_ref, out_ref, count_row):
    step = pl.program_id(0)
    rows = row_ref.shape[1]
    width = grad_ref.shape[1]
    half = capacity // 2

    @pl.when(step == 0)
    def _():
        first = lax.broadcasted_iota(jnp.int32, (rows, rows), 0)
        second = lax.broadcasted_iota(jnp.int32, (rows, rows), 1)
        ids = row_ref[...]
        picked = picked_rows(ids, experts).astype(F32)
        before = mm(picked.astype(BF16), (first < second).astype(F32).astype(BF16))
        place = jnp.sum(before * picked, axis=0, keepdims=True).astype(jnp.int32)
        slots_ref[...] = ids * capacity + place
        ids = col_ref[...]
        picked = (lax.broadcasted_iota(jnp.int32, (rows, 128), 1) == ids).astype(F32)
        before = mm((second < first).astype(F32).astype(BF16), picked.astype(BF16))
        place = jnp.sum(before * picked, axis=1, keepdims=True).astype(jnp.int32)
        late = experts * half + ids * (half + EXTRA) + place - half
        columns_ref[:, 0:1] = jnp.where(place < half, ids * half + place, late)
        columns_ref[:, 1:2] = ids * capacity + place
        count_row[...] = jnp.zeros_like(count_row)
        count_row[0:1, 0:128] = jnp.sum(picked, axis=0, keepdims=True)

    chosen = one_hot_rows(slots_ref[...], step * capacity, capacity)
    out_ref[0, :capacity, :] = mm(chosen, grad_ref[...]).astype(BF16)
    out_ref[0, capacity:, :] = count_row[...].astype(BF16)


def route(routes, grad_out, experts, capacity):
    rows, width = grad_out.shape
    whole = lambda e: (0, 0)
    return pl.pallas_call(
        functools.partial(route_kernel, experts, capacity),
        grid=(experts,),
        in_specs=[
            pl.BlockSpec((1, rows), whole),
            pl.BlockSpec((rows, 1), whole),
            pl.BlockSpec((rows, width), whole),
        ],
        out_specs=[
            pl.BlockSpec((1, rows), whole),
            pl.BlockSpec((rows, 2), whole),
            pl.BlockSpec((1, capacity + EXTRA, width), lambda e: (e, 0, 0)),
        ],
        out_shape=[
            jax.ShapeDtypeStruct((1, rows), jnp.int32),
            jax.ShapeDtypeStruct((rows, 2), jnp.int32),
            jax.ShapeDtypeStruct((experts, capacity + EXTRA, width), BF16),
        ],
        scratch_shapes=[pltpu.VMEM((EXTRA, width), F32)],
        compiler_params=params("arbitrary"),
        cost_estimate=cost(2 * experts * capacity * rows * width, 6 * rows * width),
        name="route",
    )(routes.reshape(1, rows), routes, grad_out)


def project_kernel(tokens_ref, gain_ref, shift_ref, wq_ref, bq_ref, wk_ref, wv_ref, bv_ref,
                   normed_ref, q_ref, k_ref, v_ref):
    unit, _ = normalise(tokens_ref[...].astype(F32))
    normed = (unit * gain_ref[...] + shift_ref[...]).astype(BF16)
    normed_ref[...] = jnp.transpose(normed)
    q_ref[...] = ((mm(normed, wq_ref[...]) + bq_ref[...]) * 0.125).astype(BF16)
    k_ref[...] = mm(normed, wk_ref[...]).astype(BF16)
    v_ref[...] = (mm(normed, wv_ref[...]) + bv_ref[...]).astype(BF16)


def project(tokens, gain, shift, w_query, bias_query, w_key, w_value, bias_value, tile=256):
    rows, width = tokens.shape
    row_spec = pl.BlockSpec((tile, width), lambda t: (t, 0))
    vector = pl.BlockSpec((1, width), lambda t: (0, 0))
    square = pl.BlockSpec((width, width), lambda t: (0, 0))
    return pl.pallas_call(
        project_kernel,
        grid=(rows // tile,),
        in_specs=[row_spec, vector, vector, square, vector, square, square, vector],
        out_specs=[pl.BlockSpec((width, tile), lambda t: (0, t))] + [row_spec] * 3,
        out_shape=[jax.ShapeDtypeStruct((width, rows), BF16)]
        + [jax.ShapeDtypeStruct((rows, width), BF16)] * 3,
        compiler_params=params("arbitrary"),
        cost_estimate=cost(6 * rows * width * width, 10 * rows * width + 6 * width * width),
        name="project",
    )(tokens, gain, shift, w_query, bias_query, w_key, w_value, bias_value)


def settle_kernel(context_ref, tokens_ref, w_out_ref, bias_ref, gain_ref, shift_ref, router_ref,
                  hidden_ref, moe_ref, logits_ref):
    hidden = tokens_ref[...].astype(F32) + mm(context_ref[...], w_out_ref[...]) + bias_ref[...]
    unit, _ = normalise(hidden)
    moe_in = (unit * gain_ref[...] + shift_ref[...]).astype(BF16)
    hidden_ref[...] = hidden
    moe_ref[...] = moe_in
    logits_ref[...] = mm_nt(router_ref[...], moe_in)


def settle(context, tokens, w_out, bias_out, gain, shift, router_rows, tile=256):
    rows, width = tokens.shape
    experts = router_rows.shape[0]
    row_spec = pl.BlockSpec((tile, width), lambda t: (t, 0))
    vector = pl.BlockSpec((1, width), lambda t: (0, 0))
    return pl.pallas_call(
        settle_kernel,
        grid=(rows // tile,),
        in_specs=[
            row_spec,
            row_spec,
            pl.BlockSpec((width, width), lambda t: (0, 0)),
            vector,
            vector,
            vector,
            pl.BlockSpec((experts, width), lambda t: (0, 0)),
        ],
        out_specs=[row_spec, row_spec, pl.BlockSpec((experts, tile), lambda t: (0, t))],
        out_shape=[
            jax.ShapeDtypeStruct((rows, width), F32),
            jax.ShapeDtypeStruct((rows, width), BF16),
            jax.ShapeDtypeStruct((experts, rows), F32),
        ],
        compiler_params=params("arbitrary"),
        cost_estimate=cost(2 * rows * width * width, 10 * rows * width + 2 * width * width),
        name="settle",
    )(context, tokens, w_out, bias_out, gain, shift, router_rows)


def dispatch_kernel(weight_ref, slots_ref, ids_ref, logits_ref, moe_ref, first_ref, second_ref, parts):
    step = pl.program_id(0)
    experts = logits_ref.shape[0]
    half = first_ref.shape[1]

    @pl.when(step == 0)
    def _():
        gate = gate_row(logits_ref[...], picked_rows(ids_ref[...], experts))
        parts[...] = pieces(gate * weight_ref[0, 0])

    chosen = one_hot_rows(slots_ref[...], step * 2 * half, 2 * half)
    rows = mm(chosen, moe_ref[...]).astype(BF16)
    first_ref[0] = rows[:half]
    second_ref[0, :half, :] = rows[half:]
    second_ref[0, half:, :] = jnp.zeros((EXTRA, rows.shape[1]), BF16)
    second_ref[0, half:, 0 : 2 * half] = mm_nt(parts[...], chosen).astype(BF16)


def dispatch(weight, slots, ids, logits, moe_in, capacity):
    rows, width = moe_in.shape
    experts = logits.shape[0]
    half = capacity // 2
    whole = lambda e: (0, 0)
    return pl.pallas_call(
        dispatch_kernel,
        grid=(experts,),
        in_specs=[
            pl.BlockSpec(memory_space=pltpu.SMEM),
            pl.BlockSpec((1, rows), whole),
            pl.BlockSpec((1, rows), whole),
            pl.BlockSpec((experts, rows), whole),
            pl.BlockSpec((rows, width), whole),
        ],
        out_specs=[
            pl.BlockSpec((1, half, width), lambda e: (e, 0, 0)),
            pl.BlockSpec((1, half + EXTRA, width), lambda e: (e, 0, 0)),
        ],
        out_shape=[
            jax.ShapeDtypeStruct((experts, half, width), BF16),
            jax.ShapeDtypeStruct((experts, half + EXTRA, width), BF16),
        ],
        scratch_shapes=[pltpu.VMEM((8, rows), BF16)],
        compiler_params=params("arbitrary"),
        cost_estimate=cost(2 * experts * capacity * rows * width, 6 * rows * width),
        name="dispatch",
    )(weight, slots, ids, logits, moe_in)


def row_sum(values):
    ones = jnp.ones((8, values.shape[1]), BF16)
    high = values.astype(BF16)
    rest = values - high.astype(F32)
    middle = rest.astype(BF16)
    low = (rest - middle.astype(F32)).astype(BF16)
    return (mm_nt(ones, high) + mm_nt(ones, middle) + mm_nt(ones, low))[0:1]


def expert_kernel(steps, chunk, *refs):
    if chunk == 0:
        (x_ref, g_ref, w_in_ref, b_in_ref, w_down_ref, b_down_ref,
         act_ref, up_ref, out_ref, back_ref, dot_ref, back_acc, dot_acc, out_acc) = refs
    else:
        (x_ref, g_ref, w_in_ref, b_in_ref, w_down_ref, b_down_ref, _, _, _, earlier_ref,
         act_ref, up_ref, out_ref, back_ref, back_acc, dot_acc, out_acc) = refs
    part = pl.program_id(0)
    tile = pl.program_id(1)
    group, half, width = x_ref.shape
    rows = group * half
    x = x_ref[...].reshape(rows, width)
    g = g_ref[...].reshape(rows, width)
    w_in = w_in_ref[0]
    pre = mm(x, w_in) + b_in_ref[0].astype(F32)
    grad_act = mm_nt(g, w_down_ref[0])
    below = 0.5 + 0.5 * lax.erf(pre * 0.7071067811865476)
    act = pre * below
    slope = below + pre * (0.3989422804014327 * jnp.exp(-0.5 * pre * pre))
    up = (grad_act * slope).astype(BF16)
    rounded = act.astype(BF16)
    act_ref[0, 0] = rounded
    up_ref[0, 0] = up
    out = mm(rounded, w_down_ref[0])
    product = act * grad_act
    lanes = min(128, product.shape[1])
    folded = product[:, :lanes]
    for lane in range(lanes, product.shape[1], lanes):
        folded = folded + product[:, lane : lane + lanes]
    where = pl.ds(pl.multiple_of(tile * rows, rows), rows)
    back = mm_nt(up, w_in)

    @pl.when(part == 0)
    def _():
        biased = g.astype(F32) * b_down_ref[...].astype(F32)
        total = folded
        for lane in range(0, biased.shape[1], lanes):
            total = total + biased[:, lane : lane + lanes]
        back_acc[where, :] = back
        out_acc[where, :] = out + b_down_ref[...].astype(F32)
        dot_acc[where, :] = total

    @pl.when(part > 0)
    def _():
        back_acc[where, :] += back
        out_acc[where, :] += out
        dot_acc[where, :] += folded

    @pl.when(part == steps - 1)
    def _():
        out_ref[...] = out_acc[where, :].astype(BF16).reshape(group, half, width)
        back_ref[:, :half, :] = back_acc[where, :].astype(BF16).reshape(group, half, width)
        dots = dot_acc[where, :]
        for index in range(group):
            own = pieces(row_sum(dots[index * half : (index + 1) * half, :])).astype(F32)
            if chunk == 0:
                dot_ref[index] = own.astype(BF16)
            else:
                before = earlier_ref[index].astype(F32)
                extra = jnp.concatenate([own[0:3], before[0:3], own[6:8]], axis=0)
                back_ref[index, half:, :] = jnp.zeros((EXTRA, width), BF16)
                back_ref[index, half:, 0:half] = extra.astype(BF16)


def expert(x, g, w_in, b_in, w_down, b_down, chunk, earlier=()):
    sources, width = x.shape[0], x.shape[2]
    half = (g.shape[1] - EXTRA) // 2
    rows = sources * half
    parts, _, hidden = w_in.shape
    group = max(1, 256 // half)
    tile = group * half
    tiles = sources // group
    last = parts - 1
    late = lambda p, t: jnp.where(p == last, t, 0)
    wide_spec = pl.BlockSpec((1, 1, tile, hidden), lambda p, t: (p, chunk, t, 0))
    wide_shape = jax.ShapeDtypeStruct((parts, 2, rows, hidden), BF16)
    dot_shape = jax.ShapeDtypeStruct((sources, 8, half), BF16)
    dot_spec = pl.BlockSpec((group, 8, half), lambda p, t: (late(p, t), 0, 0))
    back_rows = half + EXTRA * chunk
    return pl.pallas_call(
        functools.partial(expert_kernel, parts, chunk),
        grid=(parts, tiles),
        in_specs=[
            pl.BlockSpec((group, half, width), lambda p, t: (t, 0, 0)),
            pl.BlockSpec((group, half, width), lambda p, t: (t, chunk, 0)),
            pl.BlockSpec((1, width, hidden), lambda p, t: (p, 0, 0)),
            pl.BlockSpec((1, 1, hidden), lambda p, t: (p, 0, 0)),
            pl.BlockSpec((1, hidden, width), lambda p, t: (p, 0, 0)),
            pl.BlockSpec((1, width), lambda p, t: (0, 0)),
        ]
        + ([pl.BlockSpec(memory_space=pl.ANY)] * 3 + [dot_spec] if chunk else []),
        out_specs=[
            wide_spec,
            wide_spec,
            pl.BlockSpec((group, half, width), lambda p, t: (late(p, t), chunk, 0)),
            pl.BlockSpec((group, back_rows, width), lambda p, t: (late(p, t), 0, 0)),
        ]
        + ([] if chunk else [dot_spec]),
        out_shape=[
            wide_shape,
            wide_shape,
            jax.ShapeDtypeStruct((sources, 2 * half, width), BF16),
            jax.ShapeDtypeStruct((sources, back_rows, width), BF16),
        ]
        + ([] if chunk else [dot_shape]),
        scratch_shapes=[
            pltpu.VMEM((rows, width), F32),
            pltpu.VMEM((rows, min(128, hidden)), F32),
            pltpu.VMEM((rows, width), F32),
        ],
        input_output_aliases={6: 0, 7: 1, 8: 2} if chunk else {},
        compiler_params=params("arbitrary", "arbitrary"),
        cost_estimate=cost(
            6 * rows * width * hidden * parts, rows * hidden * parts * 4, 2 * rows * hidden * parts
        ),
        name="expert",
    )(x, g, w_in, b_in, w_down, b_down, *earlier)


def weight_kernel(parts, x0_ref, x1_ref, g_ref, act_ref, up_ref, scale_ref,
                  grad_ref, down_acc, in_acc, bias_acc, bias_down_acc, flipped):
    part = pl.program_id(0)
    chunk = pl.program_id(1)
    sources, half, width = x0_ref.shape
    rows = sources * half
    hidden = act_ref.shape[3]
    scale = scale_ref[0]
    split = pieces(scale)
    g = g_ref[...].reshape(rows, width)

    def flip(values):
        return (jnp.transpose(values).astype(F32) * scale).astype(BF16)

    @pl.when((part == 0) & (chunk == 0))
    def _():
        flipped[0] = flip(x0_ref[...].reshape(rows, width))

    @pl.when((part == 0) & (chunk == 1))
    def _():
        flipped[1] = flip(x1_ref[...].reshape(rows, width))

    act = act_ref[0, 0]
    up = up_ref[0, 0]
    down = mm(flip(act), g)
    into = mm(flipped[chunk], up)
    bias_in = join(mm(split, up))

    @pl.when(chunk == 0)
    def _():
        down_acc[...] = down
        in_acc[...] = into
        bias_acc[...] = bias_in

    @pl.when(chunk == 1)
    def _():
        grad_ref[0, width : width + hidden, :] = (down_acc[...] + down).astype(BF16)
        grad_ref[0, :width, 0:hidden] = (in_acc[...] + into).astype(BF16)

    @pl.when(part == 0)
    def _():
        bias_down = join(mm(split, g))
        bias_down_acc[...] = jnp.where(chunk == 0, bias_down, bias_down_acc[...] + bias_down)

    @pl.when(chunk == 1)
    def _():
        first = width + hidden
        grad_ref[0, first:, :] = jnp.zeros((EXTRA, width), BF16)
        grad_ref[0, first : first + 1, 0:hidden] = (bias_acc[...] + bias_in).astype(BF16)
        grad_ref[0, first + 1 : first + 2, :] = bias_down_acc[...].astype(BF16)


def weight_grads(x0, x1, g, act, up, scale):
    sources, half, width = x0.shape
    parts, _, rows, hidden = act.shape
    wide_spec = pl.BlockSpec((1, 1, rows, hidden), lambda p, t: (p, t, 0, 0))
    return pl.pallas_call(
        functools.partial(weight_kernel, parts),
        grid=(parts, 2),
        in_specs=[
            pl.BlockSpec((sources, half, width), lambda p, t: (0, 0, 0)),
            pl.BlockSpec((sources, half, width), lambda p, t: (0, 0, 0)),
            pl.BlockSpec((sources, half, width), lambda p, t: (0, t, 0)),
            wide_spec,
            wide_spec,
            pl.BlockSpec((1, 1, rows), lambda p, t: (t, 0, 0)),
        ],
        out_specs=pl.BlockSpec((1, width + hidden + EXTRA, width), lambda p, t: (p, 0, 0)),
        out_shape=jax.ShapeDtypeStruct((parts, width + hidden + EXTRA, width), BF16),
        scratch_shapes=[
            pltpu.VMEM((hidden, width), F32),
            pltpu.VMEM((width, hidden), F32),
            pltpu.VMEM((1, hidden), F32),
            pltpu.VMEM((1, width), F32),
            pltpu.VMEM((2, width, rows), BF16),
        ],
        compiler_params=params("arbitrary", "arbitrary"),
        cost_estimate=cost(12 * rows * width * hidden * parts, rows * hidden * parts * 8),
        name="weight_grads",
    )(x0, x1, g, act, up, scale)


def combine_kernel(weight_ref, back0_ref, back1_ref, dots0_ref, dots1_ref, columns_ref, ids_ref, logits_ref, pull_ref,
                   hidden_ref, grad_ref, context_ref, moe_ref, w_out_ref, router_ref, gain_ref,
                   hid_grad_ref, con_grad_ref, out_grad_ref, sums_ref, router_grad_ref, probs_ref, out_acc):
    step = pl.program_id(0)
    experts = logits_ref.shape[0]
    count0 = back0_ref.shape[0]
    count1 = back1_ref.shape[0]
    weight = weight_ref[0, 0]
    columns = columns_ref[:, 0:1]
    chosen0 = one_hot_columns(columns, 0, count0)
    chosen1 = one_hot_columns(columns, count0, count1)
    rows = mm(chosen0, back0_ref[...]) + mm(chosen1, back1_ref[...])
    dots = join(mm_nt(dots0_ref[...], chosen0)) + join(mm_nt(dots1_ref[...], chosen1))
    logits = logits_ref[...]
    picked = picked_rows(ids_ref[...], experts)
    gate = gate_row(logits, picked)
    powers = jnp.exp(logits - jnp.max(logits, axis=0, keepdims=True))
    probs = powers / jnp.sum(powers, axis=0, keepdims=True)
    pull = pull_ref[...]
    slope = dots * weight * gate * (1.0 - gate)
    logit_grad = probs * (pull - jnp.sum(probs * pull, axis=0, keepdims=True))
    logit_grad = (logit_grad + jnp.where(picked, slope, 0.0)).astype(BF16)
    moe_grad = mm_tn(logit_grad, router_ref[...]) + rows * column(gate * weight)
    unit, spread = normalise(hidden_ref[...])
    hid_grad = weight * grad_ref[...].astype(F32) + normalise_back(
        moe_grad, unit, spread, gain_ref[...]
    )
    branch = hid_grad.astype(BF16)
    hid_grad_ref[...] = hid_grad
    con_grad_ref[...] = mm_nt(branch, w_out_ref[...]).astype(BF16)
    out_grad = mm_tn(context_ref[...], branch)
    router_grad = mm(logit_grad, moe_ref[...])
    prob_sum = jnp.sum(probs, axis=1, keepdims=True)
    sums = jnp.concatenate(
        [
            jnp.sum(moe_grad * unit, axis=0, keepdims=True),
            jnp.sum(moe_grad, axis=0, keepdims=True),
            jnp.sum(branch.astype(F32), axis=0, keepdims=True),
            jnp.zeros((5, unit.shape[1]), F32),
        ],
        axis=0,
    )

    @pl.when(step == 0)
    def _():
        out_acc[...] = out_grad
        router_grad_ref[...] = router_grad
        probs_ref[...] = prob_sum
        sums_ref[...] = sums

    @pl.when(step > 0)
    def _():
        out_acc[...] += out_grad
        router_grad_ref[...] += router_grad
        probs_ref[...] += prob_sum
        sums_ref[...] += sums

    @pl.when(step == pl.num_programs(0) - 1)
    def _():
        out_grad_ref[...] = out_acc[...].astype(BF16)


def combine(weight, back0, back1, dots0, dots1, columns, ids, logits, pull, hidden, grad_out, context, moe_in,
            w_out, router_rows, gain, tile=256):
    rows, width = hidden.shape
    experts = logits.shape[0]
    count = back0.shape[0]
    count1 = back1.shape[0]
    whole = lambda t: (0, 0)
    row_spec = pl.BlockSpec((tile, width), lambda t: (t, 0))
    square = pl.BlockSpec((width, width), whole)
    return pl.pallas_call(
        combine_kernel,
        grid=(rows // tile,),
        in_specs=[
            pl.BlockSpec(memory_space=pltpu.SMEM),
            pl.BlockSpec((count, width), whole),
            pl.BlockSpec((count1, width), whole),
            pl.BlockSpec((8, count), whole),
            pl.BlockSpec((8, count1), whole),
            pl.BlockSpec((tile, 2), lambda t: (t, 0)),
            pl.BlockSpec((1, tile), lambda t: (0, t)),
            pl.BlockSpec((experts, tile), lambda t: (0, t)),
            pl.BlockSpec((experts, 1), whole),
            row_spec,
            row_spec,
            row_spec,
            row_spec,
            square,
            pl.BlockSpec((experts, width), whole),
            pl.BlockSpec((1, width), whole),
        ],
        out_specs=[
            row_spec,
            row_spec,
            square,
            pl.BlockSpec((8, width), whole),
            pl.BlockSpec((experts, width), whole),
            pl.BlockSpec((experts, 1), whole),
        ],
        out_shape=[
            jax.ShapeDtypeStruct((rows, width), F32),
            jax.ShapeDtypeStruct((rows, width), BF16),
            jax.ShapeDtypeStruct((width, width), BF16),
            jax.ShapeDtypeStruct((8, width), F32),
            jax.ShapeDtypeStruct((experts, width), F32),
            jax.ShapeDtypeStruct((experts, 1), F32),
        ],
        scratch_shapes=[pltpu.VMEM((width, width), F32)],
        compiler_params=params("arbitrary"),
        cost_estimate=cost(rows * width, rows * width),
        name="combine",
    )(weight, back0, back1, dots0, dots1, columns, ids, logits, pull, hidden, grad_out, context, moe_in, w_out,
      router_rows, gain)


def close_kernel(count, *refs):
    grads = refs[: 3 * count]
    (tokens_ref, hid_grad_ref, gain_ref, wq_ref, wk_ref, wv_ref, tok_grad_ref, sums_ref) = refs[3 * count :]
    step = pl.program_id(0)
    width = tokens_ref.shape[1]
    norm_grad = None
    for index, weights in enumerate((wq_ref, wk_ref, wv_ref)):
        parts = [grads[3 * part + index][...] for part in range(count)]
        term = mm_nt(jnp.concatenate(parts, axis=1), weights[...])
        norm_grad = term if norm_grad is None else norm_grad + term
    unit, spread = normalise(tokens_ref[...].astype(F32))
    tok_grad = hid_grad_ref[...] + normalise_back(norm_grad, unit, spread, gain_ref[...])
    tok_grad_ref[...] = tok_grad.astype(BF16)
    sums = jnp.concatenate(
        [
            jnp.sum(norm_grad * unit, axis=0, keepdims=True),
            jnp.sum(norm_grad, axis=0, keepdims=True),
            jnp.zeros((6, width), F32),
        ],
        axis=0,
    )

    @pl.when(step == 0)
    def _():
        sums_ref[...] = sums

    @pl.when(step > 0)
    def _():
        sums_ref[...] += sums


def close(grads, tokens, hid_grad, gain, w_query, w_key, w_value, tile=256):
    rows, width = tokens.shape
    whole = lambda t: (0, 0)
    row_spec = pl.BlockSpec((tile, width), lambda t: (t, 0))
    square = pl.BlockSpec((width, width), whole)
    flat = [item for triple in grads for item in triple]
    return pl.pallas_call(
        functools.partial(close_kernel, len(grads)),
        grid=(rows // tile,),
        in_specs=[pl.BlockSpec((tile, item.shape[1]), lambda t: (t, 0)) for item in flat]
        + [row_spec, row_spec, pl.BlockSpec((1, width), whole), square, square, square],
        out_specs=[row_spec, pl.BlockSpec((8, width), whole)],
        out_shape=[
            jax.ShapeDtypeStruct((rows, width), BF16),
            jax.ShapeDtypeStruct((8, width), F32),
        ],
        compiler_params=params("arbitrary"),
        cost_estimate=cost(6 * rows * width * width, 16 * rows * width + 6 * width * width),
        name="close",
    )(*flat, tokens, hid_grad, gain, w_query, w_key, w_value)


def block_out_kernel(back_ref, columns_ref, ids_ref, logits_ref, hidden_ref, out_ref):
    chosen = one_hot_columns(columns_ref[:, 1:2], 0, back_ref.shape[0])
    rows = mm(chosen, back_ref[...])
    gate = gate_row(logits_ref[...], picked_rows(ids_ref[...], logits_ref.shape[0]))
    out_ref[...] = (hidden_ref[...] + column(gate) * rows).astype(BF16)


def block_output(back, columns, ids, logits, hidden, tile=256):
    rows, width = hidden.shape
    experts = logits.shape[0]
    count = back.shape[0]
    row_spec = pl.BlockSpec((tile, width), lambda t: (t, 0))
    return pl.pallas_call(
        block_out_kernel,
        grid=(rows // tile,),
        in_specs=[
            pl.BlockSpec((count, width), lambda t: (0, 0)),
            pl.BlockSpec((tile, 2), lambda t: (t, 0)),
            pl.BlockSpec((1, tile), lambda t: (0, t)),
            pl.BlockSpec((experts, tile), lambda t: (0, t)),
            row_spec,
        ],
        out_specs=row_spec,
        out_shape=jax.ShapeDtypeStruct((rows, width), BF16),
        compiler_params=params("arbitrary"),
        cost_estimate=cost(2 * rows * width * count, 6 * rows * width + 2 * count * width),
        name="block_output",
    )(back, columns, ids, logits, hidden)


def unpack_kernel(early_ref, late_ref, out_ref, *refs):
    width = out_ref.shape[1]
    out_ref[...] = early_ref[:, :width].astype(F32)
    place = 0
    for ref, first in ((early_ref, width), (late_ref, 0)):
        for base in range(first, ref.shape[1], 3 * PAIR):
            for index in range(3):
                lanes = ref[:, base + index * PAIR : base + (index + 1) * PAIR]
                refs[index][:, place : place + PAIR] = lanes.astype(F32)
            place += PAIR


def unpack(early, late, tile=256):
    rows = early.shape[0]
    width = (early.shape[1] + late.shape[1]) // 4
    spec = pl.BlockSpec((tile, width), lambda t: (t, 0))
    return pl.pallas_call(
        unpack_kernel,
        grid=(rows // tile,),
        in_specs=[
            pl.BlockSpec((tile, early.shape[1]), lambda t: (t, 0)),
            pl.BlockSpec((tile, late.shape[1]), lambda t: (t, 0)),
        ],
        out_specs=[spec] * 4,
        out_shape=[jax.ShapeDtypeStruct((rows, width), F32)] * 4,
        compiler_params=params("arbitrary"),
        cost_estimate=cost(rows * width, 24 * rows * width),
        name="unpack",
    )(early, late)


def swap(blocks, axis):
    return lax.all_to_all(blocks, axis, split_axis=0, concat_axis=0, tiled=True)


def after(value, *others):
    return lax.optimization_barrier((value,) + others)[0]


def trade(value, axis, bit):
    count = lax.axis_size(axis)
    return lax.ppermute(value, axis, [(place, place ^ bit) for place in range(count)])


def bits(axis):
    count, bit = lax.axis_size(axis), 1
    while bit < count:
        yield bit
        bit *= 2


def narrow_sum(value):
    for bit in bits("narrow"):
        value = value + trade(value, "narrow", bit)
    return value


def is_upper(axis, bit):
    return (lax.axis_index(axis) // bit) % 2


def halve(value, axis, bit):
    upper = is_upper(axis, bit)
    halves = value.reshape((2, value.shape[0] // 2) + value.shape[1:])
    mine = lax.dynamic_index_in_dim(halves, upper, 0, keepdims=False)
    other = lax.dynamic_index_in_dim(halves, 1 - upper, 0, keepdims=False)
    return (mine.astype(F32) + trade(other, axis, bit).astype(F32)).astype(value.dtype)


def rejoin(value, axis, bit):
    got = trade(value, axis, bit)
    upper = is_upper(axis, bit) == 1
    low = jnp.concatenate([value, got], axis=0)
    return jnp.where(upper, jnp.concatenate([got, value], axis=0), low)


def spread_out(value, axis):
    count = lax.axis_size(axis)
    copies = jnp.broadcast_to(value[None], (count,) + value.shape)
    return swap(copies, axis)


def narrow_part(value):
    for bit in bits("narrow"):
        value = halve(value, "narrow", bit)
    return value


def wide_part(value):
    width = value.shape[1]
    count = lax.axis_size("wide")
    parts = swap(value.reshape(count, -1, width), "wide")
    return jnp.sum(parts.astype(F32), axis=0).astype(value.dtype)


def wide_whole(value):
    return spread_out(value, "wide").reshape(-1, value.shape[1])


def narrow_whole(value):
    for bit in reversed(list(bits("narrow"))):
        value = rejoin(value, "narrow", bit)
    return value


def small_sum(value):
    for axis in ("narrow", "wide"):
        for bit in bits(axis):
            value = value + trade(value, axis, bit)
    return value


def per_device(
    tokens,
    grad_out,
    routes,
    group_counts,
    group_weights,
    norm1_gain,
    norm1_bias,
    w_query,
    bias_query,
    w_key,
    w_value,
    bias_value,
    w_out,
    bias_out,
    norm2_gain,
    norm2_bias,
    router,
    w_in,
    bias_in,
    w_down,
    bias_down,
):
    rows, width = tokens.shape
    experts = router.shape[1]
    assert rows == SEQ_LEN and w_in.shape[0] == 1
    hidden_cols = w_in.shape[2]
    wide_count = lax.axis_size("wide")
    narrow_count = lax.axis_size("narrow")
    devices = wide_count * narrow_count
    capacity = 2 * rows // experts
    half = capacity // 2
    total_tokens = rows * devices
    row = lambda vector: vector.reshape(1, -1)

    sequence = lax.axis_index(("wide", "narrow"))
    group_ends = jnp.cumsum(group_counts, dtype=jnp.int32)
    member = ((sequence >= group_ends - group_counts) & (sequence < group_ends)).astype(F32)
    factor = group_weights.astype(F32) * devices / (group_counts.shape[0] * group_counts.astype(F32))
    weight = jnp.sum(member * factor).reshape(1, 1)
    ids = routes.reshape(1, rows)
    router_rows = jnp.transpose(router)

    slots, columns, grad_outgoing = route(routes, grad_out, experts, capacity)
    grad_rows = swap(grad_outgoing, "wide")
    gathered_in = lax.all_gather(w_in[0], "narrow", axis=0)
    gathered_down = lax.all_gather(w_down[0], "narrow", axis=0)

    normed_t, queries, keys, values = project(
        tokens, row(norm1_gain), row(norm1_bias), w_query, row(bias_query), w_key, w_value, row(bias_value)
    )
    context, logs = attend(queries, keys, values)
    hidden, moe_in, logits = settle(
        context, tokens, w_out, row(bias_out), row(norm2_gain), row(norm2_bias), router_rows
    )
    first, second = dispatch(weight, slots, ids, logits, moe_in, capacity)
    gathered_bias = lax.all_gather(after(bias_in, first), "narrow", axis=0)
    x0 = swap(after(first, grad_rows), "wide")
    counted = jnp.sum(grad_rows[:, capacity, :experts].astype(F32), axis=0)
    fraction = narrow_sum(counted) / total_tokens
    x1 = swap(after(second, x0), "wide")
    act, up, out, back0, dots = expert(
        x0, grad_rows, gathered_in, gathered_bias, gathered_down, bias_down, 0
    )
    back0 = swap(after(back0, x1), "wide")
    act, up, expert_out, back1 = expert(
        x1, grad_rows, gathered_in, gathered_bias, gathered_down, bias_down, 1, (act, up, out, dots)
    )
    back1 = arrived = swap(after(back1, back0), "wide")
    scale = jnp.sum(x1[:, half : half + 3, :capacity].astype(F32), axis=1)
    scale = jnp.transpose(scale.reshape(wide_count, 2, half), (1, 0, 2)).reshape(2, 1, wide_count * half)
    expert_grad = weight_grads(after(x0, back0), x1, grad_rows, act, up, scale)
    expert_grad = lax.psum_scatter(after(expert_grad, arrived), "narrow", scatter_dimension=0).astype(F32)
    share = width // narrow_count
    grad_w_in = expert_grad[:width, :hidden_cols]
    grad_w_down = expert_grad[width : width + hidden_cols]
    grad_bias_in = expert_grad[width + hidden_cols : width + hidden_cols + 1, :hidden_cols]
    grad_bias_down = lax.dynamic_slice_in_dim(
        expert_grad[width + hidden_cols + 1 : width + hidden_cols + 2],
        lax.axis_index("narrow") * share,
        share,
        1,
    )
    back1 = after(back1, expert_grad)
    returned = swap(after(expert_out, arrived), "wide")

    extras = jnp.transpose(back1[:, half:, :half], (1, 0, 2))
    dots1 = jnp.pad(extras, ((0, 0), (0, 0), (0, EXTRA))).reshape(EXTRA, experts * (half + EXTRA))
    dots0 = jnp.concatenate([extras[3:], extras[:3]], axis=0).reshape(EXTRA, experts * half)
    pull = (BALANCE * experts * fraction).reshape(experts, 1)
    hid_grad, con_grad, out_grad, sums, router_grad, prob_sums = combine(
        weight,
        back0.reshape(experts * half, width),
        back1.reshape(experts * (half + EXTRA), width),
        dots0,
        dots1,
        columns,
        ids,
        logits,
        pull,
        hidden,
        grad_out,
        context,
        moe_in,
        w_out,
        router_rows,
        row(norm2_gain),
    )
    pairs = width // PAIR
    span = pairs // ATTEND_CALLS
    grads, bias_sums = [], []
    packed = [narrow_part(out_grad)]
    for call in range(ATTEND_CALLS):
        dq, dk, dv, weights, column_sums = attend_back(
            queries, keys, values, logs, con_grad, normed_t, call * span, span
        )
        grads.append((dq, dk, dv))
        packed.append(narrow_part(weights))
        bias_sums.append(column_sums)
    early = jnp.concatenate(packed[:-1], axis=1)
    hid_grad = after(hid_grad, early)
    grad_tokens, norm_sums = close(grads, tokens, hid_grad, row(norm1_gain), w_query, w_key, w_value)
    block_out = block_output(
        returned.reshape(experts * capacity, width), columns, ids, logits, hidden
    )
    early = wide_part(after(early, returned))
    late = wide_part(after(packed[-1], early, norm_sums))
    early = wide_whole(after(early, late, block_out))
    late = wide_whole(after(late, early, grad_w_in, grad_w_down))
    early = narrow_whole(early)
    late = narrow_whole(late)
    bias_sums = jnp.concatenate(bias_sums, axis=1)
    prob_row = jnp.pad(prob_sums.reshape(1, experts), ((0, 0), (0, width - experts)))
    small = small_sum(
        jnp.concatenate([norm_sums[:2], bias_sums[:2], sums[:3], prob_row, router_grad], axis=0)
    )
    balance_loss = experts * jnp.sum(fraction * (small[7, :experts] / total_tokens))
    grad_w_out, *weights = unpack(early, late)
    return (
        block_out,
        balance_loss,
        grad_tokens,
        small[0],
        small[1],
        weights[0],
        small[2],
        weights[1],
        weights[2],
        small[3],
        grad_w_out,
        small[6],
        small[4],
        small[5],
        jnp.transpose(small[8:]),
        grad_w_in[None],
        grad_bias_in,
        grad_w_down[None],
        grad_bias_down,
    )


def solution(mesh):
    return jax.shard_map(
        per_device,
        mesh=mesh,
        in_specs=(
            P(("wide", "narrow"), None),
            P(("wide", "narrow"), None),
            P(("wide", "narrow"), None),
            P(),
            P(),
            P(),
            P(),
            P(),
            P(),
            P(),
            P(),
            P(),
            P(),
            P(),
            P(),
            P(),
            P(),
            P("wide", None, "narrow"),
            P("wide", "narrow"),
            P("wide", "narrow", None),
            P("wide", None),
        ),
        out_specs=(
            P(("wide", "narrow"), None),
            P(),
            P(("wide", "narrow"), None),
            P(),
            P(),
            P(),
            P(),
            P(),
            P(),
            P(),
            P(),
            P(),
            P(),
            P(),
            P(),
            P("wide", None, "narrow"),
            P("wide", "narrow"),
            P("wide", "narrow", None),
            P("wide", "narrow"),
        ),
        check_vma=False,
    )
```

```python
import functools
import jax
import jax.numpy as jnp
from jax import lax
from jax.experimental import pallas as pl
from jax.experimental.pallas import tpu as pltpu
from jax.sharding import PartitionSpec as P

HEADS = 12
HEAD_DIM = 64
SEQ_LEN = 1024
EPS = 1e-05
BALANCE = 48.0
NEGATIVE = -1e30
PAIR = 2 * HEAD_DIM
F32 = jnp.float32
BF16 = jnp.bfloat16
VMEM_LIMIT = 56 * 1024 * 1024
EXTRA = 8
COVER = 4e10
ATTEND_CALLS = 2


def mm(left, right):
    return lax.dot_general(left, right, (((1,), (0,)), ((), ())), preferred_element_type=F32)


def mm_nt(left, right):
    return lax.dot_general(left, right, (((1,), (1,)), ((), ())), preferred_element_type=F32)


def mm_tn(left, right):
    return lax.dot_general(left, right, (((0,), (0,)), ((), ())), preferred_element_type=F32)


def cost(flops, nbytes, trans=0):
    return pl.CostEstimate(flops=int(flops), bytes_accessed=int(nbytes), transcendentals=int(trans))


def params(*semantics):
    return pltpu.CompilerParams(dimension_semantics=semantics, vmem_limit_bytes=VMEM_LIMIT)


def head_mask(block, head):
    lanes = lax.broadcasted_iota(jnp.int32, block.shape, 1)
    return jnp.where(lanes // HEAD_DIM == head, block, jnp.zeros_like(block))


def causal(scores, block):
    keys = scores.shape[0]
    first = lax.broadcasted_iota(jnp.int32, (block, block), 0)
    second = lax.broadcasted_iota(jnp.int32, (block, block), 1)
    last = jnp.where(first <= second, scores[keys - block :], NEGATIVE)
    if keys == block:
        return last
    return jnp.concatenate([scores[: keys - block], last], axis=0)


def attend_kernel(block, q_ref, k_ref, v_ref, context_ref, weights_ref):
    rows = q_ref.shape[0]
    keys = k_ref[...]
    values_t = jnp.transpose(v_ref[...])
    place = 0
    for first in range(0, rows, block):
        span = first + block
        query = q_ref[first:span, :]
        parts = []
        for head in range(2):
            scores = causal(mm_nt(keys[:span], head_mask(query, head)), block)
            peak = jnp.max(scores, axis=0, keepdims=True)
            powers = jnp.exp(scores - peak)
            total = jnp.sum(powers, axis=0, keepdims=True)
            weights = (powers * (1.0 / total)).astype(BF16)
            weights_ref[0, head, place : place + span, :] = weights
            parts.append(mm(values_t[head * HEAD_DIM : (head + 1) * HEAD_DIM, :span], weights))
        context_ref[first:span, :] = jnp.transpose(jnp.concatenate(parts, axis=0)).astype(BF16)
        place += span


def attend(queries, keys, values, block=256):
    rows, width = queries.shape
    pairs = width // PAIR
    kept = sum(range(block, rows + 1, block))
    spec = pl.BlockSpec((rows, PAIR), lambda p: (0, p))
    return pl.pallas_call(
        functools.partial(attend_kernel, block),
        grid=(pairs,),
        in_specs=[spec, spec, spec],
        out_specs=[spec, pl.BlockSpec((1, 2, kept, block), lambda p: (p, 0, 0, 0))],
        out_shape=[
            jax.ShapeDtypeStruct((rows, width), BF16),
            jax.ShapeDtypeStruct((pairs, 2, kept, block), BF16),
        ],
        compiler_params=params("arbitrary"),
        cost_estimate=cost(4 * rows * rows * width * 2, rows * width * 8, pairs * 2 * rows * rows),
        name="attend",
    )(queries, keys, values)


def attend_back_kernel(block, q_ref, k_ref, v_ref, weights_ref, g_ref, normed_ref,
                       dq_ref, dk_ref, dv_ref, packed_ref, sums_ref, dq_acc, dk_acc, dv_acc):
    rows = q_ref.shape[0]
    keys = k_ref[...]
    values = v_ref[...]
    keys_t = jnp.transpose(keys)
    place = weights_ref.shape[2]
    for first in reversed(range(0, rows, block)):
        span = first + block
        place -= span
        query = q_ref[first:span, :]
        grad = g_ref[first:span, :]
        grad_query, probs_both, scores_both, query_both, grad_both = [], [], [], [], []
        for head in range(2):
            query_h = head_mask(query, head)
            grad_h = head_mask(grad, head)
            weights = weights_ref[0, head, place : place + span, :]
            probs = weights.astype(F32)
            grad_probs = mm_nt(values[:span], grad_h)
            inner = jnp.sum(probs * grad_probs, axis=0, keepdims=True)
            grad_scores = (probs * (grad_probs - inner)).astype(BF16)
            grad_query.append(mm(keys_t[head * HEAD_DIM : (head + 1) * HEAD_DIM, :span], grad_scores))
            probs_both.append(weights)
            scores_both.append(grad_scores)
            query_both.append(query_h)
            grad_both.append(grad_h)
        dv = mm(jnp.concatenate(probs_both, axis=1), jnp.concatenate(grad_both, axis=0))
        dk = mm(jnp.concatenate(scores_both, axis=1), jnp.concatenate(query_both, axis=0))
        if span == rows:
            dv_acc[...] = dv
            dk_acc[...] = dk
        else:
            dv_acc[:span, :] += dv
            dk_acc[:span, :] += dk
        dq = jnp.transpose(jnp.concatenate(grad_query, axis=0)) * 0.125
        dq_acc[first:span, :] = dq.astype(BF16)
    dq = dq_acc[...]
    dk = dk_acc[...].astype(BF16)
    dv = dv_acc[...].astype(BF16)
    dq_ref[...] = dq
    dk_ref[...] = dk
    dv_ref[...] = dv
    normed = normed_ref[...]
    packed_ref[:, : 2 * PAIR] = mm(normed, jnp.concatenate([dq, dk], axis=1)).astype(BF16)
    packed_ref[:, 2 * PAIR :] = mm(normed, dv).astype(BF16)
    sums_ref[...] = jnp.concatenate(
        [
            jnp.sum(dq.astype(F32), axis=0, keepdims=True),
            jnp.sum(dv.astype(F32), axis=0, keepdims=True),
            jnp.zeros((6, PAIR), F32),
        ],
        axis=0,
    )


def attend_back(queries, keys, values, weights, grad_context, normed_t, start, pairs, block=256):
    rows, width = queries.shape
    spec = pl.BlockSpec((rows, PAIR), lambda p: (0, p + start))
    out_spec = pl.BlockSpec((rows, PAIR), lambda p: (0, p))
    return pl.pallas_call(
        functools.partial(attend_back_kernel, block),
        grid=(pairs,),
        in_specs=[
            spec,
            spec,
            spec,
            pl.BlockSpec((1, 2) + weights.shape[2:], lambda p: (p + start, 0, 0, 0)),
            spec,
            pl.BlockSpec((width, rows), lambda p: (0, 0)),
        ],
        out_specs=[
            out_spec,
            out_spec,
            out_spec,
            pl.BlockSpec((width, 3 * PAIR), lambda p: (0, p)),
            pl.BlockSpec((8, PAIR), lambda p: (0, p)),
        ],
        out_shape=[jax.ShapeDtypeStruct((rows, pairs * PAIR), BF16)] * 3
        + [
            jax.ShapeDtypeStruct((width, 3 * pairs * PAIR), BF16),
            jax.ShapeDtypeStruct((8, pairs * PAIR), F32),
        ],
        scratch_shapes=[
            pltpu.VMEM((rows, PAIR), BF16),
            pltpu.VMEM((rows, PAIR), F32),
            pltpu.VMEM((rows, PAIR), F32),
        ],
        compiler_params=params("arbitrary"),
        cost_estimate=cost(rows, rows),
        name="attend_back",
    )(queries, keys, values, weights, grad_context, normed_t)


def normalise(values):
    centred = values - jnp.mean(values, axis=-1, keepdims=True)
    spread = lax.rsqrt(jnp.mean(centred * centred, axis=-1, keepdims=True) + EPS)
    return centred * spread, spread


def normalise_back(grad, unit, spread, gain):
    scaled = grad * gain
    mean = jnp.mean(scaled, axis=-1, keepdims=True)
    tilt = jnp.mean(scaled * unit, axis=-1, keepdims=True)
    return spread * (scaled - mean - unit * tilt)


def pieces(values):
    high = values.astype(BF16)
    rest = values - high.astype(F32)
    middle = rest.astype(BF16)
    low = (rest - middle.astype(F32)).astype(BF16)
    fill = jnp.zeros((5, values.shape[1]), F32)
    stacked = jnp.concatenate(
        [high.astype(F32), middle.astype(F32), low.astype(F32), fill], axis=0
    )
    return stacked.astype(BF16)


def join(parts):
    return parts[0:1] + parts[1:2] + parts[2:3]


def column(row):
    return jnp.transpose(jnp.broadcast_to(row, (8, row.shape[1])))[:, 0:1]


def gate_row(logits, picked):
    return jax.nn.sigmoid(jnp.sum(jnp.where(picked, logits, 0.0), axis=0, keepdims=True))


def picked_rows(ids, experts):
    return lax.broadcasted_iota(jnp.int32, (experts, ids.shape[1]), 0) == ids


def one_hot_rows(slots, first, count):
    places = lax.broadcasted_iota(jnp.int32, (count, slots.shape[1]), 0) + first
    return (places == slots).astype(F32).astype(BF16)


def one_hot_columns(slots, first, count):
    places = lax.broadcasted_iota(jnp.int32, (slots.shape[0], count), 1) + first
    return (places == slots).astype(F32).astype(BF16)


def route_kernel(experts, capacity, row_ref, grad_ref, slots_ref, columns_ref, out_ref, count_row):
    step = pl.program_id(0)
    rows = row_ref.shape[1]
    width = grad_ref.shape[1]
    half = capacity // 2

    @pl.when(step == 0)
    def _():
        block = 256
        ids = row_ref[...]
        picked = picked_rows(ids, experts).astype(F32)
        first = lax.broadcasted_iota(jnp.int32, (block, block), 0)
        second = lax.broadcasted_iota(jnp.int32, (block, block), 1)
        earlier = (first < second).astype(F32).astype(BF16)
        passed = jnp.zeros((experts, 1), F32)
        places = []
        for start in range(0, rows, block):
            own = picked[:, start : start + block]
            before = mm(own.astype(BF16), earlier) + passed
            places.append(jnp.sum(before * own, axis=0, keepdims=True))
            passed = passed + jnp.sum(own, axis=1, keepdims=True)
        place = jnp.concatenate(places, axis=1).astype(jnp.int32)
        slots = ids * capacity + place
        late = experts * half + ids * (half + EXTRA) + place - half
        mixed = jnp.where(place < half, ids * half + place, late)
        slots_ref[...] = slots
        both = jnp.concatenate([mixed, slots, jnp.zeros((6, rows), jnp.int32)], axis=0)
        columns_ref[...] = jnp.transpose(both.astype(F32))[:, 0:2].astype(jnp.int32)
        count_row[...] = jnp.zeros_like(count_row)
        lanes = lax.broadcasted_iota(jnp.int32, (experts, 128), 1)
        spread = jnp.where(lanes == lax.broadcasted_iota(jnp.int32, (experts, 128), 0), passed, 0.0)
        count_row[0:1, 0:128] = jnp.sum(spread, axis=0, keepdims=True)

    chosen = one_hot_rows(slots_ref[...], step * capacity, capacity)
    out_ref[0, :capacity, :] = mm(chosen, grad_ref[...]).astype(BF16)
    out_ref[0, capacity:, :] = count_row[...].astype(BF16)


def route(routes, grad_out, experts, capacity):
    rows, width = grad_out.shape
    whole = lambda e: (0, 0)
    return pl.pallas_call(
        functools.partial(route_kernel, experts, capacity),
        grid=(experts,),
        in_specs=[
            pl.BlockSpec((1, rows), whole),
            pl.BlockSpec((rows, width), whole),
        ],
        out_specs=[
            pl.BlockSpec((1, rows), whole),
            pl.BlockSpec((rows, 2), whole),
            pl.BlockSpec((1, capacity + EXTRA, width), lambda e: (e, 0, 0)),
        ],
        out_shape=[
            jax.ShapeDtypeStruct((1, rows), jnp.int32),
            jax.ShapeDtypeStruct((rows, 2), jnp.int32),
            jax.ShapeDtypeStruct((experts, capacity + EXTRA, width), BF16),
        ],
        scratch_shapes=[pltpu.VMEM((EXTRA, width), F32)],
        compiler_params=params("arbitrary"),
        cost_estimate=cost(2 * experts * capacity * rows * width, 6 * rows * width),
        name="route",
    )(routes.reshape(1, rows), grad_out)


def project_kernel(tokens_ref, gain_ref, shift_ref, wq_ref, bq_ref, wk_ref, wv_ref, bv_ref,
                   normed_ref, q_ref, k_ref, v_ref):
    unit, _ = normalise(tokens_ref[...].astype(F32))
    normed = (unit * gain_ref[...] + shift_ref[...]).astype(BF16)
    normed_ref[...] = jnp.transpose(normed)
    q_ref[...] = ((mm(normed, wq_ref[...]) + bq_ref[...]) * 0.125).astype(BF16)
    k_ref[...] = mm(normed, wk_ref[...]).astype(BF16)
    v_ref[...] = (mm(normed, wv_ref[...]) + bv_ref[...]).astype(BF16)


def project(tokens, gain, shift, w_query, bias_query, w_key, w_value, bias_value, tile=256):
    rows, width = tokens.shape
    row_spec = pl.BlockSpec((tile, width), lambda t: (t, 0))
    vector = pl.BlockSpec((1, width), lambda t: (0, 0))
    square = pl.BlockSpec((width, width), lambda t: (0, 0))
    return pl.pallas_call(
        project_kernel,
        grid=(rows // tile,),
        in_specs=[row_spec, vector, vector, square, vector, square, square, vector],
        out_specs=[pl.BlockSpec((width, tile), lambda t: (0, t))] + [row_spec] * 3,
        out_shape=[jax.ShapeDtypeStruct((width, rows), BF16)]
        + [jax.ShapeDtypeStruct((rows, width), BF16)] * 3,
        compiler_params=params("arbitrary"),
        cost_estimate=cost(6 * rows * width * width, 10 * rows * width + 6 * width * width),
        name="project",
    )(tokens, gain, shift, w_query, bias_query, w_key, w_value, bias_value)


def settle_kernel(context_ref, tokens_ref, w_out_ref, bias_ref, gain_ref, shift_ref, router_ref,
                  hidden_ref, moe_ref, logits_ref):
    hidden = tokens_ref[...].astype(F32) + mm(context_ref[...], w_out_ref[...]) + bias_ref[...]
    unit, _ = normalise(hidden)
    moe_in = (unit * gain_ref[...] + shift_ref[...]).astype(BF16)
    hidden_ref[...] = hidden
    moe_ref[...] = moe_in
    logits_ref[...] = mm_nt(router_ref[...], moe_in)


def settle(context, tokens, w_out, bias_out, gain, shift, router_rows, tile=256):
    rows, width = tokens.shape
    experts = router_rows.shape[0]
    row_spec = pl.BlockSpec((tile, width), lambda t: (t, 0))
    vector = pl.BlockSpec((1, width), lambda t: (0, 0))
    return pl.pallas_call(
        settle_kernel,
        grid=(rows // tile,),
        in_specs=[
            row_spec,
            row_spec,
            pl.BlockSpec((width, width), lambda t: (0, 0)),
            vector,
            vector,
            vector,
            pl.BlockSpec((experts, width), lambda t: (0, 0)),
        ],
        out_specs=[row_spec, row_spec, pl.BlockSpec((experts, tile), lambda t: (0, t))],
        out_shape=[
            jax.ShapeDtypeStruct((rows, width), F32),
            jax.ShapeDtypeStruct((rows, width), BF16),
            jax.ShapeDtypeStruct((experts, rows), F32),
        ],
        compiler_params=params("arbitrary"),
        cost_estimate=cost(2 * rows * width * width, 10 * rows * width + 2 * width * width),
        name="settle",
    )(context, tokens, w_out, bias_out, gain, shift, router_rows)


def dispatch_kernel(weight_ref, slots_ref, ids_ref, logits_ref, moe_ref, first_ref, second_ref, parts):
    step = pl.program_id(0)
    experts = logits_ref.shape[0]
    half = first_ref.shape[1]

    @pl.when(step == 0)
    def _():
        gate = gate_row(logits_ref[...], picked_rows(ids_ref[...], experts))
        parts[...] = pieces(gate * weight_ref[0, 0])

    chosen = one_hot_rows(slots_ref[...], step * 2 * half, 2 * half)
    rows = mm(chosen, moe_ref[...]).astype(BF16)
    first_ref[0] = rows[:half]
    second_ref[0, :half, :] = rows[half:]
    second_ref[0, half:, :] = jnp.zeros((EXTRA, rows.shape[1]), BF16)
    second_ref[0, half:, 0 : 2 * half] = mm_nt(parts[...], chosen).astype(BF16)


def dispatch(weight, slots, ids, logits, moe_in, capacity):
    rows, width = moe_in.shape
    experts = logits.shape[0]
    half = capacity // 2
    whole = lambda e: (0, 0)
    return pl.pallas_call(
        dispatch_kernel,
        grid=(experts,),
        in_specs=[
            pl.BlockSpec(memory_space=pltpu.SMEM),
            pl.BlockSpec((1, rows), whole),
            pl.BlockSpec((1, rows), whole),
            pl.BlockSpec((experts, rows), whole),
            pl.BlockSpec((rows, width), whole),
        ],
        out_specs=[
            pl.BlockSpec((1, half, width), lambda e: (e, 0, 0)),
            pl.BlockSpec((1, half + EXTRA, width), lambda e: (e, 0, 0)),
        ],
        out_shape=[
            jax.ShapeDtypeStruct((experts, half, width), BF16),
            jax.ShapeDtypeStruct((experts, half + EXTRA, width), BF16),
        ],
        scratch_shapes=[pltpu.VMEM((8, rows), BF16)],
        compiler_params=params("arbitrary"),
        cost_estimate=cost(2 * experts * capacity * rows * width, 6 * rows * width),
        name="dispatch",
    )(weight, slots, ids, logits, moe_in)


def row_sum(values):
    ones = jnp.ones((8, values.shape[1]), BF16)
    high = values.astype(BF16)
    rest = values - high.astype(F32)
    middle = rest.astype(BF16)
    low = (rest - middle.astype(F32)).astype(BF16)
    return (mm_nt(ones, high) + mm_nt(ones, middle) + mm_nt(ones, low))[0:1]


def expert_kernel(steps, chunk, *refs):
    if chunk == 0:
        (x_ref, g_ref, w_in_ref, b_in_ref, w_down_ref, b_down_ref,
         act_ref, up_ref, out_ref, back_ref, dot_ref, back_acc, dot_acc, out_acc) = refs
    else:
        (x_ref, g_ref, w_in_ref, b_in_ref, w_down_ref, b_down_ref, _, _, _, earlier_ref,
         act_ref, up_ref, out_ref, back_ref, back_acc, dot_acc, out_acc) = refs
    part = pl.program_id(0)
    tile = pl.program_id(1)
    group, half, width = x_ref.shape
    rows = group * half
    x = x_ref[...].reshape(rows, width)
    g = g_ref[...].reshape(rows, width)
    w_in = w_in_ref[0]
    pre = mm(x, w_in) + b_in_ref[0].astype(F32)
    grad_act = mm_nt(g, w_down_ref[0])
    below = 0.5 + 0.5 * lax.erf(pre * 0.7071067811865476)
    act = pre * below
    slope = below + pre * (0.3989422804014327 * jnp.exp(-0.5 * pre * pre))
    up = (grad_act * slope).astype(BF16)
    rounded = act.astype(BF16)
    act_ref[0, 0] = rounded
    up_ref[0, 0] = up
    out = mm(rounded, w_down_ref[0])
    product = act * grad_act
    lanes = min(128, product.shape[1])
    folded = product[:, :lanes]
    for lane in range(lanes, product.shape[1], lanes):
        folded = folded + product[:, lane : lane + lanes]
    where = pl.ds(pl.multiple_of(tile * rows, rows), rows)
    back = mm_nt(up, w_in)

    @pl.when(part == 0)
    def _():
        biased = g.astype(F32) * b_down_ref[...].astype(F32)
        total = folded
        for lane in range(0, biased.shape[1], lanes):
            total = total + biased[:, lane : lane + lanes]
        back_acc[where, :] = back
        out_acc[where, :] = out + b_down_ref[...].astype(F32)
        dot_acc[where, :] = total

    @pl.when(part > 0)
    def _():
        back_acc[where, :] += back
        out_acc[where, :] += out
        dot_acc[where, :] += folded

    @pl.when(part == steps - 1)
    def _():
        out_ref[...] = out_acc[where, :].astype(BF16).reshape(group, half, width)
        back_ref[:, :half, :] = back_acc[where, :].astype(BF16).reshape(group, half, width)
        dots = dot_acc[where, :]
        for index in range(group):
            own = pieces(row_sum(dots[index * half : (index + 1) * half, :])).astype(F32)
            if chunk == 0:
                dot_ref[index] = own.astype(BF16)
            else:
                before = earlier_ref[index].astype(F32)
                extra = jnp.concatenate([own[0:3], before[0:3], own[6:8]], axis=0)
                back_ref[index, half:, :] = jnp.zeros((EXTRA, width), BF16)
                back_ref[index, half:, 0:half] = extra.astype(BF16)


def expert(x, g, w_in, b_in, w_down, b_down, chunk, earlier=()):
    sources, width = x.shape[0], x.shape[2]
    half = (g.shape[1] - EXTRA) // 2
    rows = sources * half
    parts, _, hidden = w_in.shape
    group = max(1, 256 // half)
    tile = group * half
    tiles = sources // group
    last = parts - 1
    late = lambda p, t: jnp.where(p == last, t, 0)
    wide_spec = pl.BlockSpec((1, 1, tile, hidden), lambda p, t: (p, chunk, t, 0))
    wide_shape = jax.ShapeDtypeStruct((parts, 2, rows, hidden), BF16)
    dot_shape = jax.ShapeDtypeStruct((sources, 8, half), BF16)
    dot_spec = pl.BlockSpec((group, 8, half), lambda p, t: (late(p, t), 0, 0))
    back_rows = half + EXTRA * chunk
    return pl.pallas_call(
        functools.partial(expert_kernel, parts, chunk),
        grid=(parts, tiles),
        in_specs=[
            pl.BlockSpec((group, half, width), lambda p, t: (t, 0, 0)),
            pl.BlockSpec((group, half, width), lambda p, t: (t, chunk, 0)),
            pl.BlockSpec((1, width, hidden), lambda p, t: (p, 0, 0)),
            pl.BlockSpec((1, 1, hidden), lambda p, t: (p, 0, 0)),
            pl.BlockSpec((1, hidden, width), lambda p, t: (p, 0, 0)),
            pl.BlockSpec((1, width), lambda p, t: (0, 0)),
        ]
        + ([pl.BlockSpec(memory_space=pl.ANY)] * 3 + [dot_spec] if chunk else []),
        out_specs=[
            wide_spec,
            wide_spec,
            pl.BlockSpec((group, half, width), lambda p, t: (late(p, t), chunk, 0)),
            pl.BlockSpec((group, back_rows, width), lambda p, t: (late(p, t), 0, 0)),
        ]
        + ([] if chunk else [dot_spec]),
        out_shape=[
            wide_shape,
            wide_shape,
            jax.ShapeDtypeStruct((sources, 2 * half, width), BF16),
            jax.ShapeDtypeStruct((sources, back_rows, width), BF16),
        ]
        + ([] if chunk else [dot_shape]),
        scratch_shapes=[
            pltpu.VMEM((rows, width), F32),
            pltpu.VMEM((rows, min(128, hidden)), F32),
            pltpu.VMEM((rows, width), F32),
        ],
        input_output_aliases={6: 0, 7: 1, 8: 2} if chunk else {},
        compiler_params=params("arbitrary", "arbitrary"),
        cost_estimate=cost(
            6 * rows * width * hidden * parts, rows * hidden * parts * 4, 2 * rows * hidden * parts
        ),
        name="expert",
    )(x, g, w_in, b_in, w_down, b_down, *earlier)


def weight_kernel(parts, x0_ref, x1_ref, g_ref, act_ref, up_ref, scale_ref,
                  grad_ref, down_acc, in_acc, bias_acc, bias_down_acc, flipped):
    part = pl.program_id(0)
    chunk = pl.program_id(1)
    sources, half, width = x0_ref.shape
    rows = sources * half
    hidden = act_ref.shape[3]
    scale = scale_ref[0]
    split = pieces(scale)
    g = g_ref[...].reshape(rows, width)

    def flip(values):
        return (jnp.transpose(values).astype(F32) * scale).astype(BF16)

    @pl.when((part == 0) & (chunk == 0))
    def _():
        flipped[0] = flip(x0_ref[...].reshape(rows, width))

    @pl.when((part == 0) & (chunk == 1))
    def _():
        flipped[1] = flip(x1_ref[...].reshape(rows, width))

    act = act_ref[0, 0]
    up = up_ref[0, 0]
    down = mm(flip(act), g)
    into = mm(flipped[chunk], up)
    bias_in = join(mm(split, up))

    @pl.when(chunk == 0)
    def _():
        down_acc[...] = down
        in_acc[...] = into
        bias_acc[...] = bias_in

    @pl.when(chunk == 1)
    def _():
        grad_ref[0, width : width + hidden, :] = (down_acc[...] + down).astype(BF16)
        grad_ref[0, :width, 0:hidden] = (in_acc[...] + into).astype(BF16)

    @pl.when(part == 0)
    def _():
        bias_down = join(mm(split, g))
        bias_down_acc[...] = jnp.where(chunk == 0, bias_down, bias_down_acc[...] + bias_down)

    @pl.when(chunk == 1)
    def _():
        first = width + hidden
        grad_ref[0, first:, :] = jnp.zeros((EXTRA, width), BF16)
        grad_ref[0, first : first + 1, 0:hidden] = (bias_acc[...] + bias_in).astype(BF16)
        grad_ref[0, first + 1 : first + 2, :] = bias_down_acc[...].astype(BF16)


def weight_grads(x0, x1, g, act, up, scale):
    sources, half, width = x0.shape
    parts, _, rows, hidden = act.shape
    wide_spec = pl.BlockSpec((1, 1, rows, hidden), lambda p, t: (p, t, 0, 0))
    return pl.pallas_call(
        functools.partial(weight_kernel, parts),
        grid=(parts, 2),
        in_specs=[
            pl.BlockSpec((sources, half, width), lambda p, t: (0, 0, 0)),
            pl.BlockSpec((sources, half, width), lambda p, t: (0, 0, 0)),
            pl.BlockSpec((sources, half, width), lambda p, t: (0, t, 0)),
            wide_spec,
            wide_spec,
            pl.BlockSpec((1, 1, rows), lambda p, t: (t, 0, 0)),
        ],
        out_specs=pl.BlockSpec((1, width + hidden + EXTRA, width), lambda p, t: (p, 0, 0)),
        out_shape=jax.ShapeDtypeStruct((parts, width + hidden + EXTRA, width), BF16),
        scratch_shapes=[
            pltpu.VMEM((hidden, width), F32),
            pltpu.VMEM((width, hidden), F32),
            pltpu.VMEM((1, hidden), F32),
            pltpu.VMEM((1, width), F32),
            pltpu.VMEM((2, width, rows), BF16),
        ],
        compiler_params=params("arbitrary", "arbitrary"),
        cost_estimate=cost(12 * rows * width * hidden * parts, rows * hidden * parts * 8),
        name="weight_grads",
    )(x0, x1, g, act, up, scale)


def combine_kernel(weight_ref, back0_ref, back1_ref, dots0_ref, dots1_ref, columns_ref, ids_ref, logits_ref, pull_ref,
                   hidden_ref, grad_ref, context_ref, moe_ref, w_out_ref, router_ref, gain_ref,
                   hid_grad_ref, con_grad_ref, out_grad_ref, sums_ref, router_grad_ref, probs_ref, out_acc):
    step = pl.program_id(0)
    experts = logits_ref.shape[0]
    count0 = back0_ref.shape[0]
    count1 = back1_ref.shape[0]
    weight = weight_ref[0, 0]
    columns = columns_ref[:, 0:1]
    chosen0 = one_hot_columns(columns, 0, count0)
    chosen1 = one_hot_columns(columns, count0, count1)
    rows = mm(chosen0, back0_ref[...]) + mm(chosen1, back1_ref[...])
    dots = join(mm_nt(dots0_ref[...], chosen0)) + join(mm_nt(dots1_ref[...], chosen1))
    logits = logits_ref[...]
    picked = picked_rows(ids_ref[...], experts)
    gate = gate_row(logits, picked)
    powers = jnp.exp(logits - jnp.max(logits, axis=0, keepdims=True))
    probs = powers / jnp.sum(powers, axis=0, keepdims=True)
    pull = pull_ref[...]
    slope = dots * weight * gate * (1.0 - gate)
    logit_grad = probs * (pull - jnp.sum(probs * pull, axis=0, keepdims=True))
    logit_grad = (logit_grad + jnp.where(picked, slope, 0.0)).astype(BF16)
    moe_grad = mm_tn(logit_grad, router_ref[...]) + rows * column(gate * weight)
    unit, spread = normalise(hidden_ref[...])
    hid_grad = weight * grad_ref[...].astype(F32) + normalise_back(
        moe_grad, unit, spread, gain_ref[...]
    )
    branch = hid_grad.astype(BF16)
    hid_grad_ref[...] = hid_grad
    con_grad_ref[...] = mm_nt(branch, w_out_ref[...]).astype(BF16)
    out_grad = mm_tn(context_ref[...], branch)
    router_grad = mm(logit_grad, moe_ref[...])
    prob_sum = jnp.sum(probs, axis=1, keepdims=True)
    sums = jnp.concatenate(
        [
            jnp.sum(moe_grad * unit, axis=0, keepdims=True),
            jnp.sum(moe_grad, axis=0, keepdims=True),
            jnp.sum(branch.astype(F32), axis=0, keepdims=True),
            jnp.zeros((5, unit.shape[1]), F32),
        ],
        axis=0,
    )

    @pl.when(step == 0)
    def _():
        out_acc[...] = out_grad
        router_grad_ref[...] = router_grad
        probs_ref[...] = prob_sum
        sums_ref[...] = sums

    @pl.when(step > 0)
    def _():
        out_acc[...] += out_grad
        router_grad_ref[...] += router_grad
        probs_ref[...] += prob_sum
        sums_ref[...] += sums

    @pl.when(step == pl.num_programs(0) - 1)
    def _():
        out_grad_ref[...] = out_acc[...].astype(BF16)


def combine(weight, back0, back1, dots0, dots1, columns, ids, logits, pull, hidden, grad_out, context, moe_in,
            w_out, router_rows, gain, tile=256):
    rows, width = hidden.shape
    experts = logits.shape[0]
    count = back0.shape[0]
    count1 = back1.shape[0]
    whole = lambda t: (0, 0)
    row_spec = pl.BlockSpec((tile, width), lambda t: (t, 0))
    square = pl.BlockSpec((width, width), whole)
    return pl.pallas_call(
        combine_kernel,
        grid=(rows // tile,),
        in_specs=[
            pl.BlockSpec(memory_space=pltpu.SMEM),
            pl.BlockSpec((count, width), whole),
            pl.BlockSpec((count1, width), whole),
            pl.BlockSpec((8, count), whole),
            pl.BlockSpec((8, count1), whole),
            pl.BlockSpec((tile, 2), lambda t: (t, 0)),
            pl.BlockSpec((1, tile), lambda t: (0, t)),
            pl.BlockSpec((experts, tile), lambda t: (0, t)),
            pl.BlockSpec((experts, 1), whole),
            row_spec,
            row_spec,
            row_spec,
            row_spec,
            square,
            pl.BlockSpec((experts, width), whole),
            pl.BlockSpec((1, width), whole),
        ],
        out_specs=[
            row_spec,
            row_spec,
            square,
            pl.BlockSpec((8, width), whole),
            pl.BlockSpec((experts, width), whole),
            pl.BlockSpec((experts, 1), whole),
        ],
        out_shape=[
            jax.ShapeDtypeStruct((rows, width), F32),
            jax.ShapeDtypeStruct((rows, width), BF16),
            jax.ShapeDtypeStruct((width, width), BF16),
            jax.ShapeDtypeStruct((8, width), F32),
            jax.ShapeDtypeStruct((experts, width), F32),
            jax.ShapeDtypeStruct((experts, 1), F32),
        ],
        scratch_shapes=[pltpu.VMEM((width, width), F32)],
        compiler_params=params("arbitrary"),
        cost_estimate=cost(rows, rows),
        name="combine",
    )(weight, back0, back1, dots0, dots1, columns, ids, logits, pull, hidden, grad_out, context, moe_in, w_out,
      router_rows, gain)


def close_kernel(count, *refs):
    grads = refs[: 3 * count]
    (tokens_ref, hid_grad_ref, gain_ref, wq_ref, wk_ref, wv_ref, tok_grad_ref, sums_ref) = refs[3 * count :]
    step = pl.program_id(0)
    width = tokens_ref.shape[1]
    norm_grad = None
    for index, weights in enumerate((wq_ref, wk_ref, wv_ref)):
        parts = [grads[3 * part + index][...] for part in range(count)]
        term = mm_nt(jnp.concatenate(parts, axis=1), weights[...])
        norm_grad = term if norm_grad is None else norm_grad + term
    unit, spread = normalise(tokens_ref[...].astype(F32))
    tok_grad = hid_grad_ref[...] + normalise_back(norm_grad, unit, spread, gain_ref[...])
    tok_grad_ref[...] = tok_grad.astype(BF16)
    sums = jnp.concatenate(
        [
            jnp.sum(norm_grad * unit, axis=0, keepdims=True),
            jnp.sum(norm_grad, axis=0, keepdims=True),
            jnp.zeros((6, width), F32),
        ],
        axis=0,
    )

    @pl.when(step == 0)
    def _():
        sums_ref[...] = sums

    @pl.when(step > 0)
    def _():
        sums_ref[...] += sums


def close(grads, tokens, hid_grad, gain, w_query, w_key, w_value, tile=256):
    rows, width = tokens.shape
    whole = lambda t: (0, 0)
    row_spec = pl.BlockSpec((tile, width), lambda t: (t, 0))
    square = pl.BlockSpec((width, width), whole)
    flat = [item for triple in grads for item in triple]
    return pl.pallas_call(
        functools.partial(close_kernel, len(grads)),
        grid=(rows // tile,),
        in_specs=[pl.BlockSpec((tile, item.shape[1]), lambda t: (t, 0)) for item in flat]
        + [row_spec, row_spec, pl.BlockSpec((1, width), whole), square, square, square],
        out_specs=[row_spec, pl.BlockSpec((8, width), whole)],
        out_shape=[
            jax.ShapeDtypeStruct((rows, width), BF16),
            jax.ShapeDtypeStruct((8, width), F32),
        ],
        compiler_params=params("arbitrary"),
        cost_estimate=cost(COVER, 4096),
        name="close",
    )(*flat, tokens, hid_grad, gain, w_query, w_key, w_value)


def block_out_kernel(back_ref, columns_ref, ids_ref, logits_ref, hidden_ref, out_ref):
    chosen = one_hot_columns(columns_ref[:, 1:2], 0, back_ref.shape[0])
    rows = mm(chosen, back_ref[...])
    gate = gate_row(logits_ref[...], picked_rows(ids_ref[...], logits_ref.shape[0]))
    out_ref[...] = (hidden_ref[...] + column(gate) * rows).astype(BF16)


def block_output(back, columns, ids, logits, hidden, tile=256):
    rows, width = hidden.shape
    experts = logits.shape[0]
    count = back.shape[0]
    row_spec = pl.BlockSpec((tile, width), lambda t: (t, 0))
    return pl.pallas_call(
        block_out_kernel,
        grid=(rows // tile,),
        in_specs=[
            pl.BlockSpec((count, width), lambda t: (0, 0)),
            pl.BlockSpec((tile, 2), lambda t: (t, 0)),
            pl.BlockSpec((1, tile), lambda t: (0, t)),
            pl.BlockSpec((experts, tile), lambda t: (0, t)),
            row_spec,
        ],
        out_specs=row_spec,
        out_shape=jax.ShapeDtypeStruct((rows, width), BF16),
        compiler_params=params("arbitrary"),
        cost_estimate=cost(COVER, 4096),
        name="block_output",
    )(back, columns, ids, logits, hidden)


def unpack_expert_kernel(hidden, packed_ref, in_ref, down_ref, bias_ref):
    width = in_ref.shape[0]
    in_ref[...] = packed_ref[:width, :hidden].astype(F32)
    down_ref[...] = packed_ref[width : width + hidden, :].astype(F32)
    bias_ref[...] = packed_ref[width + hidden :, :].astype(F32)


def unpack_expert(packed, hidden):
    rows, width = packed.shape
    return pl.pallas_call(
        functools.partial(unpack_expert_kernel, hidden),
        out_shape=[
            jax.ShapeDtypeStruct((width, hidden), F32),
            jax.ShapeDtypeStruct((hidden, width), F32),
            jax.ShapeDtypeStruct((EXTRA, width), F32),
        ],
        compiler_params=params(),
        cost_estimate=cost(COVER, 4096),
        name="unpack_expert",
    )(packed)


def unpack_kernel(lead, upper_ref, own_ref, other_ref, *refs):
    outs = refs[len(refs) - (3 + lead) :]
    width = outs[-1].shape[1]

    def write(ref):
        base = 0
        if lead:
            base = outs[0].shape[1]
            outs[0][...] = ref[:, :base].astype(F32)
        for place in range(0, width, PAIR):
            for index in range(3):
                first = base + 3 * place + index * PAIR
                outs[lead + index][:, place : place + PAIR] = ref[:, first : first + PAIR].astype(F32)

    own = pl.program_id(0) == upper_ref[0, 0]

    @pl.when(own)
    def _():
        write(own_ref)

    @pl.when(jnp.logical_not(own))
    def _():
        write(other_ref)


def unpack(upper, own, other, blocks, width, lead, earlier=()):
    total, lanes = own.shape
    rows = total // blocks
    span = (lanes - lead * width) // 3
    offset = 0 if lead else width // span - 1
    source = pl.BlockSpec((rows, lanes), lambda c, x: (x, 0))
    return pl.pallas_call(
        functools.partial(unpack_kernel, lead),
        grid=(2, blocks),
        in_specs=[pl.BlockSpec(memory_space=pltpu.SMEM), source, source]
        + [pl.BlockSpec(memory_space=pl.ANY)] * len(earlier),
        out_specs=[pl.BlockSpec((rows, width), lambda c, x: (c * blocks + x, 0))] * lead
        + [pl.BlockSpec((rows, span), lambda c, x: (c * blocks + x, offset))] * 3,
        out_shape=[jax.ShapeDtypeStruct((2 * total, width), F32)] * (3 + lead),
        input_output_aliases={3 + index: index for index in range(len(earlier))},
        compiler_params=params("arbitrary", "arbitrary"),
        cost_estimate=cost(COVER, 4096),
        name="unpack",
    )(upper, own, other, *earlier)


def swap(blocks, axis):
    return lax.all_to_all(blocks, axis, split_axis=0, concat_axis=0, tiled=True)


def after(value, *others):
    return lax.optimization_barrier((value,) + others)[0]


def trade(value, axis, bit):
    count = lax.axis_size(axis)
    return lax.ppermute(value, axis, [(place, place ^ bit) for place in range(count)])


def bits(axis):
    count, bit = lax.axis_size(axis), 1
    while bit < count:
        yield bit
        bit *= 2


def narrow_sum(value):
    for bit in bits("narrow"):
        value = value + trade(value, "narrow", bit)
    return value


def is_upper(axis, bit):
    return (lax.axis_index(axis) // bit) % 2


def halve(value, axis, bit):
    upper = is_upper(axis, bit)
    halves = value.reshape((2, value.shape[0] // 2) + value.shape[1:])
    mine = lax.dynamic_index_in_dim(halves, upper, 0, keepdims=False)
    other = lax.dynamic_index_in_dim(halves, 1 - upper, 0, keepdims=False)
    return (mine.astype(F32) + trade(other, axis, bit).astype(F32)).astype(value.dtype)


def rejoin(value, axis, bit):
    got = trade(value, axis, bit)
    upper = is_upper(axis, bit) == 1
    low = jnp.concatenate([value, got], axis=0)
    return jnp.where(upper, jnp.concatenate([got, value], axis=0), low)


def spread_out(value, axis):
    count = lax.axis_size(axis)
    copies = jnp.broadcast_to(value[None], (count,) + value.shape)
    return swap(copies, axis)


def narrow_part(value):
    for bit in bits("narrow"):
        value = halve(value, "narrow", bit)
    return value


def wide_part(value):
    width = value.shape[1]
    count = lax.axis_size("wide")
    parts = swap(value.reshape(count, -1, width), "wide")
    return jnp.sum(parts.astype(F32), axis=0).astype(value.dtype)


def wide_whole(value):
    return spread_out(value, "wide").reshape(-1, value.shape[1])


def narrow_half(value):
    for bit in reversed(list(bits("narrow"))[1:]):
        value = rejoin(value, "narrow", bit)
    return value, trade(value, "narrow", 1)


def small_sum(value):
    for axis in ("narrow", "wide"):
        for bit in bits(axis):
            value = value + trade(value, axis, bit)
    return value


def per_device(
    tokens,
    grad_out,
    routes,
    group_counts,
    group_weights,
    norm1_gain,
    norm1_bias,
    w_query,
    bias_query,
    w_key,
    w_value,
    bias_value,
    w_out,
    bias_out,
    norm2_gain,
    norm2_bias,
    router,
    w_in,
    bias_in,
    w_down,
    bias_down,
):
    rows, width = tokens.shape
    experts = router.shape[1]
    assert rows == SEQ_LEN and w_in.shape[0] == 1
    hidden_cols = w_in.shape[2]
    wide_count = lax.axis_size("wide")
    narrow_count = lax.axis_size("narrow")
    devices = wide_count * narrow_count
    capacity = 2 * rows // experts
    half = capacity // 2
    total_tokens = rows * devices
    row = lambda vector: vector.reshape(1, -1)

    sequence = lax.axis_index(("wide", "narrow"))
    group_ends = jnp.cumsum(group_counts, dtype=jnp.int32)
    member = ((sequence >= group_ends - group_counts) & (sequence < group_ends)).astype(F32)
    factor = group_weights.astype(F32) * devices / (group_counts.shape[0] * group_counts.astype(F32))
    weight = jnp.sum(member * factor).reshape(1, 1)
    ids = routes.reshape(1, rows)
    router_rows = jnp.transpose(router)

    slots, columns, grad_outgoing = route(routes, grad_out, experts, capacity)
    grad_rows = swap(grad_outgoing, "wide")
    gathered_in = lax.all_gather(w_in[0], "narrow", axis=0)
    gathered_down = lax.all_gather(w_down[0], "narrow", axis=0)

    normed_t, queries, keys, values = project(
        tokens, row(norm1_gain), row(norm1_bias), w_query, row(bias_query), w_key, w_value, row(bias_value)
    )
    context, soft_weights = attend(queries, keys, values)
    hidden, moe_in, logits = settle(
        context, tokens, w_out, row(bias_out), row(norm2_gain), row(norm2_bias), router_rows
    )
    first, second = dispatch(weight, slots, ids, logits, moe_in, capacity)
    gathered_bias = lax.all_gather(after(bias_in, first), "narrow", axis=0)
    x0 = swap(after(first, grad_rows), "wide")
    counted = jnp.sum(grad_rows[:, capacity, :experts].astype(F32), axis=0)
    fraction = narrow_sum(counted) / total_tokens
    x1 = swap(after(second, x0, fraction), "wide")
    act, up, out, back0, dots = expert(
        x0, grad_rows, gathered_in, gathered_bias, gathered_down, bias_down, 0
    )
    back0 = swap(after(back0, x1), "wide")
    act, up, expert_out, back1 = expert(
        x1, grad_rows, gathered_in, gathered_bias, gathered_down, bias_down, 1, (act, up, out, dots)
    )
    back1 = arrived = swap(after(back1, back0), "wide")
    scale = jnp.sum(x1[:, half : half + 3, :capacity].astype(F32), axis=1)
    scale = jnp.transpose(scale.reshape(wide_count, 2, half), (1, 0, 2)).reshape(2, 1, wide_count * half)
    expert_sums = weight_grads(after(x0, back0), x1, grad_rows, act, up, scale)
    expert_grad = lax.psum_scatter(after(expert_sums, arrived), "narrow", scatter_dimension=0)
    grad_w_in, grad_w_down, bias_rows = unpack_expert(expert_grad, hidden_cols)
    share = width // narrow_count
    grad_bias_in = bias_rows[0:1, :hidden_cols]
    grad_bias_down = lax.dynamic_slice_in_dim(
        bias_rows[1:2], lax.axis_index("narrow") * share, share, 1
    )
    back1 = after(back1, expert_sums)
    returned = swap(after(expert_out, arrived), "wide")

    extras = jnp.transpose(back1[:, half:, :half], (1, 0, 2))
    dots1 = jnp.pad(extras, ((0, 0), (0, 0), (0, EXTRA))).reshape(EXTRA, experts * (half + EXTRA))
    dots0 = jnp.concatenate([extras[3:], extras[:3]], axis=0).reshape(EXTRA, experts * half)
    pull = (BALANCE * experts * fraction).reshape(experts, 1)
    hid_grad, con_grad, out_grad, sums, router_grad, prob_sums = combine(
        weight,
        back0.reshape(experts * half, width),
        back1.reshape(experts * (half + EXTRA), width),
        dots0,
        dots1,
        columns,
        ids,
        logits,
        pull,
        hidden,
        grad_out,
        context,
        moe_in,
        w_out,
        router_rows,
        row(norm2_gain),
    )
    pairs = width // PAIR
    span = pairs // ATTEND_CALLS
    grads, bias_sums = [], []
    packed = [narrow_part(out_grad)]
    for call in range(ATTEND_CALLS):
        dq, dk, dv, weights, column_sums = attend_back(
            queries, keys, values, soft_weights, con_grad, normed_t, call * span, span
        )
        grads.append((dq, dk, dv))
        packed.append(narrow_part(weights))
        bias_sums.append(column_sums)
    early = jnp.concatenate(packed[:-1], axis=1)
    hid_grad = after(hid_grad, early)
    grad_tokens, norm_sums = close(grads, tokens, hid_grad, row(norm1_gain), w_query, w_key, w_value)
    block_out = block_output(
        returned.reshape(experts * capacity, width), columns, ids, logits, hidden
    )
    bias_sums = jnp.concatenate(bias_sums, axis=1)
    prob_row = jnp.pad(prob_sums.reshape(1, experts), ((0, 0), (0, width - experts)))
    small = small_sum(
        jnp.concatenate([norm_sums[:2], bias_sums[:2], sums[:3], prob_row, router_grad], axis=0)
    )
    early = wide_part(after(early, returned))
    late = wide_part(after(packed[-1], early, norm_sums))
    early = wide_whole(after(early, late, small))
    late = wide_whole(after(late, early, bias_rows, block_out))
    early, early_other = narrow_half(early)
    late, late_other = narrow_half(late)
    balance_loss = experts * jnp.sum(fraction * (small[7, :experts] / total_tokens))
    upper = is_upper("narrow", 1).astype(jnp.int32).reshape(1, 1)
    blocks = narrow_count // 2
    grad_w_out, *weights = unpack(upper, early, early_other, blocks, width, 1)
    weights = unpack(upper, late, late_other, blocks, width, 0, weights)
    return (
        block_out,
        balance_loss,
        grad_tokens,
        small[0],
        small[1],
        weights[0],
        small[2],
        weights[1],
        weights[2],
        small[3],
        grad_w_out,
        small[6],
        small[4],
        small[5],
        jnp.transpose(small[8:]),
        grad_w_in[None],
        grad_bias_in,
        grad_w_down[None],
        grad_bias_down,
    )


def solution(mesh):
    return jax.shard_map(
        per_device,
        mesh=mesh,
        in_specs=(
            P(("wide", "narrow"), None),
            P(("wide", "narrow"), None),
            P(("wide", "narrow"), None),
            P(),
            P(),
            P(),
            P(),
            P(),
            P(),
            P(),
            P(),
            P(),
            P(),
            P(),
            P(),
            P(),
            P(),
            P("wide", None, "narrow"),
            P("wide", "narrow"),
            P("wide", "narrow", None),
            P("wide", None),
        ),
        out_specs=(
            P(("wide", "narrow"), None),
            P(),
            P(("wide", "narrow"), None),
            P(),
            P(),
            P(),
            P(),
            P(),
            P(),
            P(),
            P(),
            P(),
            P(),
            P(),
            P(),
            P("wide", None, "narrow"),
            P("wide", "narrow"),
            P("wide", "narrow", None),
            P("wide", "narrow"),
        ),
        check_vma=False,
    )
```

```python
import functools
import jax
import jax.numpy as jnp
from jax import lax
from jax.experimental import pallas as pl
from jax.experimental.pallas import tpu as pltpu
from jax.sharding import PartitionSpec as P

HEADS = 12
HEAD_DIM = 64
SEQ_LEN = 1024
EPS = 1e-05
BALANCE = 48.0
NEGATIVE = -1e30
PAIR = 2 * HEAD_DIM
F32 = jnp.float32
BF16 = jnp.bfloat16
VMEM_LIMIT = 56 * 1024 * 1024
EXTRA = 8
COVER = 4e10
ATTEND_CALLS = 2


def mm(left, right):
    return lax.dot_general(left, right, (((1,), (0,)), ((), ())), preferred_element_type=F32)


def mm_nt(left, right):
    return lax.dot_general(left, right, (((1,), (1,)), ((), ())), preferred_element_type=F32)


def mm_tn(left, right):
    return lax.dot_general(left, right, (((0,), (0,)), ((), ())), preferred_element_type=F32)


def cost(flops, nbytes, trans=0):
    return pl.CostEstimate(flops=int(flops), bytes_accessed=int(nbytes), transcendentals=int(trans))


def params(*semantics):
    return pltpu.CompilerParams(dimension_semantics=semantics, vmem_limit_bytes=VMEM_LIMIT)


def head_mask(block, head):
    lanes = lax.broadcasted_iota(jnp.int32, block.shape, 1)
    return jnp.where(lanes // HEAD_DIM == head, block, jnp.zeros_like(block))


def causal(scores, block):
    keys = scores.shape[0]
    first = lax.broadcasted_iota(jnp.int32, (block, block), 0)
    second = lax.broadcasted_iota(jnp.int32, (block, block), 1)
    last = jnp.where(first <= second, scores[keys - block :], NEGATIVE)
    if keys == block:
        return last
    return jnp.concatenate([scores[: keys - block], last], axis=0)


def attend_kernel(block, q_ref, k_ref, v_ref, context_ref, weights_ref):
    rows = q_ref.shape[0]
    keys = k_ref[...]
    values = v_ref[...]
    place = 0
    for first in range(0, rows, block):
        span = first + block
        query = q_ref[first:span, :]
        weights_both, values_both = [], []
        for head in range(2):
            scores = causal(mm_nt(keys[:span], head_mask(query, head)), block)
            peak = jnp.max(scores, axis=0, keepdims=True)
            powers = jnp.exp(scores - peak)
            total = jnp.sum(powers, axis=0, keepdims=True)
            weights = (powers * (1.0 / total)).astype(BF16)
            weights_ref[0, head, place : place + span, :] = weights
            weights_both.append(weights)
            values_both.append(head_mask(values[:span], head))
        out = mm_tn(jnp.concatenate(weights_both, axis=0), jnp.concatenate(values_both, axis=0))
        context_ref[first:span, :] = out.astype(BF16)
        place += span


def attend(queries, keys, values, block=256):
    rows, width = queries.shape
    pairs = width // PAIR
    kept = sum(range(block, rows + 1, block))
    spec = pl.BlockSpec((rows, PAIR), lambda p: (0, p))
    return pl.pallas_call(
        functools.partial(attend_kernel, block),
        grid=(pairs,),
        in_specs=[spec, spec, spec],
        out_specs=[spec, pl.BlockSpec((1, 2, kept, block), lambda p: (p, 0, 0, 0))],
        out_shape=[
            jax.ShapeDtypeStruct((rows, width), BF16),
            jax.ShapeDtypeStruct((pairs, 2, kept, block), BF16),
        ],
        compiler_params=params("arbitrary"),
        cost_estimate=cost(4 * rows * rows * width * 2, rows * width * 8, pairs * 2 * rows * rows),
        name="attend",
    )(queries, keys, values)


def attend_back_kernel(block, q_ref, k_ref, v_ref, weights_ref, g_ref, normed_ref,
                       dq_ref, dk_ref, dv_ref, packed_ref, sums_ref, dq_acc, dk_acc, dv_acc):
    rows = q_ref.shape[0]
    keys = k_ref[...]
    values = v_ref[...]
    place = weights_ref.shape[2]
    for first in reversed(range(0, rows, block)):
        span = first + block
        place -= span
        query = q_ref[first:span, :]
        grad = g_ref[first:span, :]
        probs_both, scores_both, query_both, grad_both = [], [], [], []
        for head in range(2):
            query_h = head_mask(query, head)
            grad_h = head_mask(grad, head)
            weights = weights_ref[0, head, place : place + span, :]
            probs = weights.astype(F32)
            grad_probs = mm_nt(values[:span], grad_h)
            inner = jnp.sum(probs * grad_probs, axis=0, keepdims=True)
            grad_scores = (probs * (grad_probs - inner)).astype(BF16)
            probs_both.append(weights)
            scores_both.append(grad_scores)
            query_both.append(query_h)
            grad_both.append(grad_h)
        dv = mm(jnp.concatenate(probs_both, axis=1), jnp.concatenate(grad_both, axis=0))
        dk = mm(jnp.concatenate(scores_both, axis=1), jnp.concatenate(query_both, axis=0))
        if span == rows:
            dv_acc[...] = dv
            dk_acc[...] = dk
        else:
            dv_acc[:span, :] += dv
            dk_acc[:span, :] += dk
        keys_both = jnp.concatenate([head_mask(keys[:span], head) for head in range(2)], axis=0)
        dq = mm_tn(jnp.concatenate(scores_both, axis=0), keys_both) * 0.125
        dq_acc[first:span, :] = dq.astype(BF16)
    dq = dq_acc[...]
    dk = dk_acc[...].astype(BF16)
    dv = dv_acc[...].astype(BF16)
    dq_ref[...] = dq
    dk_ref[...] = dk
    dv_ref[...] = dv
    normed = normed_ref[...]
    packed_ref[:, : 2 * PAIR] = mm(normed, jnp.concatenate([dq, dk], axis=1)).astype(BF16)
    packed_ref[:, 2 * PAIR :] = mm(normed, dv).astype(BF16)
    sums_ref[...] = jnp.concatenate(
        [
            jnp.sum(dq.astype(F32), axis=0, keepdims=True),
            jnp.sum(dv.astype(F32), axis=0, keepdims=True),
            jnp.zeros((6, PAIR), F32),
        ],
        axis=0,
    )


def attend_back(queries, keys, values, weights, grad_context, normed_t, start, pairs, block=256):
    rows, width = queries.shape
    spec = pl.BlockSpec((rows, PAIR), lambda p: (0, p + start))
    out_spec = pl.BlockSpec((rows, PAIR), lambda p: (0, p))
    return pl.pallas_call(
        functools.partial(attend_back_kernel, block),
        grid=(pairs,),
        in_specs=[
            spec,
            spec,
            spec,
            pl.BlockSpec((1, 2) + weights.shape[2:], lambda p: (p + start, 0, 0, 0)),
            spec,
            pl.BlockSpec((width, rows), lambda p: (0, 0)),
        ],
        out_specs=[
            out_spec,
            out_spec,
            out_spec,
            pl.BlockSpec((width, 3 * PAIR), lambda p: (0, p)),
            pl.BlockSpec((8, PAIR), lambda p: (0, p)),
        ],
        out_shape=[jax.ShapeDtypeStruct((rows, pairs * PAIR), BF16)] * 3
        + [
            jax.ShapeDtypeStruct((width, 3 * pairs * PAIR), BF16),
            jax.ShapeDtypeStruct((8, pairs * PAIR), F32),
        ],
        scratch_shapes=[
            pltpu.VMEM((rows, PAIR), BF16),
            pltpu.VMEM((rows, PAIR), F32),
            pltpu.VMEM((rows, PAIR), F32),
        ],
        compiler_params=params("arbitrary"),
        cost_estimate=cost(rows, rows),
        name="attend_back",
    )(queries, keys, values, weights, grad_context, normed_t)


def normalise(values):
    centred = values - jnp.mean(values, axis=-1, keepdims=True)
    spread = lax.rsqrt(jnp.mean(centred * centred, axis=-1, keepdims=True) + EPS)
    return centred * spread, spread


def normalise_back(grad, unit, spread, gain):
    scaled = grad * gain
    mean = jnp.mean(scaled, axis=-1, keepdims=True)
    tilt = jnp.mean(scaled * unit, axis=-1, keepdims=True)
    return spread * (scaled - mean - unit * tilt)


def pieces(values):
    high = values.astype(BF16)
    rest = values - high.astype(F32)
    middle = rest.astype(BF16)
    low = (rest - middle.astype(F32)).astype(BF16)
    fill = jnp.zeros((5, values.shape[1]), F32)
    stacked = jnp.concatenate(
        [high.astype(F32), middle.astype(F32), low.astype(F32), fill], axis=0
    )
    return stacked.astype(BF16)


def join(parts):
    return parts[0:1] + parts[1:2] + parts[2:3]


def column(row):
    return jnp.transpose(jnp.broadcast_to(row, (8, row.shape[1])))[:, 0:1]


def gate_row(logits, picked):
    return jax.nn.sigmoid(jnp.sum(jnp.where(picked, logits, 0.0), axis=0, keepdims=True))


def picked_rows(ids, experts):
    return lax.broadcasted_iota(jnp.int32, (experts, ids.shape[1]), 0) == ids


def one_hot_rows(slots, first, count):
    places = lax.broadcasted_iota(jnp.int32, (count, slots.shape[1]), 0) + first
    return (places == slots).astype(F32).astype(BF16)


def one_hot_columns(slots, first, count):
    places = lax.broadcasted_iota(jnp.int32, (slots.shape[0], count), 1) + first
    return (places == slots).astype(F32).astype(BF16)


def route_kernel(experts, capacity, row_ref, grad_ref, slots_ref, columns_ref, out_ref, count_row):
    step = pl.program_id(0)
    rows = row_ref.shape[1]
    width = grad_ref.shape[1]
    half = capacity // 2

    @pl.when(step == 0)
    def _():
        block = 256
        ids = row_ref[...]
        picked = picked_rows(ids, experts).astype(F32)
        first = lax.broadcasted_iota(jnp.int32, (block, block), 0)
        second = lax.broadcasted_iota(jnp.int32, (block, block), 1)
        earlier = (first < second).astype(F32).astype(BF16)
        passed = jnp.zeros((experts, 1), F32)
        places = []
        for start in range(0, rows, block):
            own = picked[:, start : start + block]
            before = mm(own.astype(BF16), earlier) + passed
            places.append(jnp.sum(before * own, axis=0, keepdims=True))
            passed = passed + jnp.sum(own, axis=1, keepdims=True)
        place = jnp.concatenate(places, axis=1).astype(jnp.int32)
        slots = ids * capacity + place
        late = experts * half + ids * (half + EXTRA) + place - half
        mixed = jnp.where(place < half, ids * half + place, late)
        slots_ref[...] = slots
        both = jnp.concatenate([mixed, slots, jnp.zeros((6, rows), jnp.int32)], axis=0)
        columns_ref[...] = jnp.transpose(both.astype(F32))[:, 0:2].astype(jnp.int32)
        count_row[...] = jnp.zeros_like(count_row)
        lanes = lax.broadcasted_iota(jnp.int32, (experts, 128), 1)
        spread = jnp.where(lanes == lax.broadcasted_iota(jnp.int32, (experts, 128), 0), passed, 0.0)
        count_row[0:1, 0:128] = jnp.sum(spread, axis=0, keepdims=True)

    chosen = one_hot_rows(slots_ref[...], step * capacity, capacity)
    out_ref[0, :capacity, :] = mm(chosen, grad_ref[...]).astype(BF16)
    out_ref[0, capacity:, :] = count_row[...].astype(BF16)


def route(routes, grad_out, experts, capacity):
    rows, width = grad_out.shape
    whole = lambda e: (0, 0)
    return pl.pallas_call(
        functools.partial(route_kernel, experts, capacity),
        grid=(experts,),
        in_specs=[
            pl.BlockSpec((1, rows), whole),
            pl.BlockSpec((rows, width), whole),
        ],
        out_specs=[
            pl.BlockSpec((1, rows), whole),
            pl.BlockSpec((rows, 2), whole),
            pl.BlockSpec((1, capacity + EXTRA, width), lambda e: (e, 0, 0)),
        ],
        out_shape=[
            jax.ShapeDtypeStruct((1, rows), jnp.int32),
            jax.ShapeDtypeStruct((rows, 2), jnp.int32),
            jax.ShapeDtypeStruct((experts, capacity + EXTRA, width), BF16),
        ],
        scratch_shapes=[pltpu.VMEM((EXTRA, width), F32)],
        compiler_params=params("arbitrary"),
        cost_estimate=cost(2 * experts * capacity * rows * width, 6 * rows * width),
        name="route",
    )(routes.reshape(1, rows), grad_out)


def project_kernel(tokens_ref, gain_ref, shift_ref, wq_ref, bq_ref, wk_ref, wv_ref, bv_ref,
                   normed_ref, q_ref, k_ref, v_ref):
    unit, _ = normalise(tokens_ref[...].astype(F32))
    normed = (unit * gain_ref[...] + shift_ref[...]).astype(BF16)
    normed_ref[...] = jnp.transpose(normed)
    q_ref[...] = ((mm(normed, wq_ref[...]) + bq_ref[...]) * 0.125).astype(BF16)
    k_ref[...] = mm(normed, wk_ref[...]).astype(BF16)
    v_ref[...] = (mm(normed, wv_ref[...]) + bv_ref[...]).astype(BF16)


def project(tokens, gain, shift, w_query, bias_query, w_key, w_value, bias_value, tile=256):
    rows, width = tokens.shape
    row_spec = pl.BlockSpec((tile, width), lambda t: (t, 0))
    vector = pl.BlockSpec((1, width), lambda t: (0, 0))
    square = pl.BlockSpec((width, width), lambda t: (0, 0))
    return pl.pallas_call(
        project_kernel,
        grid=(rows // tile,),
        in_specs=[row_spec, vector, vector, square, vector, square, square, vector],
        out_specs=[pl.BlockSpec((width, tile), lambda t: (0, t))] + [row_spec] * 3,
        out_shape=[jax.ShapeDtypeStruct((width, rows), BF16)]
        + [jax.ShapeDtypeStruct((rows, width), BF16)] * 3,
        compiler_params=params("arbitrary"),
        cost_estimate=cost(6 * rows * width * width, 10 * rows * width + 6 * width * width),
        name="project",
    )(tokens, gain, shift, w_query, bias_query, w_key, w_value, bias_value)


def settle_kernel(context_ref, tokens_ref, w_out_ref, bias_ref, gain_ref, shift_ref, router_ref,
                  hidden_ref, moe_ref, logits_ref):
    hidden = tokens_ref[...].astype(F32) + mm(context_ref[...], w_out_ref[...]) + bias_ref[...]
    unit, _ = normalise(hidden)
    moe_in = (unit * gain_ref[...] + shift_ref[...]).astype(BF16)
    hidden_ref[...] = hidden
    moe_ref[...] = moe_in
    logits_ref[...] = mm_nt(router_ref[...], moe_in)


def settle(context, tokens, w_out, bias_out, gain, shift, router_rows, tile=256):
    rows, width = tokens.shape
    experts = router_rows.shape[0]
    row_spec = pl.BlockSpec((tile, width), lambda t: (t, 0))
    vector = pl.BlockSpec((1, width), lambda t: (0, 0))
    return pl.pallas_call(
        settle_kernel,
        grid=(rows // tile,),
        in_specs=[
            row_spec,
            row_spec,
            pl.BlockSpec((width, width), lambda t: (0, 0)),
            vector,
            vector,
            vector,
            pl.BlockSpec((experts, width), lambda t: (0, 0)),
        ],
        out_specs=[row_spec, row_spec, pl.BlockSpec((experts, tile), lambda t: (0, t))],
        out_shape=[
            jax.ShapeDtypeStruct((rows, width), F32),
            jax.ShapeDtypeStruct((rows, width), BF16),
            jax.ShapeDtypeStruct((experts, rows), F32),
        ],
        compiler_params=params("arbitrary"),
        cost_estimate=cost(2 * rows * width * width, 10 * rows * width + 2 * width * width),
        name="settle",
    )(context, tokens, w_out, bias_out, gain, shift, router_rows)


def dispatch_kernel(weight_ref, slots_ref, ids_ref, logits_ref, moe_ref, first_ref, second_ref, parts):
    step = pl.program_id(0)
    experts = logits_ref.shape[0]
    half = first_ref.shape[1]

    @pl.when(step == 0)
    def _():
        gate = gate_row(logits_ref[...], picked_rows(ids_ref[...], experts))
        parts[...] = pieces(gate * weight_ref[0, 0])

    chosen = one_hot_rows(slots_ref[...], step * 2 * half, 2 * half)
    rows = mm(chosen, moe_ref[...]).astype(BF16)
    first_ref[0] = rows[:half]
    second_ref[0, :half, :] = rows[half:]
    second_ref[0, half:, :] = jnp.zeros((EXTRA, rows.shape[1]), BF16)
    second_ref[0, half:, 0 : 2 * half] = mm_nt(parts[...], chosen).astype(BF16)


def dispatch(weight, slots, ids, logits, moe_in, capacity):
    rows, width = moe_in.shape
    experts = logits.shape[0]
    half = capacity // 2
    whole = lambda e: (0, 0)
    return pl.pallas_call(
        dispatch_kernel,
        grid=(experts,),
        in_specs=[
            pl.BlockSpec(memory_space=pltpu.SMEM),
            pl.BlockSpec((1, rows), whole),
            pl.BlockSpec((1, rows), whole),
            pl.BlockSpec((experts, rows), whole),
            pl.BlockSpec((rows, width), whole),
        ],
        out_specs=[
            pl.BlockSpec((1, half, width), lambda e: (e, 0, 0)),
            pl.BlockSpec((1, half + EXTRA, width), lambda e: (e, 0, 0)),
        ],
        out_shape=[
            jax.ShapeDtypeStruct((experts, half, width), BF16),
            jax.ShapeDtypeStruct((experts, half + EXTRA, width), BF16),
        ],
        scratch_shapes=[pltpu.VMEM((8, rows), BF16)],
        compiler_params=params("arbitrary"),
        cost_estimate=cost(2 * experts * capacity * rows * width, 6 * rows * width),
        name="dispatch",
    )(weight, slots, ids, logits, moe_in)


def row_sum(values):
    ones = jnp.ones((8, values.shape[1]), BF16)
    high = values.astype(BF16)
    rest = values - high.astype(F32)
    middle = rest.astype(BF16)
    low = (rest - middle.astype(F32)).astype(BF16)
    return (mm_nt(ones, high) + mm_nt(ones, middle) + mm_nt(ones, low))[0:1]


def expert_kernel(steps, chunk, *refs):
    if chunk == 0:
        (x_ref, g_ref, w_in_ref, b_in_ref, w_down_ref, b_down_ref,
         act_ref, up_ref, out_ref, back_ref, dot_ref, back_acc, dot_acc, out_acc) = refs
    else:
        (x_ref, g_ref, w_in_ref, b_in_ref, w_down_ref, b_down_ref, _, _, _, earlier_ref,
         act_ref, up_ref, out_ref, back_ref, back_acc, dot_acc, out_acc) = refs
    part = pl.program_id(0)
    tile = pl.program_id(1)
    group, half, width = x_ref.shape
    rows = group * half
    x = x_ref[...].reshape(rows, width)
    g = g_ref[...].reshape(rows, width)
    w_in = w_in_ref[0]
    pre = mm(x, w_in) + b_in_ref[0].astype(F32)
    grad_act = mm_nt(g, w_down_ref[0])
    below = 0.5 + 0.5 * lax.erf(pre * 0.7071067811865476)
    act = pre * below
    slope = below + pre * (0.3989422804014327 * jnp.exp(-0.5 * pre * pre))
    up = (grad_act * slope).astype(BF16)
    rounded = act.astype(BF16)
    act_ref[0, 0] = rounded
    up_ref[0, 0] = up
    out = mm(rounded, w_down_ref[0])
    product = act * grad_act
    lanes = min(128, product.shape[1])
    folded = product[:, :lanes]
    for lane in range(lanes, product.shape[1], lanes):
        folded = folded + product[:, lane : lane + lanes]
    where = pl.ds(pl.multiple_of(tile * rows, rows), rows)
    back = mm_nt(up, w_in)

    @pl.when(part == 0)
    def _():
        biased = g.astype(F32) * b_down_ref[...].astype(F32)
        total = folded
        for lane in range(0, biased.shape[1], lanes):
            total = total + biased[:, lane : lane + lanes]
        back_acc[where, :] = back
        out_acc[where, :] = out + b_down_ref[...].astype(F32)
        dot_acc[where, :] = total

    @pl.when(part > 0)
    def _():
        back_acc[where, :] += back
        out_acc[where, :] += out
        dot_acc[where, :] += folded

    @pl.when(part == steps - 1)
    def _():
        out_ref[...] = out_acc[where, :].astype(BF16).reshape(group, half, width)
        back_ref[:, :half, :] = back_acc[where, :].astype(BF16).reshape(group, half, width)
        dots = dot_acc[where, :]
        for index in range(group):
            own = pieces(row_sum(dots[index * half : (index + 1) * half, :])).astype(F32)
            if chunk == 0:
                dot_ref[index] = own.astype(BF16)
            else:
                before = earlier_ref[index].astype(F32)
                extra = jnp.concatenate([own[0:3], before[0:3], own[6:8]], axis=0)
                back_ref[index, half:, :] = jnp.zeros((EXTRA, width), BF16)
                back_ref[index, half:, 0:half] = extra.astype(BF16)


def expert(x, g, w_in, b_in, w_down, b_down, chunk, earlier=()):
    sources, width = x.shape[0], x.shape[2]
    half = (g.shape[1] - EXTRA) // 2
    rows = sources * half
    parts, _, hidden = w_in.shape
    group = max(1, 256 // half)
    tile = group * half
    tiles = sources // group
    last = parts - 1
    late = lambda p, t: jnp.where(p == last, t, 0)
    wide_spec = pl.BlockSpec((1, 1, tile, hidden), lambda p, t: (p, chunk, t, 0))
    wide_shape = jax.ShapeDtypeStruct((parts, 2, rows, hidden), BF16)
    dot_shape = jax.ShapeDtypeStruct((sources, 8, half), BF16)
    dot_spec = pl.BlockSpec((group, 8, half), lambda p, t: (late(p, t), 0, 0))
    back_rows = half + EXTRA * chunk
    return pl.pallas_call(
        functools.partial(expert_kernel, parts, chunk),
        grid=(parts, tiles),
        in_specs=[
            pl.BlockSpec((group, half, width), lambda p, t: (t, 0, 0)),
            pl.BlockSpec((group, half, width), lambda p, t: (t, chunk, 0)),
            pl.BlockSpec((1, width, hidden), lambda p, t: (p, 0, 0)),
            pl.BlockSpec((1, 1, hidden), lambda p, t: (p, 0, 0)),
            pl.BlockSpec((1, hidden, width), lambda p, t: (p, 0, 0)),
            pl.BlockSpec((1, width), lambda p, t: (0, 0)),
        ]
        + ([pl.BlockSpec(memory_space=pl.ANY)] * 3 + [dot_spec] if chunk else []),
        out_specs=[
            wide_spec,
            wide_spec,
            pl.BlockSpec((group, half, width), lambda p, t: (late(p, t), chunk, 0)),
            pl.BlockSpec((group, back_rows, width), lambda p, t: (late(p, t), 0, 0)),
        ]
        + ([] if chunk else [dot_spec]),
        out_shape=[
            wide_shape,
            wide_shape,
            jax.ShapeDtypeStruct((sources, 2 * half, width), BF16),
            jax.ShapeDtypeStruct((sources, back_rows, width), BF16),
        ]
        + ([] if chunk else [dot_shape]),
        scratch_shapes=[
            pltpu.VMEM((rows, width), F32),
            pltpu.VMEM((rows, min(128, hidden)), F32),
            pltpu.VMEM((rows, width), F32),
        ],
        input_output_aliases={6: 0, 7: 1, 8: 2} if chunk else {},
        compiler_params=params("arbitrary", "arbitrary"),
        cost_estimate=cost(
            6 * rows * width * hidden * parts, rows * hidden * parts * 4, 2 * rows * hidden * parts
        ),
        name="expert",
    )(x, g, w_in, b_in, w_down, b_down, *earlier)


def weight_kernel(parts, x0_ref, x1_ref, g_ref, act_ref, up_ref, scale_ref,
                  down_ref, in_ref, down_acc, in_acc, bias_acc, bias_down_acc, flipped):
    part = pl.program_id(0)
    chunk = pl.program_id(1)
    sources, half, width = x0_ref.shape
    rows = sources * half
    hidden = act_ref.shape[3]
    scale = scale_ref[0]
    split = pieces(scale)
    g = g_ref[...].reshape(rows, width)

    def flip(values):
        return (jnp.transpose(values).astype(F32) * scale).astype(BF16)

    @pl.when((part == 0) & (chunk == 0))
    def _():
        flipped[0] = flip(x0_ref[...].reshape(rows, width))

    @pl.when((part == 0) & (chunk == 1))
    def _():
        flipped[1] = flip(x1_ref[...].reshape(rows, width))

    act = act_ref[0, 0]
    up = up_ref[0, 0]
    down = mm(flip(act), g)
    into = mm(flipped[chunk], up)
    bias_in = join(mm(split, up))

    @pl.when(chunk == 0)
    def _():
        down_acc[...] = down
        in_acc[...] = into
        bias_acc[...] = bias_in

    @pl.when(chunk == 1)
    def _():
        down_ref[0, :hidden, :] = (down_acc[...] + down).astype(BF16)
        in_ref[0] = (in_acc[...] + into).astype(BF16)

    @pl.when(part == 0)
    def _():
        bias_down = join(mm(split, g))
        bias_down_acc[...] = jnp.where(chunk == 0, bias_down, bias_down_acc[...] + bias_down)

    @pl.when(chunk == 1)
    def _():
        down_ref[0, hidden:, :] = jnp.zeros((EXTRA, width), BF16)
        down_ref[0, hidden : hidden + 1, 0:hidden] = (bias_acc[...] + bias_in).astype(BF16)
        down_ref[0, hidden + 1 : hidden + 2, :] = bias_down_acc[...].astype(BF16)


def weight_grads(x0, x1, g, act, up, scale):
    sources, half, width = x0.shape
    parts, _, rows, hidden = act.shape
    wide_spec = pl.BlockSpec((1, 1, rows, hidden), lambda p, t: (p, t, 0, 0))
    return pl.pallas_call(
        functools.partial(weight_kernel, parts),
        grid=(parts, 2),
        in_specs=[
            pl.BlockSpec((sources, half, width), lambda p, t: (0, 0, 0)),
            pl.BlockSpec((sources, half, width), lambda p, t: (0, 0, 0)),
            pl.BlockSpec((sources, half, width), lambda p, t: (0, t, 0)),
            wide_spec,
            wide_spec,
            pl.BlockSpec((1, 1, rows), lambda p, t: (t, 0, 0)),
        ],
        out_specs=[
            pl.BlockSpec((1, hidden + EXTRA, width), lambda p, t: (p, 0, 0)),
            pl.BlockSpec((1, width, hidden), lambda p, t: (p, 0, 0)),
        ],
        out_shape=[
            jax.ShapeDtypeStruct((parts, hidden + EXTRA, width), BF16),
            jax.ShapeDtypeStruct((parts, width, hidden), BF16),
        ],
        scratch_shapes=[
            pltpu.VMEM((hidden, width), F32),
            pltpu.VMEM((width, hidden), F32),
            pltpu.VMEM((1, hidden), F32),
            pltpu.VMEM((1, width), F32),
            pltpu.VMEM((2, width, rows), BF16),
        ],
        compiler_params=params("arbitrary", "arbitrary"),
        cost_estimate=cost(12 * rows * width * hidden * parts, rows * hidden * parts * 8),
        name="weight_grads",
    )(x0, x1, g, act, up, scale)


def combine_kernel(weight_ref, back0_ref, back1_ref, dots0_ref, dots1_ref, columns_ref, ids_ref, logits_ref, pull_ref,
                   hidden_ref, grad_ref, context_ref, moe_ref, w_out_ref, router_ref, gain_ref,
                   hid_grad_ref, con_grad_ref, out_grad_ref, sums_ref, router_grad_ref, probs_ref, branches):
    step = pl.program_id(0)
    experts = logits_ref.shape[0]
    count0 = back0_ref.shape[0]
    count1 = back1_ref.shape[0]
    weight = weight_ref[0, 0]
    columns = columns_ref[:, 0:1]
    chosen0 = one_hot_columns(columns, 0, count0)
    chosen1 = one_hot_columns(columns, count0, count1)
    rows = mm(chosen0, back0_ref[...]) + mm(chosen1, back1_ref[...])
    dots = join(mm_nt(dots0_ref[...], chosen0)) + join(mm_nt(dots1_ref[...], chosen1))
    logits = logits_ref[...]
    picked = picked_rows(ids_ref[...], experts)
    gate = gate_row(logits, picked)
    powers = jnp.exp(logits - jnp.max(logits, axis=0, keepdims=True))
    probs = powers / jnp.sum(powers, axis=0, keepdims=True)
    pull = pull_ref[...]
    slope = dots * weight * gate * (1.0 - gate)
    logit_grad = probs * (pull - jnp.sum(probs * pull, axis=0, keepdims=True))
    logit_grad = (logit_grad + jnp.where(picked, slope, 0.0)).astype(BF16)
    moe_grad = mm_tn(logit_grad, router_ref[...]) + rows * column(gate * weight)
    unit, spread = normalise(hidden_ref[...])
    hid_grad = weight * grad_ref[...].astype(F32) + normalise_back(
        moe_grad, unit, spread, gain_ref[...]
    )
    branch = hid_grad.astype(BF16)
    hid_grad_ref[...] = hid_grad
    con_grad_ref[...] = mm_nt(branch, w_out_ref[...]).astype(BF16)
    branches[pl.ds(pl.multiple_of(step * branch.shape[0], branch.shape[0]), branch.shape[0]), :] = branch
    router_grad = mm(logit_grad, moe_ref[...])
    prob_sum = jnp.sum(probs, axis=1, keepdims=True)
    sums = jnp.concatenate(
        [
            jnp.sum(moe_grad * unit, axis=0, keepdims=True),
            jnp.sum(moe_grad, axis=0, keepdims=True),
            jnp.sum(branch.astype(F32), axis=0, keepdims=True),
            jnp.zeros((5, unit.shape[1]), F32),
        ],
        axis=0,
    )

    @pl.when(step == 0)
    def _():
        router_grad_ref[...] = router_grad
        probs_ref[...] = prob_sum
        sums_ref[...] = sums

    @pl.when(step > 0)
    def _():
        router_grad_ref[...] += router_grad
        probs_ref[...] += prob_sum
        sums_ref[...] += sums

    @pl.when(step == pl.num_programs(0) - 1)
    def _():
        out_grad_ref[...] = mm_tn(context_ref[...], branches[...]).astype(BF16)


def combine(weight, back0, back1, dots0, dots1, columns, ids, logits, pull, hidden, grad_out, context, moe_in,
            w_out, router_rows, gain, tile=256):
    rows, width = hidden.shape
    experts = logits.shape[0]
    count = back0.shape[0]
    count1 = back1.shape[0]
    whole = lambda t: (0, 0)
    row_spec = pl.BlockSpec((tile, width), lambda t: (t, 0))
    square = pl.BlockSpec((width, width), whole)
    return pl.pallas_call(
        combine_kernel,
        grid=(rows // tile,),
        in_specs=[
            pl.BlockSpec(memory_space=pltpu.SMEM),
            pl.BlockSpec((count, width), whole),
            pl.BlockSpec((count1, width), whole),
            pl.BlockSpec((8, count), whole),
            pl.BlockSpec((8, count1), whole),
            pl.BlockSpec((tile, 2), lambda t: (t, 0)),
            pl.BlockSpec((1, tile), lambda t: (0, t)),
            pl.BlockSpec((experts, tile), lambda t: (0, t)),
            pl.BlockSpec((experts, 1), whole),
            row_spec,
            row_spec,
            pl.BlockSpec((rows, width), whole),
            row_spec,
            square,
            pl.BlockSpec((experts, width), whole),
            pl.BlockSpec((1, width), whole),
        ],
        out_specs=[
            row_spec,
            row_spec,
            square,
            pl.BlockSpec((8, width), whole),
            pl.BlockSpec((experts, width), whole),
            pl.BlockSpec((experts, 1), whole),
        ],
        out_shape=[
            jax.ShapeDtypeStruct((rows, width), F32),
            jax.ShapeDtypeStruct((rows, width), BF16),
            jax.ShapeDtypeStruct((width, width), BF16),
            jax.ShapeDtypeStruct((8, width), F32),
            jax.ShapeDtypeStruct((experts, width), F32),
            jax.ShapeDtypeStruct((experts, 1), F32),
        ],
        scratch_shapes=[pltpu.VMEM((rows, width), BF16)],
        compiler_params=params("arbitrary"),
        cost_estimate=cost(rows, rows),
        name="combine",
    )(weight, back0, back1, dots0, dots1, columns, ids, logits, pull, hidden, grad_out, context, moe_in, w_out,
      router_rows, gain)


def close_kernel(count, *refs):
    grads = refs[: 3 * count]
    (tokens_ref, hid_grad_ref, gain_ref, wq_ref, wk_ref, wv_ref, tok_grad_ref, sums_ref) = refs[3 * count :]
    step = pl.program_id(0)
    width = tokens_ref.shape[1]
    norm_grad = None
    for index, weights in enumerate((wq_ref, wk_ref, wv_ref)):
        parts = [grads[3 * part + index][...] for part in range(count)]
        term = mm_nt(jnp.concatenate(parts, axis=1), weights[...])
        norm_grad = term if norm_grad is None else norm_grad + term
    unit, spread = normalise(tokens_ref[...].astype(F32))
    tok_grad = hid_grad_ref[...] + normalise_back(norm_grad, unit, spread, gain_ref[...])
    tok_grad_ref[...] = tok_grad.astype(BF16)
    sums = jnp.concatenate(
        [
            jnp.sum(norm_grad * unit, axis=0, keepdims=True),
            jnp.sum(norm_grad, axis=0, keepdims=True),
            jnp.zeros((6, width), F32),
        ],
        axis=0,
    )

    @pl.when(step == 0)
    def _():
        sums_ref[...] = sums

    @pl.when(step > 0)
    def _():
        sums_ref[...] += sums


def close(grads, tokens, hid_grad, gain, w_query, w_key, w_value, tile=256):
    rows, width = tokens.shape
    whole = lambda t: (0, 0)
    row_spec = pl.BlockSpec((tile, width), lambda t: (t, 0))
    square = pl.BlockSpec((width, width), whole)
    flat = [item for triple in grads for item in triple]
    return pl.pallas_call(
        functools.partial(close_kernel, len(grads)),
        grid=(rows // tile,),
        in_specs=[pl.BlockSpec((tile, item.shape[1]), lambda t: (t, 0)) for item in flat]
        + [row_spec, row_spec, pl.BlockSpec((1, width), whole), square, square, square],
        out_specs=[row_spec, pl.BlockSpec((8, width), whole)],
        out_shape=[
            jax.ShapeDtypeStruct((rows, width), BF16),
            jax.ShapeDtypeStruct((8, width), F32),
        ],
        compiler_params=params("arbitrary"),
        cost_estimate=cost(COVER, 4096),
        name="close",
    )(*flat, tokens, hid_grad, gain, w_query, w_key, w_value)


def block_out_kernel(back_ref, columns_ref, ids_ref, logits_ref, hidden_ref, out_ref):
    chosen = one_hot_columns(columns_ref[:, 1:2], 0, back_ref.shape[0])
    rows = mm(chosen, back_ref[...])
    gate = gate_row(logits_ref[...], picked_rows(ids_ref[...], logits_ref.shape[0]))
    out_ref[...] = (hidden_ref[...] + column(gate) * rows).astype(BF16)


def block_output(back, columns, ids, logits, hidden, tile=256):
    rows, width = hidden.shape
    experts = logits.shape[0]
    count = back.shape[0]
    row_spec = pl.BlockSpec((tile, width), lambda t: (t, 0))
    return pl.pallas_call(
        block_out_kernel,
        grid=(rows // tile,),
        in_specs=[
            pl.BlockSpec((count, width), lambda t: (0, 0)),
            pl.BlockSpec((tile, 2), lambda t: (t, 0)),
            pl.BlockSpec((1, tile), lambda t: (0, t)),
            pl.BlockSpec((experts, tile), lambda t: (0, t)),
            row_spec,
        ],
        out_specs=row_spec,
        out_shape=jax.ShapeDtypeStruct((rows, width), BF16),
        compiler_params=params("arbitrary"),
        cost_estimate=cost(COVER, 4096),
        name="block_output",
    )(back, columns, ids, logits, hidden)


def unpack_expert_kernel(place_ref, down_rows, in_rows, in_ref, down_ref, bias_in_ref, bias_down_ref):
    width, hidden = in_ref.shape
    share = bias_down_ref.shape[1]
    in_ref[...] = in_rows[...].astype(F32)
    down_ref[...] = down_rows[:hidden, :].astype(F32)
    extra = down_rows[hidden:, :].astype(F32)
    bias_in_ref[...] = extra[0:1, :hidden]
    for place in range(width // share):

        @pl.when(place_ref[0, 0] == place)
        def _():
            bias_down_ref[...] = extra[1:2, place * share : (place + 1) * share]


def unpack_expert(place, down_rows, in_rows, share):
    width, hidden = in_rows.shape
    memory = pl.BlockSpec(memory_space=pltpu.VMEM)
    return pl.pallas_call(
        unpack_expert_kernel,
        in_specs=[pl.BlockSpec(memory_space=pltpu.SMEM), memory, memory],
        out_specs=[memory] * 4,
        out_shape=[
            jax.ShapeDtypeStruct((width, hidden), F32),
            jax.ShapeDtypeStruct((hidden, width), F32),
            jax.ShapeDtypeStruct((1, hidden), F32),
            jax.ShapeDtypeStruct((1, share), F32),
        ],
        compiler_params=params(),
        cost_estimate=cost(COVER, width * hidden),
        name="unpack_expert",
    )(place, down_rows, in_rows)


def unpack_kernel(lead, upper_ref, own_ref, other_ref, *refs):
    outs = refs[len(refs) - (3 + lead) :]
    width = outs[-1].shape[1]

    def write(ref):
        base = 0
        if lead:
            base = outs[0].shape[1]
            outs[0][...] = ref[:, :base].astype(F32)
        for place in range(0, width, PAIR):
            for index in range(3):
                first = base + 3 * place + index * PAIR
                outs[lead + index][:, place : place + PAIR] = ref[:, first : first + PAIR].astype(F32)

    own = pl.program_id(0) == upper_ref[0, 0]

    @pl.when(own)
    def _():
        write(own_ref)

    @pl.when(jnp.logical_not(own))
    def _():
        write(other_ref)


def unpack(upper, own, other, blocks, width, lead, earlier=()):
    total, lanes = own.shape
    rows = total // blocks
    span = (lanes - lead * width) // 3
    offset = 0 if lead else width // span - 1
    source = pl.BlockSpec((rows, lanes), lambda c, x: (x, 0))
    return pl.pallas_call(
        functools.partial(unpack_kernel, lead),
        grid=(2, blocks),
        in_specs=[pl.BlockSpec(memory_space=pltpu.SMEM), source, source]
        + [pl.BlockSpec(memory_space=pl.ANY)] * len(earlier),
        out_specs=[pl.BlockSpec((rows, width), lambda c, x: (c * blocks + x, 0))] * lead
        + [pl.BlockSpec((rows, span), lambda c, x: (c * blocks + x, offset))] * 3,
        out_shape=[jax.ShapeDtypeStruct((2 * total, width), F32)] * (3 + lead),
        input_output_aliases={3 + index: index for index in range(len(earlier))},
        compiler_params=params("arbitrary", "arbitrary"),
        cost_estimate=cost(COVER, 4096),
        name="unpack",
    )(upper, own, other, *earlier)


def swap(blocks, axis):
    return lax.all_to_all(blocks, axis, split_axis=0, concat_axis=0, tiled=True)


def after(value, *others):
    return lax.optimization_barrier((value,) + others)[0]


def trade(value, axis, bit):
    count = lax.axis_size(axis)
    return lax.ppermute(value, axis, [(place, place ^ bit) for place in range(count)])


def bits(axis):
    count, bit = lax.axis_size(axis), 1
    while bit < count:
        yield bit
        bit *= 2


def is_upper(axis, bit):
    return (lax.axis_index(axis) // bit) % 2


def halve(value, axis, bit):
    upper = is_upper(axis, bit)
    halves = value.reshape((2, value.shape[0] // 2) + value.shape[1:])
    mine = lax.dynamic_index_in_dim(halves, upper, 0, keepdims=False)
    other = lax.dynamic_index_in_dim(halves, 1 - upper, 0, keepdims=False)
    return (mine.astype(F32) + trade(other, axis, bit).astype(F32)).astype(value.dtype)


def rejoin(value, axis, bit):
    got = trade(value, axis, bit)
    upper = is_upper(axis, bit) == 1
    low = jnp.concatenate([value, got], axis=0)
    return jnp.where(upper, jnp.concatenate([got, value], axis=0), low)


def spread_out(value, axis):
    count = lax.axis_size(axis)
    copies = jnp.broadcast_to(value[None], (count,) + value.shape)
    return swap(copies, axis)


def core_part(value):
    return halve(value, "narrow", 1)


def outer_part(value):
    for bit in list(bits("narrow"))[1:]:
        value = halve(value, "narrow", bit)
    return value


def narrow_part(value):
    return outer_part(core_part(value))


def wide_part(value):
    width = value.shape[1]
    count = lax.axis_size("wide")
    parts = swap(value.reshape(count, -1, width), "wide")
    return jnp.sum(parts.astype(F32), axis=0).astype(value.dtype)


def wide_whole(value):
    return spread_out(value, "wide").reshape(-1, value.shape[1])


def outer_whole(value):
    for bit in list(bits("narrow"))[1:]:
        value = rejoin(value, "narrow", bit)
    return value


def axis_sum(value, axis):
    for bit in bits(axis):
        value = value + trade(value, axis, bit)
    return value


def per_device(
    tokens,
    grad_out,
    routes,
    group_counts,
    group_weights,
    norm1_gain,
    norm1_bias,
    w_query,
    bias_query,
    w_key,
    w_value,
    bias_value,
    w_out,
    bias_out,
    norm2_gain,
    norm2_bias,
    router,
    w_in,
    bias_in,
    w_down,
    bias_down,
):
    rows, width = tokens.shape
    experts = router.shape[1]
    assert rows == SEQ_LEN and w_in.shape[0] == 1
    hidden_cols = w_in.shape[2]
    wide_count = lax.axis_size("wide")
    narrow_count = lax.axis_size("narrow")
    devices = wide_count * narrow_count
    capacity = 2 * rows // experts
    half = capacity // 2
    total_tokens = rows * devices
    row = lambda vector: vector.reshape(1, -1)

    sequence = lax.axis_index(("wide", "narrow"))
    group_ends = jnp.cumsum(group_counts, dtype=jnp.int32)
    member = ((sequence >= group_ends - group_counts) & (sequence < group_ends)).astype(F32)
    factor = group_weights.astype(F32) * devices / (group_counts.shape[0] * group_counts.astype(F32))
    weight = jnp.sum(member * factor).reshape(1, 1)
    ids = routes.reshape(1, rows)
    router_rows = jnp.transpose(router)

    slots, columns, grad_outgoing = route(routes, grad_out, experts, capacity)
    grad_rows = swap(grad_outgoing, "wide")
    gathered_in = lax.all_gather(w_in[0], "narrow", axis=0)
    gathered_down = lax.all_gather(w_down[0], "narrow", axis=0)

    normed_t, queries, keys, values = project(
        tokens, row(norm1_gain), row(norm1_bias), w_query, row(bias_query), w_key, w_value, row(bias_value)
    )
    context, soft_weights = attend(queries, keys, values)
    hidden, moe_in, logits = settle(
        context, tokens, w_out, row(bias_out), row(norm2_gain), row(norm2_bias), router_rows
    )
    first, second = dispatch(weight, slots, ids, logits, moe_in, capacity)
    gathered_bias = lax.all_gather(after(bias_in, first), "narrow", axis=0)
    x0 = swap(after(first, grad_rows), "wide")
    counted = jnp.sum(grad_rows[:, capacity, :experts].astype(F32), axis=0)
    fraction = axis_sum(counted, "narrow") / total_tokens
    x1 = swap(after(second, x0, fraction), "wide")
    act, up, out, back0, dots = expert(
        x0, grad_rows, gathered_in, gathered_bias, gathered_down, bias_down, 0
    )
    back0 = swap(after(back0, x1), "wide")
    act, up, expert_out, back1 = expert(
        x1, grad_rows, gathered_in, gathered_bias, gathered_down, bias_down, 1, (act, up, out, dots)
    )
    back1 = arrived = swap(after(back1, back0), "wide")
    scale = jnp.sum(x1[:, half : half + 3, :capacity].astype(F32), axis=1)
    scale = jnp.transpose(scale.reshape(wide_count, 2, half), (1, 0, 2)).reshape(2, 1, wide_count * half)
    down_sums, in_sums = weight_grads(after(x0, back0), x1, grad_rows, act, up, scale)
    in_grad = lax.psum_scatter(after(in_sums, arrived), "narrow", scatter_dimension=0)
    back1 = after(back1, in_sums)
    returned = swap(after(expert_out, arrived), "wide")

    extras = jnp.transpose(back1[:, half:, :half], (1, 0, 2))
    dots1 = jnp.pad(extras, ((0, 0), (0, 0), (0, EXTRA))).reshape(EXTRA, experts * (half + EXTRA))
    dots0 = jnp.concatenate([extras[3:], extras[:3]], axis=0).reshape(EXTRA, experts * half)
    pull = (BALANCE * experts * fraction).reshape(experts, 1)
    hid_grad, con_grad, out_grad, sums, router_grad, prob_sums = combine(
        weight,
        back0.reshape(experts * half, width),
        back1.reshape(experts * (half + EXTRA), width),
        dots0,
        dots1,
        columns,
        ids,
        logits,
        pull,
        hidden,
        grad_out,
        context,
        moe_in,
        w_out,
        router_rows,
        row(norm2_gain),
    )
    pairs = width // PAIR
    span = pairs // ATTEND_CALLS
    grads, bias_sums = [], []
    out_core = core_part(out_grad)
    packed = [outer_part(out_core)]
    for call in range(ATTEND_CALLS):
        dq, dk, dv, weights, column_sums = attend_back(
            queries,
            keys,
            values,
            soft_weights,
            after(con_grad, out_core) if call else con_grad,
            normed_t,
            call * span,
            span,
        )
        grads.append((dq, dk, dv))
        packed.append(narrow_part(weights))
        bias_sums.append(column_sums)
    early = jnp.concatenate(packed[:-1], axis=1)
    hid_grad = after(hid_grad, early)
    down_grad = lax.psum_scatter(after(down_sums, early, in_grad), "narrow", scatter_dimension=0)
    place = lax.axis_index("narrow").reshape(1, 1)
    grad_w_in, grad_w_down, grad_bias_in, grad_bias_down = unpack_expert(
        place, down_grad, in_grad, width // narrow_count
    )
    grad_tokens, norm_sums = close(grads, tokens, hid_grad, row(norm1_gain), w_query, w_key, w_value)
    block_out = block_output(
        returned.reshape(experts * capacity, width), columns, ids, logits, hidden
    )
    bias_sums = jnp.concatenate(bias_sums, axis=1)
    prob_row = jnp.pad(prob_sums.reshape(1, experts), ((0, 0), (0, width - experts)))
    small = jnp.concatenate([norm_sums[:2], bias_sums[:2], sums[:3], prob_row, router_grad], axis=0)
    small = axis_sum(small, "narrow")
    early = wide_part(after(early, returned))
    late = wide_part(after(packed[-1], early, small))
    small = axis_sum(small, "wide")
    early = wide_whole(after(early, late, small))
    late = wide_whole(after(late, early, grad_w_in, block_out))
    upper = is_upper("narrow", 1).astype(jnp.int32).reshape(1, 1)
    blocks = narrow_count // 2
    early = outer_whole(early)
    grad_w_out, *weights = unpack(upper, early, trade(early, "narrow", 1), blocks, width, 1)
    late = outer_whole(late)
    weights = unpack(upper, late, trade(late, "narrow", 1), blocks, width, 0, weights)
    balance_loss = experts * jnp.sum(fraction * (small[7, :experts] / total_tokens))
    return (
        block_out,
        balance_loss,
        grad_tokens,
        small[0],
        small[1],
        weights[0],
        small[2],
        weights[1],
        weights[2],
        small[3],
        grad_w_out,
        small[6],
        small[4],
        small[5],
        jnp.transpose(small[8:]),
        grad_w_in[None],
        grad_bias_in,
        grad_w_down[None],
        grad_bias_down,
    )


def solution(mesh):
    return jax.shard_map(
        per_device,
        mesh=mesh,
        in_specs=(
            P(("wide", "narrow"), None),
            P(("wide", "narrow"), None),
            P(("wide", "narrow"), None),
            P(),
            P(),
            P(),
            P(),
            P(),
            P(),
            P(),
            P(),
            P(),
            P(),
            P(),
            P(),
            P(),
            P(),
            P("wide", None, "narrow"),
            P("wide", "narrow"),
            P("wide", "narrow", None),
            P("wide", None),
        ),
        out_specs=(
            P(("wide", "narrow"), None),
            P(),
            P(("wide", "narrow"), None),
            P(),
            P(),
            P(),
            P(),
            P(),
            P(),
            P(),
            P(),
            P(),
            P(),
            P(),
            P(),
            P("wide", None, "narrow"),
            P("wide", "narrow"),
            P("wide", "narrow", None),
            P("wide", "narrow"),
        ),
        check_vma=False,
    )
```

```python
import functools
import jax
import jax.numpy as jnp
from jax import lax
from jax.experimental import pallas as pl
from jax.experimental.pallas import tpu as pltpu
from jax.sharding import PartitionSpec as P

HEADS = 12
HEAD_DIM = 64
SEQ_LEN = 1024
EPS = 1e-05
BALANCE = 48.0
NEGATIVE = -1e30
PAIR = 2 * HEAD_DIM
F32 = jnp.float32
BF16 = jnp.bfloat16
VMEM_LIMIT = 56 * 1024 * 1024
EXTRA = 8
COVER = 4e10
ATTEND_CALLS = 2


def mm(left, right):
    return lax.dot_general(left, right, (((1,), (0,)), ((), ())), preferred_element_type=F32)


def mm_nt(left, right):
    return lax.dot_general(left, right, (((1,), (1,)), ((), ())), preferred_element_type=F32)


def mm_tn(left, right):
    return lax.dot_general(left, right, (((0,), (0,)), ((), ())), preferred_element_type=F32)


def cost(flops, nbytes, trans=0):
    return pl.CostEstimate(flops=int(flops), bytes_accessed=int(nbytes), transcendentals=int(trans))


def params(*semantics):
    return pltpu.CompilerParams(dimension_semantics=semantics, vmem_limit_bytes=VMEM_LIMIT)


def head_mask(block, head):
    lanes = lax.broadcasted_iota(jnp.int32, block.shape, 1)
    return jnp.where(lanes // HEAD_DIM == head, block, jnp.zeros_like(block))


def causal(scores, block):
    keys = scores.shape[0]
    first = lax.broadcasted_iota(jnp.int32, (block, block), 0)
    second = lax.broadcasted_iota(jnp.int32, (block, block), 1)
    last = jnp.where(first <= second, scores[keys - block :], NEGATIVE)
    if keys == block:
        return last
    return jnp.concatenate([scores[: keys - block], last], axis=0)


def attend_kernel(block, q_ref, k_ref, v_ref, context_ref, weights_ref):
    rows = q_ref.shape[0]
    keys = k_ref[...]
    values = v_ref[...]
    place = 0
    for first in range(0, rows, block):
        span = first + block
        query = q_ref[first:span, :]
        weights_both, values_both = [], []
        for head in range(2):
            scores = causal(mm_nt(keys[:span], head_mask(query, head)), block)
            peak = jnp.max(scores, axis=0, keepdims=True)
            powers = jnp.exp(scores - peak)
            total = jnp.sum(powers, axis=0, keepdims=True)
            weights = (powers * (1.0 / total)).astype(BF16)
            weights_ref[0, head, place : place + span, :] = weights
            weights_both.append(weights)
            values_both.append(head_mask(values[:span], head))
        out = mm_tn(jnp.concatenate(weights_both, axis=0), jnp.concatenate(values_both, axis=0))
        context_ref[first:span, :] = out.astype(BF16)
        place += span


def attend(queries, keys, values, block=256):
    rows, width = queries.shape
    pairs = width // PAIR
    kept = sum(range(block, rows + 1, block))
    spec = pl.BlockSpec((rows, PAIR), lambda p: (0, p))
    return pl.pallas_call(
        functools.partial(attend_kernel, block),
        grid=(pairs,),
        in_specs=[spec, spec, spec],
        out_specs=[spec, pl.BlockSpec((1, 2, kept, block), lambda p: (p, 0, 0, 0))],
        out_shape=[
            jax.ShapeDtypeStruct((rows, width), BF16),
            jax.ShapeDtypeStruct((pairs, 2, kept, block), BF16),
        ],
        compiler_params=params("arbitrary"),
        cost_estimate=cost(4 * rows * rows * width * 2, rows * width * 8, pairs * 2 * rows * rows),
        name="attend",
    )(queries, keys, values)


def attend_back_kernel(block, shares, place_ref, q_ref, k_ref, v_ref, weights_ref, g_ref, normed_ref,
                       dq_ref, dk_ref, dv_ref, sums_ref, *refs):
    share_refs, (packed_ref, dq_acc, dk_acc, dv_acc) = refs[:shares], refs[shares:]
    rows = q_ref.shape[0]
    keys = k_ref[...]
    values = v_ref[...]
    place = weights_ref.shape[2]
    for first in reversed(range(0, rows, block)):
        span = first + block
        place -= span
        query = q_ref[first:span, :]
        grad = g_ref[first:span, :]
        probs_both, scores_both, query_both, grad_both = [], [], [], []
        for head in range(2):
            query_h = head_mask(query, head)
            grad_h = head_mask(grad, head)
            weights = weights_ref[0, head, place : place + span, :]
            probs = weights.astype(F32)
            grad_probs = mm_nt(values[:span], grad_h)
            inner = jnp.sum(probs * grad_probs, axis=0, keepdims=True)
            grad_scores = (probs * (grad_probs - inner)).astype(BF16)
            probs_both.append(weights)
            scores_both.append(grad_scores)
            query_both.append(query_h)
            grad_both.append(grad_h)
        dv = mm(jnp.concatenate(probs_both, axis=1), jnp.concatenate(grad_both, axis=0))
        dk = mm(jnp.concatenate(scores_both, axis=1), jnp.concatenate(query_both, axis=0))
        if span == rows:
            dv_acc[...] = dv
            dk_acc[...] = dk
        else:
            dv_acc[:span, :] += dv
            dk_acc[:span, :] += dk
        keys_both = jnp.concatenate([head_mask(keys[:span], head) for head in range(2)], axis=0)
        dq = mm_tn(jnp.concatenate(scores_both, axis=0), keys_both) * 0.125
        dq_acc[first:span, :] = dq.astype(BF16)
    dq = dq_acc[...]
    dk = dk_acc[...].astype(BF16)
    dv = dv_acc[...].astype(BF16)
    dq_ref[...] = dq
    dk_ref[...] = dk
    dv_ref[...] = dv
    normed = normed_ref[...]
    packed_ref[:, : 2 * PAIR] = mm(normed, jnp.concatenate([dq, dk], axis=1)).astype(BF16)
    packed_ref[:, 2 * PAIR :] = mm(normed, dv).astype(BF16)
    deal(packed_ref, share_refs, place_ref[0, 0])
    sums_ref[...] = jnp.concatenate(
        [
            jnp.sum(dq.astype(F32), axis=0, keepdims=True),
            jnp.sum(dv.astype(F32), axis=0, keepdims=True),
            jnp.zeros((6, PAIR), F32),
        ],
        axis=0,
    )


def attend_back(queries, keys, values, weights, grad_context, normed_t, place, shares, start, pairs, block=256):
    rows, width = queries.shape
    spec = pl.BlockSpec((rows, PAIR), lambda p: (0, p + start))
    out_spec = pl.BlockSpec((rows, PAIR), lambda p: (0, p))
    return pl.pallas_call(
        functools.partial(attend_back_kernel, block, shares),
        grid=(pairs,),
        in_specs=[
            pl.BlockSpec(memory_space=pltpu.SMEM),
            spec,
            spec,
            spec,
            pl.BlockSpec((1, 2) + weights.shape[2:], lambda p: (p + start, 0, 0, 0)),
            spec,
            pl.BlockSpec((width, rows), lambda p: (0, 0)),
        ],
        out_specs=[
            out_spec,
            out_spec,
            out_spec,
            pl.BlockSpec((8, PAIR), lambda p: (0, p)),
        ]
        + [pl.BlockSpec((width // shares, 3 * PAIR), lambda p: (0, p))] * shares,
        out_shape=[jax.ShapeDtypeStruct((rows, pairs * PAIR), BF16)] * 3
        + [jax.ShapeDtypeStruct((8, pairs * PAIR), F32)]
        + [jax.ShapeDtypeStruct((width // shares, 3 * pairs * PAIR), BF16)] * shares,
        scratch_shapes=[
            pltpu.VMEM((width, 3 * PAIR), BF16),
            pltpu.VMEM((rows, PAIR), BF16),
            pltpu.VMEM((rows, PAIR), F32),
            pltpu.VMEM((rows, PAIR), F32),
        ],
        compiler_params=params("arbitrary"),
        cost_estimate=cost(rows, rows),
        name="attend_back",
    )(place, queries, keys, values, weights, grad_context, normed_t)


def normalise(values):
    centred = values - jnp.mean(values, axis=-1, keepdims=True)
    spread = lax.rsqrt(jnp.mean(centred * centred, axis=-1, keepdims=True) + EPS)
    return centred * spread, spread


def normalise_back(grad, unit, spread, gain):
    scaled = grad * gain
    mean = jnp.mean(scaled, axis=-1, keepdims=True)
    tilt = jnp.mean(scaled * unit, axis=-1, keepdims=True)
    return spread * (scaled - mean - unit * tilt)


def pieces(values):
    high = values.astype(BF16)
    rest = values - high.astype(F32)
    middle = rest.astype(BF16)
    low = (rest - middle.astype(F32)).astype(BF16)
    fill = jnp.zeros((5, values.shape[1]), F32)
    stacked = jnp.concatenate(
        [high.astype(F32), middle.astype(F32), low.astype(F32), fill], axis=0
    )
    return stacked.astype(BF16)


def join(parts):
    return parts[0:1] + parts[1:2] + parts[2:3]


def column(row):
    return jnp.transpose(jnp.broadcast_to(row, (8, row.shape[1])))[:, 0:1]


def gate_row(logits, picked):
    return jax.nn.sigmoid(jnp.sum(jnp.where(picked, logits, 0.0), axis=0, keepdims=True))


def picked_rows(ids, experts):
    return lax.broadcasted_iota(jnp.int32, (experts, ids.shape[1]), 0) == ids


def one_hot_rows(slots, first, count):
    places = lax.broadcasted_iota(jnp.int32, (count, slots.shape[1]), 0) + first
    return (places == slots).astype(F32).astype(BF16)


def one_hot_columns(slots, first, count):
    places = lax.broadcasted_iota(jnp.int32, (slots.shape[0], count), 1) + first
    return (places == slots).astype(F32).astype(BF16)


def route_kernel(experts, capacity, row_ref, grad_ref, slots_ref, columns_ref, out_ref, count_row):
    step = pl.program_id(0)
    rows = row_ref.shape[1]
    width = grad_ref.shape[1]
    half = capacity // 2

    @pl.when(step == 0)
    def _():
        block = 256
        ids = row_ref[...]
        picked = picked_rows(ids, experts).astype(F32)
        first = lax.broadcasted_iota(jnp.int32, (block, block), 0)
        second = lax.broadcasted_iota(jnp.int32, (block, block), 1)
        earlier = (first < second).astype(F32).astype(BF16)
        passed = jnp.zeros((experts, 1), F32)
        places = []
        for start in range(0, rows, block):
            own = picked[:, start : start + block]
            before = mm(own.astype(BF16), earlier) + passed
            places.append(jnp.sum(before * own, axis=0, keepdims=True))
            passed = passed + jnp.sum(own, axis=1, keepdims=True)
        place = jnp.concatenate(places, axis=1).astype(jnp.int32)
        slots = ids * capacity + place
        late = experts * half + ids * (half + EXTRA) + place - half
        mixed = jnp.where(place < half, ids * half + place, late)
        slots_ref[...] = slots
        both = jnp.concatenate([mixed, slots, jnp.zeros((6, rows), jnp.int32)], axis=0)
        columns_ref[...] = jnp.transpose(both.astype(F32))[:, 0:2].astype(jnp.int32)
        count_row[...] = jnp.zeros_like(count_row)
        lanes = lax.broadcasted_iota(jnp.int32, (experts, 128), 1)
        spread = jnp.where(lanes == lax.broadcasted_iota(jnp.int32, (experts, 128), 0), passed, 0.0)
        count_row[0:1, 0:128] = jnp.sum(spread, axis=0, keepdims=True)

    chosen = one_hot_rows(slots_ref[...], step * capacity, capacity)
    out_ref[0, :capacity, :] = mm(chosen, grad_ref[...]).astype(BF16)
    out_ref[0, capacity:, :] = count_row[...].astype(BF16)


def route(routes, grad_out, experts, capacity):
    rows, width = grad_out.shape
    whole = lambda e: (0, 0)
    return pl.pallas_call(
        functools.partial(route_kernel, experts, capacity),
        grid=(experts,),
        in_specs=[
            pl.BlockSpec((1, rows), whole),
            pl.BlockSpec((rows, width), whole),
        ],
        out_specs=[
            pl.BlockSpec((1, rows), whole),
            pl.BlockSpec((rows, 2), whole),
            pl.BlockSpec((1, capacity + EXTRA, width), lambda e: (e, 0, 0)),
        ],
        out_shape=[
            jax.ShapeDtypeStruct((1, rows), jnp.int32),
            jax.ShapeDtypeStruct((rows, 2), jnp.int32),
            jax.ShapeDtypeStruct((experts, capacity + EXTRA, width), BF16),
        ],
        scratch_shapes=[pltpu.VMEM((EXTRA, width), F32)],
        compiler_params=params("arbitrary"),
        cost_estimate=cost(2 * experts * capacity * rows * width, 6 * rows * width),
        name="route",
    )(routes.reshape(1, rows), grad_out)


def project_kernel(tokens_ref, gain_ref, shift_ref, wq_ref, bq_ref, wk_ref, wv_ref, bv_ref,
                   normed_ref, q_ref, k_ref, v_ref):
    unit, _ = normalise(tokens_ref[...].astype(F32))
    normed = (unit * gain_ref[...] + shift_ref[...]).astype(BF16)
    normed_ref[...] = jnp.transpose(normed)
    q_ref[...] = ((mm(normed, wq_ref[...]) + bq_ref[...]) * 0.125).astype(BF16)
    k_ref[...] = mm(normed, wk_ref[...]).astype(BF16)
    v_ref[...] = (mm(normed, wv_ref[...]) + bv_ref[...]).astype(BF16)


def project(tokens, gain, shift, w_query, bias_query, w_key, w_value, bias_value, tile=256):
    rows, width = tokens.shape
    row_spec = pl.BlockSpec((tile, width), lambda t: (t, 0))
    vector = pl.BlockSpec((1, width), lambda t: (0, 0))
    square = pl.BlockSpec((width, width), lambda t: (0, 0))
    return pl.pallas_call(
        project_kernel,
        grid=(rows // tile,),
        in_specs=[row_spec, vector, vector, square, vector, square, square, vector],
        out_specs=[pl.BlockSpec((width, tile), lambda t: (0, t))] + [row_spec] * 3,
        out_shape=[jax.ShapeDtypeStruct((width, rows), BF16)]
        + [jax.ShapeDtypeStruct((rows, width), BF16)] * 3,
        compiler_params=params("arbitrary"),
        cost_estimate=cost(6 * rows * width * width, 10 * rows * width + 6 * width * width),
        name="project",
    )(tokens, gain, shift, w_query, bias_query, w_key, w_value, bias_value)


def settle_kernel(context_ref, tokens_ref, w_out_ref, bias_ref, gain_ref, shift_ref, router_ref,
                  hidden_ref, moe_ref, logits_ref):
    hidden = tokens_ref[...].astype(F32) + mm(context_ref[...], w_out_ref[...]) + bias_ref[...]
    unit, _ = normalise(hidden)
    moe_in = (unit * gain_ref[...] + shift_ref[...]).astype(BF16)
    hidden_ref[...] = hidden
    moe_ref[...] = moe_in
    logits_ref[...] = mm_nt(router_ref[...], moe_in)


def settle(context, tokens, w_out, bias_out, gain, shift, router_rows, tile=256):
    rows, width = tokens.shape
    experts = router_rows.shape[0]
    row_spec = pl.BlockSpec((tile, width), lambda t: (t, 0))
    vector = pl.BlockSpec((1, width), lambda t: (0, 0))
    return pl.pallas_call(
        settle_kernel,
        grid=(rows // tile,),
        in_specs=[
            row_spec,
            row_spec,
            pl.BlockSpec((width, width), lambda t: (0, 0)),
            vector,
            vector,
            vector,
            pl.BlockSpec((experts, width), lambda t: (0, 0)),
        ],
        out_specs=[row_spec, row_spec, pl.BlockSpec((experts, tile), lambda t: (0, t))],
        out_shape=[
            jax.ShapeDtypeStruct((rows, width), F32),
            jax.ShapeDtypeStruct((rows, width), BF16),
            jax.ShapeDtypeStruct((experts, rows), F32),
        ],
        compiler_params=params("arbitrary"),
        cost_estimate=cost(2 * rows * width * width, 10 * rows * width + 2 * width * width),
        name="settle",
    )(context, tokens, w_out, bias_out, gain, shift, router_rows)


def dispatch_kernel(weight_ref, slots_ref, ids_ref, logits_ref, moe_ref, first_ref, second_ref, parts):
    step = pl.program_id(0)
    experts = logits_ref.shape[0]
    half = first_ref.shape[1]

    @pl.when(step == 0)
    def _():
        gate = gate_row(logits_ref[...], picked_rows(ids_ref[...], experts))
        parts[...] = pieces(gate * weight_ref[0, 0])

    chosen = one_hot_rows(slots_ref[...], step * 2 * half, 2 * half)
    rows = mm(chosen, moe_ref[...]).astype(BF16)
    first_ref[0] = rows[:half]
    second_ref[0, :half, :] = rows[half:]
    second_ref[0, half:, :] = jnp.zeros((EXTRA, rows.shape[1]), BF16)
    second_ref[0, half:, 0 : 2 * half] = mm_nt(parts[...], chosen).astype(BF16)


def dispatch(weight, slots, ids, logits, moe_in, capacity):
    rows, width = moe_in.shape
    experts = logits.shape[0]
    half = capacity // 2
    whole = lambda e: (0, 0)
    return pl.pallas_call(
        dispatch_kernel,
        grid=(experts,),
        in_specs=[
            pl.BlockSpec(memory_space=pltpu.SMEM),
            pl.BlockSpec((1, rows), whole),
            pl.BlockSpec((1, rows), whole),
            pl.BlockSpec((experts, rows), whole),
            pl.BlockSpec((rows, width), whole),
        ],
        out_specs=[
            pl.BlockSpec((1, half, width), lambda e: (e, 0, 0)),
            pl.BlockSpec((1, half + EXTRA, width), lambda e: (e, 0, 0)),
        ],
        out_shape=[
            jax.ShapeDtypeStruct((experts, half, width), BF16),
            jax.ShapeDtypeStruct((experts, half + EXTRA, width), BF16),
        ],
        scratch_shapes=[pltpu.VMEM((8, rows), BF16)],
        compiler_params=params("arbitrary"),
        cost_estimate=cost(2 * experts * capacity * rows * width, 6 * rows * width),
        name="dispatch",
    )(weight, slots, ids, logits, moe_in)


def row_sum(values):
    ones = jnp.ones((8, values.shape[1]), BF16)
    high = values.astype(BF16)
    rest = values - high.astype(F32)
    middle = rest.astype(BF16)
    low = (rest - middle.astype(F32)).astype(BF16)
    return (mm_nt(ones, high) + mm_nt(ones, middle) + mm_nt(ones, low))[0:1]


def expert_kernel(steps, chunk, *refs):
    if chunk == 0:
        (x_ref, g_ref, w_in_ref, b_in_ref, w_down_ref, b_down_ref,
         act_ref, up_ref, out_ref, back_ref, dot_ref, back_acc, dot_acc, out_acc) = refs
    else:
        (x_ref, g_ref, w_in_ref, b_in_ref, w_down_ref, b_down_ref, _, _, _, earlier_ref,
         act_ref, up_ref, out_ref, back_ref, back_acc, dot_acc, out_acc) = refs
    part = pl.program_id(0)
    tile = pl.program_id(1)
    group, half, width = x_ref.shape
    rows = group * half
    x = x_ref[...].reshape(rows, width)
    g = g_ref[...].reshape(rows, width)
    w_in = w_in_ref[0]
    pre = mm(x, w_in) + b_in_ref[0].astype(F32)
    grad_act = mm_nt(g, w_down_ref[0])
    below = 0.5 + 0.5 * lax.erf(pre * 0.7071067811865476)
    act = pre * below
    slope = below + pre * (0.3989422804014327 * jnp.exp(-0.5 * pre * pre))
    up = (grad_act * slope).astype(BF16)
    rounded = act.astype(BF16)
    act_ref[0, 0] = rounded
    up_ref[0, 0] = up
    out = mm(rounded, w_down_ref[0])
    product = act * grad_act
    lanes = min(128, product.shape[1])
    folded = product[:, :lanes]
    for lane in range(lanes, product.shape[1], lanes):
        folded = folded + product[:, lane : lane + lanes]
    where = pl.ds(pl.multiple_of(tile * rows, rows), rows)
    back = mm_nt(up, w_in)

    @pl.when(part == 0)
    def _():
        biased = g.astype(F32) * b_down_ref[...].astype(F32)
        total = folded
        for lane in range(0, biased.shape[1], lanes):
            total = total + biased[:, lane : lane + lanes]
        back_acc[where, :] = back
        out_acc[where, :] = out + b_down_ref[...].astype(F32)
        dot_acc[where, :] = total

    @pl.when(part > 0)
    def _():
        back_acc[where, :] += back
        out_acc[where, :] += out
        dot_acc[where, :] += folded

    @pl.when(part == steps - 1)
    def _():
        out_ref[...] = out_acc[where, :].astype(BF16).reshape(group, half, width)
        back_ref[:, :half, :] = back_acc[where, :].astype(BF16).reshape(group, half, width)
        dots = dot_acc[where, :]
        for index in range(group):
            own = pieces(row_sum(dots[index * half : (index + 1) * half, :])).astype(F32)
            if chunk == 0:
                dot_ref[index] = own.astype(BF16)
            else:
                before = earlier_ref[index].astype(F32)
                extra = jnp.concatenate([own[0:3], before[0:3], own[6:8]], axis=0)
                back_ref[index, half:, :] = jnp.zeros((EXTRA, width), BF16)
                back_ref[index, half:, 0:half] = extra.astype(BF16)


def expert(x, g, w_in, b_in, w_down, b_down, chunk, earlier=()):
    sources, width = x.shape[0], x.shape[2]
    half = (g.shape[1] - EXTRA) // 2
    rows = sources * half
    parts, _, hidden = w_in.shape
    group = max(1, 256 // half)
    tile = group * half
    tiles = sources // group
    last = parts - 1
    late = lambda p, t: jnp.where(p == last, t, 0)
    wide_spec = pl.BlockSpec((1, 1, tile, hidden), lambda p, t: (p, chunk, t, 0))
    wide_shape = jax.ShapeDtypeStruct((parts, 2, rows, hidden), BF16)
    dot_shape = jax.ShapeDtypeStruct((sources, 8, half), BF16)
    dot_spec = pl.BlockSpec((group, 8, half), lambda p, t: (late(p, t), 0, 0))
    back_rows = half + EXTRA * chunk
    return pl.pallas_call(
        functools.partial(expert_kernel, parts, chunk),
        grid=(parts, tiles),
        in_specs=[
            pl.BlockSpec((group, half, width), lambda p, t: (t, 0, 0)),
            pl.BlockSpec((group, half, width), lambda p, t: (t, chunk, 0)),
            pl.BlockSpec((1, width, hidden), lambda p, t: (p, 0, 0)),
            pl.BlockSpec((1, 1, hidden), lambda p, t: (p, 0, 0)),
            pl.BlockSpec((1, hidden, width), lambda p, t: (p, 0, 0)),
            pl.BlockSpec((1, width), lambda p, t: (0, 0)),
        ]
        + ([pl.BlockSpec(memory_space=pl.ANY)] * 3 + [dot_spec] if chunk else []),
        out_specs=[
            wide_spec,
            wide_spec,
            pl.BlockSpec((group, half, width), lambda p, t: (late(p, t), chunk, 0)),
            pl.BlockSpec((group, back_rows, width), lambda p, t: (late(p, t), 0, 0)),
        ]
        + ([] if chunk else [dot_spec]),
        out_shape=[
            wide_shape,
            wide_shape,
            jax.ShapeDtypeStruct((sources, 2 * half, width), BF16),
            jax.ShapeDtypeStruct((sources, back_rows, width), BF16),
        ]
        + ([] if chunk else [dot_shape]),
        scratch_shapes=[
            pltpu.VMEM((rows, width), F32),
            pltpu.VMEM((rows, min(128, hidden)), F32),
            pltpu.VMEM((rows, width), F32),
        ],
        input_output_aliases={6: 0, 7: 1, 8: 2} if chunk else {},
        compiler_params=params("arbitrary", "arbitrary"),
        cost_estimate=cost(
            6 * rows * width * hidden * parts, rows * hidden * parts * 4, 2 * rows * hidden * parts
        ),
        name="expert",
    )(x, g, w_in, b_in, w_down, b_down, *earlier)


def weight_kernel(parts, x0_ref, x1_ref, g_ref, act_ref, up_ref, scale_ref,
                  down_ref, in_ref, down_acc, in_acc, bias_acc, bias_down_acc, flipped):
    part = pl.program_id(0)
    chunk = pl.program_id(1)
    sources, half, width = x0_ref.shape
    rows = sources * half
    hidden = act_ref.shape[3]
    scale = scale_ref[0]
    split = pieces(scale)
    g = g_ref[...].reshape(rows, width)

    def flip(values):
        return (jnp.transpose(values).astype(F32) * scale).astype(BF16)

    @pl.when((part == 0) & (chunk == 0))
    def _():
        flipped[0] = flip(x0_ref[...].reshape(rows, width))

    @pl.when((part == 0) & (chunk == 1))
    def _():
        flipped[1] = flip(x1_ref[...].reshape(rows, width))

    act = act_ref[0, 0]
    up = up_ref[0, 0]
    down = mm(flip(act), g)
    into = mm(flipped[chunk], up)
    bias_in = join(mm(split, up))

    @pl.when(chunk == 0)
    def _():
        down_acc[...] = down
        in_acc[...] = into
        bias_acc[...] = bias_in

    @pl.when(chunk == 1)
    def _():
        down_ref[0, :hidden, :] = (down_acc[...] + down).astype(BF16)
        in_ref[0] = (in_acc[...] + into).astype(BF16)

    @pl.when(part == 0)
    def _():
        bias_down = join(mm(split, g))
        bias_down_acc[...] = jnp.where(chunk == 0, bias_down, bias_down_acc[...] + bias_down)

    @pl.when(chunk == 1)
    def _():
        down_ref[0, hidden:, :] = jnp.zeros((EXTRA, width), BF16)
        down_ref[0, hidden : hidden + 1, 0:hidden] = (bias_acc[...] + bias_in).astype(BF16)
        down_ref[0, hidden + 1 : hidden + 2, :] = bias_down_acc[...].astype(BF16)


def weight_grads(x0, x1, g, act, up, scale):
    sources, half, width = x0.shape
    parts, _, rows, hidden = act.shape
    wide_spec = pl.BlockSpec((1, 1, rows, hidden), lambda p, t: (p, t, 0, 0))
    return pl.pallas_call(
        functools.partial(weight_kernel, parts),
        grid=(parts, 2),
        in_specs=[
            pl.BlockSpec((sources, half, width), lambda p, t: (0, 0, 0)),
            pl.BlockSpec((sources, half, width), lambda p, t: (0, 0, 0)),
            pl.BlockSpec((sources, half, width), lambda p, t: (0, t, 0)),
            wide_spec,
            wide_spec,
            pl.BlockSpec((1, 1, rows), lambda p, t: (t, 0, 0)),
        ],
        out_specs=[
            pl.BlockSpec((1, hidden + EXTRA, width), lambda p, t: (p, 0, 0)),
            pl.BlockSpec((1, width, hidden), lambda p, t: (p, 0, 0)),
        ],
        out_shape=[
            jax.ShapeDtypeStruct((parts, hidden + EXTRA, width), BF16),
            jax.ShapeDtypeStruct((parts, width, hidden), BF16),
        ],
        scratch_shapes=[
            pltpu.VMEM((hidden, width), F32),
            pltpu.VMEM((width, hidden), F32),
            pltpu.VMEM((1, hidden), F32),
            pltpu.VMEM((1, width), F32),
            pltpu.VMEM((2, width, rows), BF16),
        ],
        compiler_params=params("arbitrary", "arbitrary"),
        cost_estimate=cost(12 * rows * width * hidden * parts, rows * hidden * parts * 8),
        name="weight_grads",
    )(x0, x1, g, act, up, scale)


def deal(rows_ref, share_refs, place):
    count = share_refs[0].shape[0]
    for index, share_ref in enumerate(share_refs):
        first = jnp.bitwise_xor(place, index) * count
        share_ref[...] = rows_ref[pl.ds(pl.multiple_of(first, count), count), :]


def combine_kernel(shares, weight_ref, place_ref, back0_ref, back1_ref, dots0_ref, dots1_ref, columns_ref, ids_ref, logits_ref, pull_ref,
                   hidden_ref, grad_ref, context_ref, moe_ref, w_out_ref, router_ref, gain_ref,
                   hid_grad_ref, con_grad_ref, sums_ref, router_grad_ref, probs_ref, *refs):
    out_refs, (branches, out_rows) = refs[:shares], refs[shares:]
    step = pl.program_id(0)
    experts = logits_ref.shape[0]
    count0 = back0_ref.shape[0]
    count1 = back1_ref.shape[0]
    weight = weight_ref[0, 0]
    columns = columns_ref[:, 0:1]
    chosen0 = one_hot_columns(columns, 0, count0)
    chosen1 = one_hot_columns(columns, count0, count1)
    rows = mm(chosen0, back0_ref[...]) + mm(chosen1, back1_ref[...])
    dots = join(mm_nt(dots0_ref[...], chosen0)) + join(mm_nt(dots1_ref[...], chosen1))
    logits = logits_ref[...]
    picked = picked_rows(ids_ref[...], experts)
    gate = gate_row(logits, picked)
    powers = jnp.exp(logits - jnp.max(logits, axis=0, keepdims=True))
    probs = powers / jnp.sum(powers, axis=0, keepdims=True)
    pull = pull_ref[...]
    slope = dots * weight * gate * (1.0 - gate)
    logit_grad = probs * (pull - jnp.sum(probs * pull, axis=0, keepdims=True))
    logit_grad = (logit_grad + jnp.where(picked, slope, 0.0)).astype(BF16)
    moe_grad = mm_tn(logit_grad, router_ref[...]) + rows * column(gate * weight)
    unit, spread = normalise(hidden_ref[...])
    hid_grad = weight * grad_ref[...].astype(F32) + normalise_back(
        moe_grad, unit, spread, gain_ref[...]
    )
    branch = hid_grad.astype(BF16)
    hid_grad_ref[...] = hid_grad
    con_grad_ref[...] = mm_nt(branch, w_out_ref[...]).astype(BF16)
    branches[pl.ds(pl.multiple_of(step * branch.shape[0], branch.shape[0]), branch.shape[0]), :] = branch
    router_grad = mm(logit_grad, moe_ref[...])
    prob_sum = jnp.sum(probs, axis=1, keepdims=True)
    sums = jnp.concatenate(
        [
            jnp.sum(moe_grad * unit, axis=0, keepdims=True),
            jnp.sum(moe_grad, axis=0, keepdims=True),
            jnp.sum(branch.astype(F32), axis=0, keepdims=True),
            jnp.zeros((5, unit.shape[1]), F32),
        ],
        axis=0,
    )

    @pl.when(step == 0)
    def _():
        router_grad_ref[...] = router_grad
        probs_ref[...] = prob_sum
        sums_ref[...] = sums

    @pl.when(step > 0)
    def _():
        router_grad_ref[...] += router_grad
        probs_ref[...] += prob_sum
        sums_ref[...] += sums

    @pl.when(step == pl.num_programs(0) - 1)
    def _():
        out_rows[...] = mm_tn(context_ref[...], branches[...]).astype(BF16)
        deal(out_rows, out_refs, place_ref[0, 0])


def combine(weight, place, shares, back0, back1, dots0, dots1, columns, ids, logits, pull, hidden, grad_out, context, moe_in,
            w_out, router_rows, gain, tile=256):
    rows, width = hidden.shape
    experts = logits.shape[0]
    count = back0.shape[0]
    count1 = back1.shape[0]
    whole = lambda t: (0, 0)
    row_spec = pl.BlockSpec((tile, width), lambda t: (t, 0))
    square = pl.BlockSpec((width, width), whole)
    return pl.pallas_call(
        functools.partial(combine_kernel, shares),
        grid=(rows // tile,),
        in_specs=[
            pl.BlockSpec(memory_space=pltpu.SMEM),
            pl.BlockSpec(memory_space=pltpu.SMEM),
            pl.BlockSpec((count, width), whole),
            pl.BlockSpec((count1, width), whole),
            pl.BlockSpec((8, count), whole),
            pl.BlockSpec((8, count1), whole),
            pl.BlockSpec((tile, 2), lambda t: (t, 0)),
            pl.BlockSpec((1, tile), lambda t: (0, t)),
            pl.BlockSpec((experts, tile), lambda t: (0, t)),
            pl.BlockSpec((experts, 1), whole),
            row_spec,
            row_spec,
            pl.BlockSpec((rows, width), whole),
            row_spec,
            square,
            pl.BlockSpec((experts, width), whole),
            pl.BlockSpec((1, width), whole),
        ],
        out_specs=[
            row_spec,
            row_spec,
            pl.BlockSpec((8, width), whole),
            pl.BlockSpec((experts, width), whole),
            pl.BlockSpec((experts, 1), whole),
        ]
        + [pl.BlockSpec((width // shares, width), whole)] * shares,
        out_shape=[
            jax.ShapeDtypeStruct((rows, width), F32),
            jax.ShapeDtypeStruct((rows, width), BF16),
            jax.ShapeDtypeStruct((8, width), F32),
            jax.ShapeDtypeStruct((experts, width), F32),
            jax.ShapeDtypeStruct((experts, 1), F32),
        ]
        + [jax.ShapeDtypeStruct((width // shares, width), BF16)] * shares,
        scratch_shapes=[pltpu.VMEM((rows, width), BF16), pltpu.VMEM((width, width), BF16)],
        compiler_params=params("arbitrary"),
        cost_estimate=cost(rows, rows),
        name="combine",
    )(weight, place, back0, back1, dots0, dots1, columns, ids, logits, pull, hidden, grad_out, context, moe_in, w_out,
      router_rows, gain)


def close_kernel(count, *refs):
    grads = refs[: 3 * count]
    (tokens_ref, hid_grad_ref, gain_ref, wq_ref, wk_ref, wv_ref, tok_grad_ref, sums_ref) = refs[3 * count :]
    step = pl.program_id(0)
    width = tokens_ref.shape[1]
    norm_grad = None
    for index, weights in enumerate((wq_ref, wk_ref, wv_ref)):
        parts = [grads[3 * part + index][...] for part in range(count)]
        term = mm_nt(jnp.concatenate(parts, axis=1), weights[...])
        norm_grad = term if norm_grad is None else norm_grad + term
    unit, spread = normalise(tokens_ref[...].astype(F32))
    tok_grad = hid_grad_ref[...] + normalise_back(norm_grad, unit, spread, gain_ref[...])
    tok_grad_ref[...] = tok_grad.astype(BF16)
    sums = jnp.concatenate(
        [
            jnp.sum(norm_grad * unit, axis=0, keepdims=True),
            jnp.sum(norm_grad, axis=0, keepdims=True),
            jnp.zeros((6, width), F32),
        ],
        axis=0,
    )

    @pl.when(step == 0)
    def _():
        sums_ref[...] = sums

    @pl.when(step > 0)
    def _():
        sums_ref[...] += sums


def close(grads, tokens, hid_grad, gain, w_query, w_key, w_value, tile=256):
    rows, width = tokens.shape
    whole = lambda t: (0, 0)
    row_spec = pl.BlockSpec((tile, width), lambda t: (t, 0))
    square = pl.BlockSpec((width, width), whole)
    flat = [item for triple in grads for item in triple]
    return pl.pallas_call(
        functools.partial(close_kernel, len(grads)),
        grid=(rows // tile,),
        in_specs=[pl.BlockSpec((tile, item.shape[1]), lambda t: (t, 0)) for item in flat]
        + [row_spec, row_spec, pl.BlockSpec((1, width), whole), square, square, square],
        out_specs=[row_spec, pl.BlockSpec((8, width), whole)],
        out_shape=[
            jax.ShapeDtypeStruct((rows, width), BF16),
            jax.ShapeDtypeStruct((8, width), F32),
        ],
        compiler_params=params("arbitrary"),
        cost_estimate=cost(COVER, 4096),
        name="close",
    )(*flat, tokens, hid_grad, gain, w_query, w_key, w_value)


def block_out_kernel(back_ref, columns_ref, ids_ref, logits_ref, hidden_ref, out_ref):
    chosen = one_hot_columns(columns_ref[:, 1:2], 0, back_ref.shape[0])
    rows = mm(chosen, back_ref[...])
    gate = gate_row(logits_ref[...], picked_rows(ids_ref[...], logits_ref.shape[0]))
    out_ref[...] = (hidden_ref[...] + column(gate) * rows).astype(BF16)


def block_output(back, columns, ids, logits, hidden, tile=256):
    rows, width = hidden.shape
    experts = logits.shape[0]
    count = back.shape[0]
    row_spec = pl.BlockSpec((tile, width), lambda t: (t, 0))
    return pl.pallas_call(
        block_out_kernel,
        grid=(rows // tile,),
        in_specs=[
            pl.BlockSpec((count, width), lambda t: (0, 0)),
            pl.BlockSpec((tile, 2), lambda t: (t, 0)),
            pl.BlockSpec((1, tile), lambda t: (0, t)),
            pl.BlockSpec((experts, tile), lambda t: (0, t)),
            row_spec,
        ],
        out_specs=row_spec,
        out_shape=jax.ShapeDtypeStruct((rows, width), BF16),
        compiler_params=params("arbitrary"),
        cost_estimate=cost(COVER, 4096),
        name="block_output",
    )(back, columns, ids, logits, hidden)


def unpack_expert_kernel(place_ref, down_rows, in_rows, in_ref, down_ref, bias_in_ref, bias_down_ref):
    width, hidden = in_ref.shape
    share = bias_down_ref.shape[1]
    in_ref[...] = in_rows[...].astype(F32)
    down_ref[...] = down_rows[:hidden, :].astype(F32)
    extra = down_rows[hidden:, :].astype(F32)
    bias_in_ref[...] = extra[0:1, :hidden]
    for place in range(width // share):

        @pl.when(place_ref[0, 0] == place)
        def _():
            bias_down_ref[...] = extra[1:2, place * share : (place + 1) * share]


def unpack_expert(place, down_rows, in_rows, share):
    width, hidden = in_rows.shape
    memory = pl.BlockSpec(memory_space=pltpu.VMEM)
    return pl.pallas_call(
        unpack_expert_kernel,
        in_specs=[pl.BlockSpec(memory_space=pltpu.SMEM), memory, memory],
        out_specs=[memory] * 4,
        out_shape=[
            jax.ShapeDtypeStruct((width, hidden), F32),
            jax.ShapeDtypeStruct((hidden, width), F32),
            jax.ShapeDtypeStruct((1, hidden), F32),
            jax.ShapeDtypeStruct((1, share), F32),
        ],
        compiler_params=params(),
        cost_estimate=cost(COVER, width * hidden),
        name="unpack_expert",
    )(place, down_rows, in_rows)


def unpack_kernel(lead, upper_ref, own_ref, other_ref, *refs):
    outs = refs[len(refs) - (3 + lead) :]
    width = outs[-1].shape[1]

    def write(ref):
        base = 0
        if lead:
            base = outs[0].shape[1]
            outs[0][...] = ref[:, :base].astype(F32)
        for place in range(0, width, PAIR):
            for index in range(3):
                first = base + 3 * place + index * PAIR
                outs[lead + index][:, place : place + PAIR] = ref[:, first : first + PAIR].astype(F32)

    own = pl.program_id(0) == upper_ref[0, 0]

    @pl.when(own)
    def _():
        write(own_ref)

    @pl.when(jnp.logical_not(own))
    def _():
        write(other_ref)


def unpack(upper, own, other, blocks, width, lead, earlier=()):
    total, lanes = own.shape
    rows = total // blocks
    span = (lanes - lead * width) // 3
    offset = 0 if lead else width // span - 1
    source = pl.BlockSpec((rows, lanes), lambda c, x: (x, 0))
    return pl.pallas_call(
        functools.partial(unpack_kernel, lead),
        grid=(2, blocks),
        in_specs=[pl.BlockSpec(memory_space=pltpu.SMEM), source, source]
        + [pl.BlockSpec(memory_space=pl.ANY)] * len(earlier),
        out_specs=[pl.BlockSpec((rows, width), lambda c, x: (2 * x + c, 0))] * lead
        + [pl.BlockSpec((rows, span), lambda c, x: (2 * x + c, offset))] * 3,
        out_shape=[jax.ShapeDtypeStruct((2 * total, width), F32)] * (3 + lead),
        input_output_aliases={3 + index: index for index in range(len(earlier))},
        compiler_params=params("arbitrary", "arbitrary"),
        cost_estimate=cost(COVER, 4096),
        name="unpack",
    )(upper, own, other, *earlier)


def swap(blocks, axis):
    return lax.all_to_all(blocks, axis, split_axis=0, concat_axis=0, tiled=True)


def after(value, *others):
    return lax.optimization_barrier((value,) + others)[0]


def trade(value, axis, bit):
    count = lax.axis_size(axis)
    return lax.ppermute(value, axis, [(place, place ^ bit) for place in range(count)])


def bits(axis):
    count, bit = lax.axis_size(axis), 1
    while bit < count:
        yield bit
        bit *= 2


def is_upper(axis, bit):
    return (lax.axis_index(axis) // bit) % 2


def rejoin(value, axis, bit):
    got = trade(value, axis, bit)
    upper = is_upper(axis, bit) == 1
    low = jnp.concatenate([value, got], axis=0)
    return jnp.where(upper, jnp.concatenate([got, value], axis=0), low)


def spread_out(value, axis):
    count = lax.axis_size(axis)
    copies = jnp.broadcast_to(value[None], (count,) + value.shape)
    return swap(copies, axis)


def narrow_part(shares):
    total = shares[0].astype(F32)
    for index, share in enumerate(shares[1:], 1):
        total = total + trade(share, "narrow", index).astype(F32)
    return total.astype(BF16)


def wide_part(value):
    width = value.shape[1]
    count = lax.axis_size("wide")
    parts = swap(value.reshape(count, -1, width), "wide")
    return jnp.sum(parts.astype(F32), axis=0).astype(value.dtype)


def wide_whole(value):
    return spread_out(value, "wide").reshape(-1, value.shape[1])


def outer_whole(value):
    for bit in list(bits("narrow"))[1:]:
        value = rejoin(value, "narrow", bit)
    return value


def axis_sum(value, axis):
    for bit in bits(axis):
        value = value + trade(value, axis, bit)
    return value


def per_device(
    tokens,
    grad_out,
    routes,
    group_counts,
    group_weights,
    norm1_gain,
    norm1_bias,
    w_query,
    bias_query,
    w_key,
    w_value,
    bias_value,
    w_out,
    bias_out,
    norm2_gain,
    norm2_bias,
    router,
    w_in,
    bias_in,
    w_down,
    bias_down,
):
    rows, width = tokens.shape
    experts = router.shape[1]
    assert rows == SEQ_LEN and w_in.shape[0] == 1
    hidden_cols = w_in.shape[2]
    wide_count = lax.axis_size("wide")
    narrow_count = lax.axis_size("narrow")
    devices = wide_count * narrow_count
    capacity = 2 * rows // experts
    half = capacity // 2
    total_tokens = rows * devices
    row = lambda vector: vector.reshape(1, -1)

    sequence = lax.axis_index(("wide", "narrow"))
    group_ends = jnp.cumsum(group_counts, dtype=jnp.int32)
    member = ((sequence >= group_ends - group_counts) & (sequence < group_ends)).astype(F32)
    factor = group_weights.astype(F32) * devices / (group_counts.shape[0] * group_counts.astype(F32))
    weight = jnp.sum(member * factor).reshape(1, 1)
    ids = routes.reshape(1, rows)
    router_rows = jnp.transpose(router)
    place = lax.axis_index("narrow").reshape(1, 1)

    slots, columns, grad_outgoing = route(routes, grad_out, experts, capacity)
    grad_rows = swap(grad_outgoing, "wide")
    gathered_in = lax.all_gather(w_in[0], "narrow", axis=0)
    gathered_down = lax.all_gather(w_down[0], "narrow", axis=0)

    normed_t, queries, keys, values = project(
        tokens, row(norm1_gain), row(norm1_bias), w_query, row(bias_query), w_key, w_value, row(bias_value)
    )
    context, soft_weights = attend(queries, keys, values)
    hidden, moe_in, logits = settle(
        context, tokens, w_out, row(bias_out), row(norm2_gain), row(norm2_bias), router_rows
    )
    first, second = dispatch(weight, slots, ids, logits, moe_in, capacity)
    gathered_bias = lax.all_gather(after(bias_in, first), "narrow", axis=0)
    x0 = swap(after(first, grad_rows), "wide")
    counted = jnp.sum(grad_rows[:, capacity, :experts].astype(F32), axis=0)
    fraction = axis_sum(counted, "narrow") / total_tokens
    x1 = swap(after(second, x0, fraction), "wide")
    act, up, out, back0, dots = expert(
        x0, grad_rows, gathered_in, gathered_bias, gathered_down, bias_down, 0
    )
    back0 = swap(after(back0, x1), "wide")
    act, up, expert_out, back1 = expert(
        x1, grad_rows, gathered_in, gathered_bias, gathered_down, bias_down, 1, (act, up, out, dots)
    )
    back1 = arrived = swap(after(back1, back0), "wide")
    scale = jnp.sum(x1[:, half : half + 3, :capacity].astype(F32), axis=1)
    scale = jnp.transpose(scale.reshape(wide_count, 2, half), (1, 0, 2)).reshape(2, 1, wide_count * half)
    down_sums, in_sums = weight_grads(after(x0, back0), x1, grad_rows, act, up, scale)
    in_grad = lax.psum_scatter(after(in_sums, arrived), "narrow", scatter_dimension=0)
    back1 = after(back1, in_sums)
    returned = swap(after(expert_out, arrived), "wide")

    extras = jnp.transpose(back1[:, half:, :half], (1, 0, 2))
    dots1 = jnp.pad(extras, ((0, 0), (0, 0), (0, EXTRA))).reshape(EXTRA, experts * (half + EXTRA))
    dots0 = jnp.concatenate([extras[3:], extras[:3]], axis=0).reshape(EXTRA, experts * half)
    pull = (BALANCE * experts * fraction).reshape(experts, 1)
    hid_grad, con_grad, sums, router_grad, prob_sums, *out_grad = combine(
        weight,
        place,
        narrow_count,
        back0.reshape(experts * half, width),
        back1.reshape(experts * (half + EXTRA), width),
        dots0,
        dots1,
        columns,
        ids,
        logits,
        pull,
        hidden,
        grad_out,
        context,
        moe_in,
        w_out,
        router_rows,
        row(norm2_gain),
    )
    pairs = width // PAIR
    span = pairs // ATTEND_CALLS
    grads, bias_sums = [], []
    packed = [narrow_part(out_grad)]
    for call in range(ATTEND_CALLS):
        dq, dk, dv, column_sums, *weights = attend_back(
            queries,
            keys,
            values,
            soft_weights,
            con_grad,
            normed_t,
            place,
            narrow_count,
            call * span,
            span,
        )
        grads.append((dq, dk, dv))
        packed.append(narrow_part(weights))
        bias_sums.append(column_sums)
    early = jnp.concatenate(packed[:-1], axis=1)
    hid_grad = after(hid_grad, early)
    down_grad = lax.psum_scatter(after(down_sums, early, in_grad, column_sums), "narrow", scatter_dimension=0)
    grad_w_in, grad_w_down, grad_bias_in, grad_bias_down = unpack_expert(
        place, down_grad, in_grad, width // narrow_count
    )
    grad_tokens, norm_sums = close(grads, tokens, hid_grad, row(norm1_gain), w_query, w_key, w_value)
    block_out = block_output(
        returned.reshape(experts * capacity, width), columns, ids, logits, hidden
    )
    bias_sums = jnp.concatenate(bias_sums, axis=1)
    prob_row = jnp.pad(prob_sums.reshape(1, experts), ((0, 0), (0, width - experts)))
    small = jnp.concatenate([norm_sums[:2], bias_sums[:2], sums[:3], prob_row, router_grad], axis=0)
    small = axis_sum(small, "narrow")
    early = wide_part(after(early, returned))
    late = wide_part(after(packed[-1], early, small))
    small = axis_sum(small, "wide")
    early = wide_whole(after(early, late, small))
    late = wide_whole(after(late, early, grad_w_in, block_out))
    upper = is_upper("narrow", 1).astype(jnp.int32).reshape(1, 1)
    blocks = narrow_count // 2
    early = outer_whole(early)
    grad_w_out, *weights = unpack(upper, early, trade(early, "narrow", 1), blocks, width, 1)
    late = outer_whole(late)
    weights = unpack(upper, late, trade(late, "narrow", 1), blocks, width, 0, weights)
    balance_loss = experts * jnp.sum(fraction * (small[7, :experts] / total_tokens))
    return (
        block_out,
        balance_loss,
        grad_tokens,
        small[0],
        small[1],
        weights[0],
        small[2],
        weights[1],
        weights[2],
        small[3],
        grad_w_out,
        small[6],
        small[4],
        small[5],
        jnp.transpose(small[8:]),
        grad_w_in[None],
        grad_bias_in,
        grad_w_down[None],
        grad_bias_down,
    )


def solution(mesh):
    return jax.shard_map(
        per_device,
        mesh=mesh,
        in_specs=(
            P(("wide", "narrow"), None),
            P(("wide", "narrow"), None),
            P(("wide", "narrow"), None),
            P(),
            P(),
            P(),
            P(),
            P(),
            P(),
            P(),
            P(),
            P(),
            P(),
            P(),
            P(),
            P(),
            P(),
            P("wide", None, "narrow"),
            P("wide", "narrow"),
            P("wide", "narrow", None),
            P("wide", None),
        ),
        out_specs=(
            P(("wide", "narrow"), None),
            P(),
            P(("wide", "narrow"), None),
            P(),
            P(),
            P(),
            P(),
            P(),
            P(),
            P(),
            P(),
            P(),
            P(),
            P(),
            P(),
            P("wide", None, "narrow"),
            P("wide", "narrow"),
            P("wide", "narrow", None),
            P("wide", "narrow"),
        ),
        check_vma=False,
    )
```

```python
import functools
import jax
import jax.numpy as jnp
from jax import lax
from jax.experimental import pallas as pl
from jax.experimental.pallas import tpu as pltpu
from jax.sharding import PartitionSpec as P

HEADS = 12
HEAD_DIM = 64
SEQ_LEN = 1024
EPS = 1e-05
BALANCE = 48.0
NEGATIVE = -1e30
PAIR = 2 * HEAD_DIM
F32 = jnp.float32
BF16 = jnp.bfloat16
VMEM_LIMIT = 56 * 1024 * 1024
EXTRA = 8
COVER = 4e10
ATTEND_CALLS = 2


def mm(left, right):
    return lax.dot_general(left, right, (((1,), (0,)), ((), ())), preferred_element_type=F32)


def mm_nt(left, right):
    return lax.dot_general(left, right, (((1,), (1,)), ((), ())), preferred_element_type=F32)


def mm_tn(left, right):
    return lax.dot_general(left, right, (((0,), (0,)), ((), ())), preferred_element_type=F32)


def cost(flops, nbytes, trans=0):
    return pl.CostEstimate(flops=int(flops), bytes_accessed=int(nbytes), transcendentals=int(trans))


def params(*semantics):
    return pltpu.CompilerParams(dimension_semantics=semantics, vmem_limit_bytes=VMEM_LIMIT)


def head_mask(block, head):
    lanes = lax.broadcasted_iota(jnp.int32, block.shape, 1)
    return jnp.where(lanes // HEAD_DIM == head, block, jnp.zeros_like(block))


def causal(scores, block):
    keys = scores.shape[0]
    first = lax.broadcasted_iota(jnp.int32, (block, block), 0)
    second = lax.broadcasted_iota(jnp.int32, (block, block), 1)
    last = jnp.where(first <= second, scores[keys - block :], NEGATIVE)
    if keys == block:
        return last
    return jnp.concatenate([scores[: keys - block], last], axis=0)


def attend_kernel(block, q_ref, k_ref, v_ref, context_ref, weights_ref):
    rows = q_ref.shape[0]
    keys = k_ref[...]
    values = v_ref[...]
    place = 0
    for first in range(0, rows, block):
        span = first + block
        query = q_ref[first:span, :]
        weights_both, values_both = [], []
        for head in range(2):
            scores = causal(mm_nt(keys[:span], head_mask(query, head)), block)
            peak = jnp.max(scores, axis=0, keepdims=True)
            powers = jnp.exp(scores - peak)
            total = jnp.sum(powers, axis=0, keepdims=True)
            weights = (powers * (1.0 / total)).astype(BF16)
            weights_ref[0, head, place : place + span, :] = weights
            weights_both.append(weights)
            values_both.append(head_mask(values[:span], head))
        out = mm_tn(jnp.concatenate(weights_both, axis=0), jnp.concatenate(values_both, axis=0))
        context_ref[first:span, :] = out.astype(BF16)
        place += span


def attend(queries, keys, values, block=256):
    rows, width = queries.shape
    pairs = width // PAIR
    kept = sum(range(block, rows + 1, block))
    spec = pl.BlockSpec((rows, PAIR), lambda p: (0, p))
    return pl.pallas_call(
        functools.partial(attend_kernel, block),
        grid=(pairs,),
        in_specs=[spec, spec, spec],
        out_specs=[spec, pl.BlockSpec((1, 2, kept, block), lambda p: (p, 0, 0, 0))],
        out_shape=[
            jax.ShapeDtypeStruct((rows, width), BF16),
            jax.ShapeDtypeStruct((pairs, 2, kept, block), BF16),
        ],
        compiler_params=params("arbitrary"),
        cost_estimate=cost(4 * rows * rows * width * 2, rows * width * 8, pairs * 2 * rows * rows),
        name="attend",
    )(queries, keys, values)


def attend_back_kernel(block, shares, place_ref, q_ref, k_ref, v_ref, weights_ref, g_ref, normed_ref,
                       dq_ref, dk_ref, dv_ref, sums_ref, *refs):
    share_refs, (packed_ref, dq_acc, dk_acc, dv_acc) = refs[:shares], refs[shares:]
    rows = q_ref.shape[0]
    keys = k_ref[...]
    values = v_ref[...]
    place = weights_ref.shape[2]
    for first in reversed(range(0, rows, block)):
        span = first + block
        place -= span
        query = q_ref[first:span, :]
        grad = g_ref[first:span, :]
        probs_both, scores_both, query_both, grad_both = [], [], [], []
        for head in range(2):
            query_h = head_mask(query, head)
            grad_h = head_mask(grad, head)
            weights = weights_ref[0, head, place : place + span, :]
            probs = weights.astype(F32)
            grad_probs = mm_nt(values[:span], grad_h)
            inner = jnp.sum(probs * grad_probs, axis=0, keepdims=True)
            grad_scores = (probs * (grad_probs - inner)).astype(BF16)
            probs_both.append(weights)
            scores_both.append(grad_scores)
            query_both.append(query_h)
            grad_both.append(grad_h)
        dv = mm(jnp.concatenate(probs_both, axis=1), jnp.concatenate(grad_both, axis=0))
        dk = mm(jnp.concatenate(scores_both, axis=1), jnp.concatenate(query_both, axis=0))
        if span == rows:
            dv_acc[...] = dv
            dk_acc[...] = dk
        else:
            dv_acc[:span, :] += dv
            dk_acc[:span, :] += dk
        keys_both = jnp.concatenate([head_mask(keys[:span], head) for head in range(2)], axis=0)
        dq = mm_tn(jnp.concatenate(scores_both, axis=0), keys_both) * 0.125
        dq_acc[first:span, :] = dq.astype(BF16)
    dq = dq_acc[...]
    dk = dk_acc[...].astype(BF16)
    dv = dv_acc[...].astype(BF16)
    dq_ref[...] = dq
    dk_ref[...] = dk
    dv_ref[...] = dv
    normed = normed_ref[...]
    packed_ref[:, : 2 * PAIR] = mm(normed, jnp.concatenate([dq, dk], axis=1)).astype(BF16)
    packed_ref[:, 2 * PAIR :] = mm(normed, dv).astype(BF16)
    deal(packed_ref, share_refs, place_ref[0, 0])
    sums_ref[...] = jnp.concatenate(
        [
            jnp.sum(dq.astype(F32), axis=0, keepdims=True),
            jnp.sum(dv.astype(F32), axis=0, keepdims=True),
            jnp.zeros((6, PAIR), F32),
        ],
        axis=0,
    )


def attend_back(queries, keys, values, weights, grad_context, normed_t, place, shares, start, pairs, block=256):
    rows, width = queries.shape
    spec = pl.BlockSpec((rows, PAIR), lambda p: (0, p + start))
    out_spec = pl.BlockSpec((rows, PAIR), lambda p: (0, p))
    return pl.pallas_call(
        functools.partial(attend_back_kernel, block, shares),
        grid=(pairs,),
        in_specs=[
            pl.BlockSpec(memory_space=pltpu.SMEM),
            spec,
            spec,
            spec,
            pl.BlockSpec((1, 2) + weights.shape[2:], lambda p: (p + start, 0, 0, 0)),
            spec,
            pl.BlockSpec((width, rows), lambda p: (0, 0)),
        ],
        out_specs=[
            out_spec,
            out_spec,
            out_spec,
            pl.BlockSpec((8, PAIR), lambda p: (0, p)),
        ]
        + [pl.BlockSpec((width // shares, 3 * PAIR), lambda p: (0, p))] * shares,
        out_shape=[jax.ShapeDtypeStruct((rows, pairs * PAIR), BF16)] * 3
        + [jax.ShapeDtypeStruct((8, pairs * PAIR), F32)]
        + [jax.ShapeDtypeStruct((width // shares, 3 * pairs * PAIR), BF16)] * shares,
        scratch_shapes=[
            pltpu.VMEM((width, 3 * PAIR), BF16),
            pltpu.VMEM((rows, PAIR), BF16),
            pltpu.VMEM((rows, PAIR), F32),
            pltpu.VMEM((rows, PAIR), F32),
        ],
        compiler_params=params("arbitrary"),
        cost_estimate=cost(rows, rows),
        name="attend_back",
    )(place, queries, keys, values, weights, grad_context, normed_t)


def normalise(values):
    centred = values - jnp.mean(values, axis=-1, keepdims=True)
    spread = lax.rsqrt(jnp.mean(centred * centred, axis=-1, keepdims=True) + EPS)
    return centred * spread, spread


def normalise_back(grad, unit, spread, gain):
    scaled = grad * gain
    mean = jnp.mean(scaled, axis=-1, keepdims=True)
    tilt = jnp.mean(scaled * unit, axis=-1, keepdims=True)
    return spread * (scaled - mean - unit * tilt)


def pieces(values):
    high = values.astype(BF16)
    rest = values - high.astype(F32)
    middle = rest.astype(BF16)
    low = (rest - middle.astype(F32)).astype(BF16)
    fill = jnp.zeros((5, values.shape[1]), F32)
    stacked = jnp.concatenate(
        [high.astype(F32), middle.astype(F32), low.astype(F32), fill], axis=0
    )
    return stacked.astype(BF16)


def join(parts):
    return parts[0:1] + parts[1:2] + parts[2:3]


def column(row):
    return jnp.transpose(jnp.broadcast_to(row, (8, row.shape[1])))[:, 0:1]


def gate_row(logits, picked):
    return jax.nn.sigmoid(jnp.sum(jnp.where(picked, logits, 0.0), axis=0, keepdims=True))


def picked_rows(ids, experts):
    return lax.broadcasted_iota(jnp.int32, (experts, ids.shape[1]), 0) == ids


def one_hot_rows(slots, first, count):
    places = lax.broadcasted_iota(jnp.int32, (count, slots.shape[1]), 0) + first
    return (places == slots).astype(F32).astype(BF16)


def one_hot_columns(slots, first, count):
    places = lax.broadcasted_iota(jnp.int32, (slots.shape[0], count), 1) + first
    return (places == slots).astype(F32).astype(BF16)


def route_kernel(experts, capacity, row_ref, grad_ref, slots_ref, columns_ref, out_ref, count_row):
    step = pl.program_id(0)
    rows = row_ref.shape[1]
    width = grad_ref.shape[1]
    half = capacity // 2

    @pl.when(step == 0)
    def _():
        block = 256
        ids = row_ref[...]
        picked = picked_rows(ids, experts).astype(F32)
        first = lax.broadcasted_iota(jnp.int32, (block, block), 0)
        second = lax.broadcasted_iota(jnp.int32, (block, block), 1)
        earlier = (first < second).astype(F32).astype(BF16)
        passed = jnp.zeros((experts, 1), F32)
        places = []
        for start in range(0, rows, block):
            own = picked[:, start : start + block]
            before = mm(own.astype(BF16), earlier) + passed
            places.append(jnp.sum(before * own, axis=0, keepdims=True))
            passed = passed + jnp.sum(own, axis=1, keepdims=True)
        place = jnp.concatenate(places, axis=1).astype(jnp.int32)
        slots = ids * capacity + place
        late = experts * half + ids * (half + EXTRA) + place - half
        mixed = jnp.where(place < half, ids * half + place, late)
        slots_ref[...] = slots
        both = jnp.concatenate([mixed, slots, jnp.zeros((6, rows), jnp.int32)], axis=0)
        columns_ref[...] = jnp.transpose(both.astype(F32))[:, 0:2].astype(jnp.int32)
        count_row[...] = jnp.zeros_like(count_row)
        lanes = lax.broadcasted_iota(jnp.int32, (experts, 128), 1)
        spread = jnp.where(lanes == lax.broadcasted_iota(jnp.int32, (experts, 128), 0), passed, 0.0)
        count_row[0:1, 0:128] = jnp.sum(spread, axis=0, keepdims=True)

    group = out_ref.shape[0]
    chosen = one_hot_rows(slots_ref[...], step * group * capacity, group * capacity)
    dealt = mm(chosen, grad_ref[...]).astype(BF16)
    for index in range(group):
        out_ref[index, :capacity, :] = dealt[index * capacity : (index + 1) * capacity]
        out_ref[index, capacity:, :] = count_row[...].astype(BF16)


def route(routes, grad_out, experts, capacity):
    rows, width = grad_out.shape
    whole = lambda e: (0, 0)
    group = 2
    return pl.pallas_call(
        functools.partial(route_kernel, experts, capacity),
        grid=(experts // group,),
        in_specs=[
            pl.BlockSpec((1, rows), whole),
            pl.BlockSpec((rows, width), whole),
        ],
        out_specs=[
            pl.BlockSpec((1, rows), whole),
            pl.BlockSpec((rows, 2), whole),
            pl.BlockSpec((group, capacity + EXTRA, width), lambda e: (e, 0, 0)),
        ],
        out_shape=[
            jax.ShapeDtypeStruct((1, rows), jnp.int32),
            jax.ShapeDtypeStruct((rows, 2), jnp.int32),
            jax.ShapeDtypeStruct((experts, capacity + EXTRA, width), BF16),
        ],
        scratch_shapes=[pltpu.VMEM((EXTRA, width), F32)],
        compiler_params=params("arbitrary"),
        cost_estimate=cost(2 * experts * capacity * rows * width, 6 * rows * width),
        name="route",
    )(routes.reshape(1, rows), grad_out)


def project_kernel(tokens_ref, gain_ref, shift_ref, wq_ref, bq_ref, wk_ref, wv_ref, bv_ref,
                   normed_ref, q_ref, k_ref, v_ref):
    unit, _ = normalise(tokens_ref[...].astype(F32))
    normed = (unit * gain_ref[...] + shift_ref[...]).astype(BF16)
    normed_ref[...] = jnp.transpose(normed)
    q_ref[...] = ((mm(normed, wq_ref[...]) + bq_ref[...]) * 0.125).astype(BF16)
    k_ref[...] = mm(normed, wk_ref[...]).astype(BF16)
    v_ref[...] = (mm(normed, wv_ref[...]) + bv_ref[...]).astype(BF16)


def project(tokens, gain, shift, w_query, bias_query, w_key, w_value, bias_value, tile=256):
    rows, width = tokens.shape
    row_spec = pl.BlockSpec((tile, width), lambda t: (t, 0))
    vector = pl.BlockSpec((1, width), lambda t: (0, 0))
    square = pl.BlockSpec((width, width), lambda t: (0, 0))
    return pl.pallas_call(
        project_kernel,
        grid=(rows // tile,),
        in_specs=[row_spec, vector, vector, square, vector, square, square, vector],
        out_specs=[pl.BlockSpec((width, tile), lambda t: (0, t))] + [row_spec] * 3,
        out_shape=[jax.ShapeDtypeStruct((width, rows), BF16)]
        + [jax.ShapeDtypeStruct((rows, width), BF16)] * 3,
        compiler_params=params("arbitrary"),
        cost_estimate=cost(6 * rows * width * width, 10 * rows * width + 6 * width * width),
        name="project",
    )(tokens, gain, shift, w_query, bias_query, w_key, w_value, bias_value)


def settle_kernel(context_ref, tokens_ref, w_out_ref, bias_ref, gain_ref, shift_ref, router_ref,
                  hidden_ref, moe_ref, logits_ref):
    hidden = tokens_ref[...].astype(F32) + mm(context_ref[...], w_out_ref[...]) + bias_ref[...]
    unit, _ = normalise(hidden)
    moe_in = (unit * gain_ref[...] + shift_ref[...]).astype(BF16)
    hidden_ref[...] = hidden
    moe_ref[...] = moe_in
    logits_ref[...] = mm_nt(router_ref[...], moe_in)


def settle(context, tokens, w_out, bias_out, gain, shift, router_rows, tile=256):
    rows, width = tokens.shape
    experts = router_rows.shape[0]
    row_spec = pl.BlockSpec((tile, width), lambda t: (t, 0))
    vector = pl.BlockSpec((1, width), lambda t: (0, 0))
    return pl.pallas_call(
        settle_kernel,
        grid=(rows // tile,),
        in_specs=[
            row_spec,
            row_spec,
            pl.BlockSpec((width, width), lambda t: (0, 0)),
            vector,
            vector,
            vector,
            pl.BlockSpec((experts, width), lambda t: (0, 0)),
        ],
        out_specs=[row_spec, row_spec, pl.BlockSpec((experts, tile), lambda t: (0, t))],
        out_shape=[
            jax.ShapeDtypeStruct((rows, width), F32),
            jax.ShapeDtypeStruct((rows, width), BF16),
            jax.ShapeDtypeStruct((experts, rows), F32),
        ],
        compiler_params=params("arbitrary"),
        cost_estimate=cost(2 * rows * width * width, 10 * rows * width + 2 * width * width),
        name="settle",
    )(context, tokens, w_out, bias_out, gain, shift, router_rows)


def dispatch_kernel(weight_ref, slots_ref, ids_ref, logits_ref, moe_ref, first_ref, second_ref, parts):
    step = pl.program_id(0)
    experts = logits_ref.shape[0]
    half = first_ref.shape[1]

    @pl.when(step == 0)
    def _():
        gate = gate_row(logits_ref[...], picked_rows(ids_ref[...], experts))
        parts[...] = pieces(gate * weight_ref[0, 0])

    chosen = one_hot_rows(slots_ref[...], step * 2 * half, 2 * half)
    rows = mm(chosen, moe_ref[...]).astype(BF16)
    first_ref[0] = rows[:half]
    second_ref[0, :half, :] = rows[half:]
    second_ref[0, half:, :] = jnp.zeros((EXTRA, rows.shape[1]), BF16)
    second_ref[0, half:, 0 : 2 * half] = mm_nt(parts[...], chosen).astype(BF16)


def dispatch(weight, slots, ids, logits, moe_in, capacity):
    rows, width = moe_in.shape
    experts = logits.shape[0]
    half = capacity // 2
    whole = lambda e: (0, 0)
    return pl.pallas_call(
        dispatch_kernel,
        grid=(experts,),
        in_specs=[
            pl.BlockSpec(memory_space=pltpu.SMEM),
            pl.BlockSpec((1, rows), whole),
            pl.BlockSpec((1, rows), whole),
            pl.BlockSpec((experts, rows), whole),
            pl.BlockSpec((rows, width), whole),
        ],
        out_specs=[
            pl.BlockSpec((1, half, width), lambda e: (e, 0, 0)),
            pl.BlockSpec((1, half + EXTRA, width), lambda e: (e, 0, 0)),
        ],
        out_shape=[
            jax.ShapeDtypeStruct((experts, half, width), BF16),
            jax.ShapeDtypeStruct((experts, half + EXTRA, width), BF16),
        ],
        scratch_shapes=[pltpu.VMEM((8, rows), BF16)],
        compiler_params=params("arbitrary"),
        cost_estimate=cost(2 * experts * capacity * rows * width, 6 * rows * width),
        name="dispatch",
    )(weight, slots, ids, logits, moe_in)


def row_sum(values):
    ones = jnp.ones((8, values.shape[1]), BF16)
    high = values.astype(BF16)
    rest = values - high.astype(F32)
    middle = rest.astype(BF16)
    low = (rest - middle.astype(F32)).astype(BF16)
    return (mm_nt(ones, high) + mm_nt(ones, middle) + mm_nt(ones, low))[0:1]


def expert_kernel(steps, chunk, *refs):
    if chunk == 0:
        (x_ref, g_ref, w_in_ref, b_in_ref, w_down_ref, b_down_ref,
         act_ref, up_ref, out_ref, back_ref, dot_ref, back_acc, dot_acc, out_acc) = refs
    else:
        (x_ref, g_ref, w_in_ref, b_in_ref, w_down_ref, b_down_ref, _, _, _, earlier_ref,
         act_ref, up_ref, out_ref, back_ref, back_acc, dot_acc, out_acc) = refs
    part = pl.program_id(0)
    tile = pl.program_id(1)
    group, half, width = x_ref.shape
    rows = group * half
    x = x_ref[...].reshape(rows, width)
    g = g_ref[...].reshape(rows, width)
    w_in = w_in_ref[0]
    pre = mm(x, w_in) + b_in_ref[0].astype(F32)
    grad_act = mm_nt(g, w_down_ref[0])
    below = 0.5 + 0.5 * lax.erf(pre * 0.7071067811865476)
    act = pre * below
    slope = below + pre * (0.3989422804014327 * jnp.exp(-0.5 * pre * pre))
    up = (grad_act * slope).astype(BF16)
    rounded = act.astype(BF16)
    act_ref[0, 0] = rounded
    up_ref[0, 0] = up
    out = mm(rounded, w_down_ref[0])
    product = act * grad_act
    lanes = min(128, product.shape[1])
    folded = product[:, :lanes]
    for lane in range(lanes, product.shape[1], lanes):
        folded = folded + product[:, lane : lane + lanes]
    where = pl.ds(pl.multiple_of(tile * rows, rows), rows)
    back = mm_nt(up, w_in)

    @pl.when(part == 0)
    def _():
        biased = g.astype(F32) * b_down_ref[...].astype(F32)
        total = folded
        for lane in range(0, biased.shape[1], lanes):
            total = total + biased[:, lane : lane + lanes]
        back_acc[where, :] = back
        out_acc[where, :] = out + b_down_ref[...].astype(F32)
        dot_acc[where, :] = total

    @pl.when(part > 0)
    def _():
        back_acc[where, :] += back
        out_acc[where, :] += out
        dot_acc[where, :] += folded

    @pl.when(part == steps - 1)
    def _():
        out_ref[...] = out_acc[where, :].astype(BF16).reshape(group, half, width)
        back_ref[:, :half, :] = back_acc[where, :].astype(BF16).reshape(group, half, width)
        dots = dot_acc[where, :]
        for index in range(group):
            own = pieces(row_sum(dots[index * half : (index + 1) * half, :])).astype(F32)
            if chunk == 0:
                dot_ref[index] = own.astype(BF16)
            else:
                before = earlier_ref[index].astype(F32)
                extra = jnp.concatenate([own[0:3], before[0:3], own[6:8]], axis=0)
                back_ref[index, half:, :] = jnp.zeros((EXTRA, width), BF16)
                back_ref[index, half:, 0:half] = extra.astype(BF16)


def expert(x, g, w_in, b_in, w_down, b_down, chunk, earlier=()):
    sources, width = x.shape[0], x.shape[2]
    half = (g.shape[1] - EXTRA) // 2
    rows = sources * half
    parts, _, hidden = w_in.shape
    group = max(1, 256 // half)
    tile = group * half
    tiles = sources // group
    last = parts - 1
    late = lambda p, t: jnp.where(p == last, t, 0)
    wide_spec = pl.BlockSpec((1, 1, tile, hidden), lambda p, t: (p, chunk, t, 0))
    wide_shape = jax.ShapeDtypeStruct((parts, 2, rows, hidden), BF16)
    dot_shape = jax.ShapeDtypeStruct((sources, 8, half), BF16)
    dot_spec = pl.BlockSpec((group, 8, half), lambda p, t: (late(p, t), 0, 0))
    back_rows = half + EXTRA * chunk
    return pl.pallas_call(
        functools.partial(expert_kernel, parts, chunk),
        grid=(parts, tiles),
        in_specs=[
            pl.BlockSpec((group, half, width), lambda p, t: (t, 0, 0)),
            pl.BlockSpec((group, half, width), lambda p, t: (t, chunk, 0)),
            pl.BlockSpec((1, width, hidden), lambda p, t: (p, 0, 0)),
            pl.BlockSpec((1, 1, hidden), lambda p, t: (p, 0, 0)),
            pl.BlockSpec((1, hidden, width), lambda p, t: (p, 0, 0)),
            pl.BlockSpec((1, width), lambda p, t: (0, 0)),
        ]
        + ([pl.BlockSpec(memory_space=pl.ANY)] * 3 + [dot_spec] if chunk else []),
        out_specs=[
            wide_spec,
            wide_spec,
            pl.BlockSpec((group, half, width), lambda p, t: (late(p, t), chunk, 0)),
            pl.BlockSpec((group, back_rows, width), lambda p, t: (late(p, t), 0, 0)),
        ]
        + ([] if chunk else [dot_spec]),
        out_shape=[
            wide_shape,
            wide_shape,
            jax.ShapeDtypeStruct((sources, 2 * half, width), BF16),
            jax.ShapeDtypeStruct((sources, back_rows, width), BF16),
        ]
        + ([] if chunk else [dot_shape]),
        scratch_shapes=[
            pltpu.VMEM((rows, width), F32),
            pltpu.VMEM((rows, min(128, hidden)), F32),
            pltpu.VMEM((rows, width), F32),
        ],
        input_output_aliases={6: 0, 7: 1, 8: 2} if chunk else {},
        compiler_params=params("arbitrary", "arbitrary"),
        cost_estimate=cost(
            6 * rows * width * hidden * parts, rows * hidden * parts * 4, 2 * rows * hidden * parts
        ),
        name="expert",
    )(x, g, w_in, b_in, w_down, b_down, *earlier)


def weight_kernel(parts, x0_ref, x1_ref, g_ref, act_ref, up_ref, scale_ref,
                  down_ref, in_ref, down_acc, in_acc, bias_acc, bias_down_acc, flipped):
    part = pl.program_id(0)
    chunk = pl.program_id(1)
    sources, half, width = x0_ref.shape
    rows = sources * half
    hidden = act_ref.shape[3]
    scale = scale_ref[0]
    split = pieces(scale)
    g = g_ref[...].reshape(rows, width)

    def flip(values):
        return (jnp.transpose(values).astype(F32) * scale).astype(BF16)

    @pl.when((part == 0) & (chunk == 0))
    def _():
        flipped[0] = flip(x0_ref[...].reshape(rows, width))

    @pl.when((part == 0) & (chunk == 1))
    def _():
        flipped[1] = flip(x1_ref[...].reshape(rows, width))

    act = act_ref[0, 0]
    up = up_ref[0, 0]
    down = mm(flip(act), g)
    into = mm(flipped[chunk], up)
    bias_in = join(mm(split, up))

    @pl.when(chunk == 0)
    def _():
        down_acc[...] = down
        in_acc[...] = into
        bias_acc[...] = bias_in

    @pl.when(chunk == 1)
    def _():
        down_ref[0, :hidden, :] = (down_acc[...] + down).astype(BF16)
        in_ref[0] = (in_acc[...] + into).astype(BF16)

    @pl.when(part == 0)
    def _():
        bias_down = join(mm(split, g))
        bias_down_acc[...] = jnp.where(chunk == 0, bias_down, bias_down_acc[...] + bias_down)

    @pl.when(chunk == 1)
    def _():
        down_ref[0, hidden:, :] = jnp.zeros((EXTRA, width), BF16)
        down_ref[0, hidden : hidden + 1, 0:hidden] = (bias_acc[...] + bias_in).astype(BF16)
        down_ref[0, hidden + 1 : hidden + 2, :] = bias_down_acc[...].astype(BF16)


def weight_grads(x0, x1, g, act, up, scale):
    sources, half, width = x0.shape
    parts, _, rows, hidden = act.shape
    wide_spec = pl.BlockSpec((1, 1, rows, hidden), lambda p, t: (p, t, 0, 0))
    return pl.pallas_call(
        functools.partial(weight_kernel, parts),
        grid=(parts, 2),
        in_specs=[
            pl.BlockSpec((sources, half, width), lambda p, t: (0, 0, 0)),
            pl.BlockSpec((sources, half, width), lambda p, t: (0, 0, 0)),
            pl.BlockSpec((sources, half, width), lambda p, t: (0, t, 0)),
            wide_spec,
            wide_spec,
            pl.BlockSpec((1, 1, rows), lambda p, t: (t, 0, 0)),
        ],
        out_specs=[
            pl.BlockSpec((1, hidden + EXTRA, width), lambda p, t: (p, 0, 0)),
            pl.BlockSpec((1, width, hidden), lambda p, t: (p, 0, 0)),
        ],
        out_shape=[
            jax.ShapeDtypeStruct((parts, hidden + EXTRA, width), BF16),
            jax.ShapeDtypeStruct((parts, width, hidden), BF16),
        ],
        scratch_shapes=[
            pltpu.VMEM((hidden, width), F32),
            pltpu.VMEM((width, hidden), F32),
            pltpu.VMEM((1, hidden), F32),
            pltpu.VMEM((1, width), F32),
            pltpu.VMEM((2, width, rows), BF16),
        ],
        compiler_params=params("arbitrary", "arbitrary"),
        cost_estimate=cost(12 * rows * width * hidden * parts, rows * hidden * parts * 8),
        name="weight_grads",
    )(x0, x1, g, act, up, scale)


def deal(rows_ref, share_refs, place):
    count = share_refs[0].shape[0]
    for index, share_ref in enumerate(share_refs):
        first = jnp.bitwise_xor(place, index) * count
        share_ref[...] = rows_ref[pl.ds(pl.multiple_of(first, count), count), :]


def combine_kernel(shares, weight_ref, place_ref, back0_ref, back1_ref, dots0_ref, dots1_ref, columns_ref, ids_ref, logits_ref, pull_ref,
                   hidden_ref, grad_ref, context_ref, moe_ref, w_out_ref, router_ref, gain_ref,
                   hid_grad_ref, con_grad_ref, sums_ref, router_grad_ref, probs_ref, *refs):
    out_refs, (branches, out_rows) = refs[:shares], refs[shares:]
    step = pl.program_id(0)
    experts = logits_ref.shape[0]
    count0 = back0_ref.shape[0]
    count1 = back1_ref.shape[0]
    weight = weight_ref[0, 0]
    columns = columns_ref[:, 0:1]
    chosen0 = one_hot_columns(columns, 0, count0)
    chosen1 = one_hot_columns(columns, count0, count1)
    rows = mm(chosen0, back0_ref[...]) + mm(chosen1, back1_ref[...])
    dots = join(mm_nt(dots0_ref[...], chosen0)) + join(mm_nt(dots1_ref[...], chosen1))
    logits = logits_ref[...]
    picked = picked_rows(ids_ref[...], experts)
    gate = gate_row(logits, picked)
    powers = jnp.exp(logits - jnp.max(logits, axis=0, keepdims=True))
    probs = powers / jnp.sum(powers, axis=0, keepdims=True)
    pull = pull_ref[...]
    slope = dots * weight * gate * (1.0 - gate)
    logit_grad = probs * (pull - jnp.sum(probs * pull, axis=0, keepdims=True))
    logit_grad = (logit_grad + jnp.where(picked, slope, 0.0)).astype(BF16)
    moe_grad = mm_tn(logit_grad, router_ref[...]) + rows * column(gate * weight)
    unit, spread = normalise(hidden_ref[...])
    hid_grad = weight * grad_ref[...].astype(F32) + normalise_back(
        moe_grad, unit, spread, gain_ref[...]
    )
    branch = hid_grad.astype(BF16)
    hid_grad_ref[...] = hid_grad
    con_grad_ref[...] = mm_nt(branch, w_out_ref[...]).astype(BF16)
    branches[pl.ds(pl.multiple_of(step * branch.shape[0], branch.shape[0]), branch.shape[0]), :] = branch
    router_grad = mm(logit_grad, moe_ref[...])
    prob_sum = jnp.sum(probs, axis=1, keepdims=True)
    sums = jnp.concatenate(
        [
            jnp.sum(moe_grad * unit, axis=0, keepdims=True),
            jnp.sum(moe_grad, axis=0, keepdims=True),
            jnp.sum(branch.astype(F32), axis=0, keepdims=True),
            jnp.zeros((5, unit.shape[1]), F32),
        ],
        axis=0,
    )

    @pl.when(step == 0)
    def _():
        router_grad_ref[...] = router_grad
        probs_ref[...] = prob_sum
        sums_ref[...] = sums

    @pl.when(step > 0)
    def _():
        router_grad_ref[...] += router_grad
        probs_ref[...] += prob_sum
        sums_ref[...] += sums

    @pl.when(step == pl.num_programs(0) - 1)
    def _():
        out_rows[...] = mm_tn(context_ref[...], branches[...]).astype(BF16)
        deal(out_rows, out_refs, place_ref[0, 0])


def combine(weight, place, shares, back0, back1, dots0, dots1, columns, ids, logits, pull, hidden, grad_out, context, moe_in,
            w_out, router_rows, gain, tile=256):
    rows, width = hidden.shape
    experts = logits.shape[0]
    count = back0.shape[0]
    count1 = back1.shape[0]
    whole = lambda t: (0, 0)
    row_spec = pl.BlockSpec((tile, width), lambda t: (t, 0))
    square = pl.BlockSpec((width, width), whole)
    return pl.pallas_call(
        functools.partial(combine_kernel, shares),
        grid=(rows // tile,),
        in_specs=[
            pl.BlockSpec(memory_space=pltpu.SMEM),
            pl.BlockSpec(memory_space=pltpu.SMEM),
            pl.BlockSpec((count, width), whole),
            pl.BlockSpec((count1, width), whole),
            pl.BlockSpec((8, count), whole),
            pl.BlockSpec((8, count1), whole),
            pl.BlockSpec((tile, 2), lambda t: (t, 0)),
            pl.BlockSpec((1, tile), lambda t: (0, t)),
            pl.BlockSpec((experts, tile), lambda t: (0, t)),
            pl.BlockSpec((experts, 1), whole),
            row_spec,
            row_spec,
            pl.BlockSpec((rows, width), whole),
            row_spec,
            square,
            pl.BlockSpec((experts, width), whole),
            pl.BlockSpec((1, width), whole),
        ],
        out_specs=[
            row_spec,
            row_spec,
            pl.BlockSpec((8, width), whole),
            pl.BlockSpec((experts, width), whole),
            pl.BlockSpec((experts, 1), whole),
        ]
        + [pl.BlockSpec((width // shares, width), whole)] * shares,
        out_shape=[
            jax.ShapeDtypeStruct((rows, width), F32),
            jax.ShapeDtypeStruct((rows, width), BF16),
            jax.ShapeDtypeStruct((8, width), F32),
            jax.ShapeDtypeStruct((experts, width), F32),
            jax.ShapeDtypeStruct((experts, 1), F32),
        ]
        + [jax.ShapeDtypeStruct((width // shares, width), BF16)] * shares,
        scratch_shapes=[pltpu.VMEM((rows, width), BF16), pltpu.VMEM((width, width), BF16)],
        compiler_params=params("arbitrary"),
        cost_estimate=cost(rows, rows),
        name="combine",
    )(weight, place, back0, back1, dots0, dots1, columns, ids, logits, pull, hidden, grad_out, context, moe_in, w_out,
      router_rows, gain)


def close_kernel(count, *refs):
    grads = refs[: 3 * count]
    (tokens_ref, hid_grad_ref, gain_ref, wq_ref, wk_ref, wv_ref, tok_grad_ref, sums_ref) = refs[3 * count :]
    step = pl.program_id(0)
    width = tokens_ref.shape[1]
    norm_grad = None
    for index, weights in enumerate((wq_ref, wk_ref, wv_ref)):
        parts = [grads[3 * part + index][...] for part in range(count)]
        term = mm_nt(jnp.concatenate(parts, axis=1), weights[...])
        norm_grad = term if norm_grad is None else norm_grad + term
    unit, spread = normalise(tokens_ref[...].astype(F32))
    tok_grad = hid_grad_ref[...] + normalise_back(norm_grad, unit, spread, gain_ref[...])
    tok_grad_ref[...] = tok_grad.astype(BF16)
    sums = jnp.concatenate(
        [
            jnp.sum(norm_grad * unit, axis=0, keepdims=True),
            jnp.sum(norm_grad, axis=0, keepdims=True),
            jnp.zeros((6, width), F32),
        ],
        axis=0,
    )

    @pl.when(step == 0)
    def _():
        sums_ref[...] = sums

    @pl.when(step > 0)
    def _():
        sums_ref[...] += sums


def close(grads, tokens, hid_grad, gain, w_query, w_key, w_value, tile=256):
    rows, width = tokens.shape
    whole = lambda t: (0, 0)
    row_spec = pl.BlockSpec((tile, width), lambda t: (t, 0))
    square = pl.BlockSpec((width, width), whole)
    flat = [item for triple in grads for item in triple]
    return pl.pallas_call(
        functools.partial(close_kernel, len(grads)),
        grid=(rows // tile,),
        in_specs=[pl.BlockSpec((tile, item.shape[1]), lambda t: (t, 0)) for item in flat]
        + [row_spec, row_spec, pl.BlockSpec((1, width), whole), square, square, square],
        out_specs=[row_spec, pl.BlockSpec((8, width), whole)],
        out_shape=[
            jax.ShapeDtypeStruct((rows, width), BF16),
            jax.ShapeDtypeStruct((8, width), F32),
        ],
        compiler_params=params("arbitrary"),
        cost_estimate=cost(COVER, 4096),
        name="close",
    )(*flat, tokens, hid_grad, gain, w_query, w_key, w_value)


def block_out_kernel(back_ref, columns_ref, ids_ref, logits_ref, hidden_ref, out_ref):
    chosen = one_hot_columns(columns_ref[:, 1:2], 0, back_ref.shape[0])
    rows = mm(chosen, back_ref[...])
    gate = gate_row(logits_ref[...], picked_rows(ids_ref[...], logits_ref.shape[0]))
    out_ref[...] = (hidden_ref[...] + column(gate) * rows).astype(BF16)


def block_output(back, columns, ids, logits, hidden, tile=256):
    rows, width = hidden.shape
    experts = logits.shape[0]
    count = back.shape[0]
    row_spec = pl.BlockSpec((tile, width), lambda t: (t, 0))
    return pl.pallas_call(
        block_out_kernel,
        grid=(rows // tile,),
        in_specs=[
            pl.BlockSpec((count, width), lambda t: (0, 0)),
            pl.BlockSpec((tile, 2), lambda t: (t, 0)),
            pl.BlockSpec((1, tile), lambda t: (0, t)),
            pl.BlockSpec((experts, tile), lambda t: (0, t)),
            row_spec,
        ],
        out_specs=row_spec,
        out_shape=jax.ShapeDtypeStruct((rows, width), BF16),
        compiler_params=params("arbitrary"),
        cost_estimate=cost(COVER, 4096),
        name="block_output",
    )(back, columns, ids, logits, hidden)


def unpack_expert_kernel(place_ref, down_rows, in_rows, in_ref, down_ref, bias_in_ref, bias_down_ref):
    width, hidden = in_ref.shape
    share = bias_down_ref.shape[1]
    in_ref[...] = in_rows[...].astype(F32)
    down_ref[...] = down_rows[:hidden, :].astype(F32)
    extra = down_rows[hidden:, :].astype(F32)
    bias_in_ref[...] = extra[0:1, :hidden]
    for place in range(width // share):

        @pl.when(place_ref[0, 0] == place)
        def _():
            bias_down_ref[...] = extra[1:2, place * share : (place + 1) * share]


def unpack_expert(place, down_rows, in_rows, share):
    width, hidden = in_rows.shape
    memory = pl.BlockSpec(memory_space=pltpu.VMEM)
    return pl.pallas_call(
        unpack_expert_kernel,
        in_specs=[pl.BlockSpec(memory_space=pltpu.SMEM), memory, memory],
        out_specs=[memory] * 4,
        out_shape=[
            jax.ShapeDtypeStruct((width, hidden), F32),
            jax.ShapeDtypeStruct((hidden, width), F32),
            jax.ShapeDtypeStruct((1, hidden), F32),
            jax.ShapeDtypeStruct((1, share), F32),
        ],
        compiler_params=params(),
        cost_estimate=cost(COVER, width * hidden),
        name="unpack_expert",
    )(place, down_rows, in_rows)


def unpack_kernel(lead, upper_ref, own_ref, other_ref, *refs):
    outs = refs[len(refs) - (3 + lead) :]
    width = outs[-1].shape[1]

    def write(ref):
        base = 0
        if lead:
            base = outs[0].shape[1]
            outs[0][...] = ref[:, :base].astype(F32)
        for place in range(0, width, PAIR):
            for index in range(3):
                first = base + 3 * place + index * PAIR
                outs[lead + index][:, place : place + PAIR] = ref[:, first : first + PAIR].astype(F32)

    own = pl.program_id(0) == upper_ref[0, 0]

    @pl.when(own)
    def _():
        write(own_ref)

    @pl.when(jnp.logical_not(own))
    def _():
        write(other_ref)


def unpack(upper, own, other, blocks, width, lead, earlier=()):
    total, lanes = own.shape
    rows = total // blocks
    span = (lanes - lead * width) // 3
    offset = 0 if lead else width // span - 1
    source = pl.BlockSpec((rows, lanes), lambda c, x: (x, 0))
    return pl.pallas_call(
        functools.partial(unpack_kernel, lead),
        grid=(2, blocks),
        in_specs=[pl.BlockSpec(memory_space=pltpu.SMEM), source, source]
        + [pl.BlockSpec(memory_space=pl.ANY)] * len(earlier),
        out_specs=[pl.BlockSpec((rows, width), lambda c, x: (2 * x + c, 0))] * lead
        + [pl.BlockSpec((rows, span), lambda c, x: (2 * x + c, offset))] * 3,
        out_shape=[jax.ShapeDtypeStruct((2 * total, width), F32)] * (3 + lead),
        input_output_aliases={3 + index: index for index in range(len(earlier))},
        compiler_params=params("arbitrary", "arbitrary"),
        cost_estimate=cost(COVER, 4096),
        name="unpack",
    )(upper, own, other, *earlier)


def swap(blocks, axis):
    return lax.all_to_all(blocks, axis, split_axis=0, concat_axis=0, tiled=True)


def after(value, *others):
    return lax.optimization_barrier((value,) + others)[0]


def trade(value, axis, bit):
    count = lax.axis_size(axis)
    return lax.ppermute(value, axis, [(place, place ^ bit) for place in range(count)])


def bits(axis):
    count, bit = lax.axis_size(axis), 1
    while bit < count:
        yield bit
        bit *= 2


def is_upper(axis, bit):
    return (lax.axis_index(axis) // bit) % 2


def rejoin(value, axis, bit):
    got = trade(value, axis, bit)
    upper = is_upper(axis, bit) == 1
    low = jnp.concatenate([value, got], axis=0)
    return jnp.where(upper, jnp.concatenate([got, value], axis=0), low)


def spread_out(value, axis):
    count = lax.axis_size(axis)
    copies = jnp.broadcast_to(value[None], (count,) + value.shape)
    return swap(copies, axis)


def narrow_part(shares):
    total = shares[0].astype(F32)
    for index, share in enumerate(shares[1:], 1):
        total = total + trade(share, "narrow", index).astype(F32)
    return total.astype(BF16)


def wide_part(value):
    width = value.shape[1]
    count = lax.axis_size("wide")
    parts = swap(value.reshape(count, -1, width), "wide")
    return jnp.sum(parts.astype(F32), axis=0).astype(value.dtype)


def wide_whole(value):
    return spread_out(value, "wide").reshape(-1, value.shape[1])


def outer_whole(value):
    for bit in list(bits("narrow"))[1:]:
        value = rejoin(value, "narrow", bit)
    return value


def axis_sum(value, axis):
    for bit in bits(axis):
        value = value + trade(value, axis, bit)
    return value


def per_device(
    tokens,
    grad_out,
    routes,
    group_counts,
    group_weights,
    norm1_gain,
    norm1_bias,
    w_query,
    bias_query,
    w_key,
    w_value,
    bias_value,
    w_out,
    bias_out,
    norm2_gain,
    norm2_bias,
    router,
    w_in,
    bias_in,
    w_down,
    bias_down,
):
    rows, width = tokens.shape
    experts = router.shape[1]
    assert rows == SEQ_LEN and w_in.shape[0] == 1
    hidden_cols = w_in.shape[2]
    wide_count = lax.axis_size("wide")
    narrow_count = lax.axis_size("narrow")
    devices = wide_count * narrow_count
    capacity = 2 * rows // experts
    half = capacity // 2
    total_tokens = rows * devices
    row = lambda vector: vector.reshape(1, -1)

    sequence = lax.axis_index(("wide", "narrow"))
    group_ends = jnp.cumsum(group_counts, dtype=jnp.int32)
    member = ((sequence >= group_ends - group_counts) & (sequence < group_ends)).astype(F32)
    factor = group_weights.astype(F32) * devices / (group_counts.shape[0] * group_counts.astype(F32))
    weight = jnp.sum(member * factor).reshape(1, 1)
    ids = routes.reshape(1, rows)
    router_rows = jnp.transpose(router)
    place = lax.axis_index("narrow").reshape(1, 1)

    slots, columns, grad_outgoing = route(routes, grad_out, experts, capacity)
    grad_rows = swap(grad_outgoing, "wide")
    gathered_in = lax.all_gather(w_in[0], "narrow", axis=0)
    gathered_down = lax.all_gather(w_down[0], "narrow", axis=0)

    normed_t, queries, keys, values = project(
        tokens, row(norm1_gain), row(norm1_bias), w_query, row(bias_query), w_key, w_value, row(bias_value)
    )
    context, soft_weights = attend(queries, keys, values)
    hidden, moe_in, logits = settle(
        context, tokens, w_out, row(bias_out), row(norm2_gain), row(norm2_bias), router_rows
    )
    first, second = dispatch(weight, slots, ids, logits, moe_in, capacity)
    gathered_bias = lax.all_gather(after(bias_in, first), "narrow", axis=0)
    x0 = swap(after(first, grad_rows), "wide")
    counted = jnp.sum(grad_rows[:, capacity, :experts].astype(F32), axis=0)
    fraction = axis_sum(counted, "narrow") / total_tokens
    pull = (BALANCE * experts * fraction).reshape(experts, 1)
    x1 = swap(after(second, x0, pull), "wide")
    act, up, out, back0, dots = expert(
        x0, grad_rows, gathered_in, gathered_bias, gathered_down, bias_down, 0
    )
    back0 = swap(after(back0, x1), "wide")
    act, up, expert_out, back1 = expert(
        x1, grad_rows, gathered_in, gathered_bias, gathered_down, bias_down, 1, (act, up, out, dots)
    )
    back1 = arrived = swap(after(back1, back0), "wide")
    scale = jnp.sum(x1[:, half : half + 3, :capacity].astype(F32), axis=1)
    scale = jnp.transpose(scale.reshape(wide_count, 2, half), (1, 0, 2)).reshape(2, 1, wide_count * half)
    down_sums, in_sums = weight_grads(after(x0, back0), x1, grad_rows, act, up, scale)
    in_grad = lax.psum_scatter(after(in_sums, arrived), "narrow", scatter_dimension=0)
    back1 = after(back1, in_sums)
    returned = swap(after(expert_out, arrived), "wide")

    extras = jnp.transpose(back1[:, half:, :half], (1, 0, 2))
    dots1 = jnp.pad(extras, ((0, 0), (0, 0), (0, EXTRA))).reshape(EXTRA, experts * (half + EXTRA))
    dots0 = jnp.concatenate([extras[3:], extras[:3]], axis=0).reshape(EXTRA, experts * half)
    hid_grad, con_grad, sums, router_grad, prob_sums, *out_grad = combine(
        weight,
        place,
        narrow_count,
        back0.reshape(experts * half, width),
        back1.reshape(experts * (half + EXTRA), width),
        dots0,
        dots1,
        columns,
        ids,
        logits,
        pull,
        hidden,
        grad_out,
        context,
        moe_in,
        w_out,
        router_rows,
        row(norm2_gain),
    )
    pairs = width // PAIR
    span = pairs // ATTEND_CALLS
    grads, bias_sums = [], []
    packed = [narrow_part(out_grad)]
    for call in range(ATTEND_CALLS):
        dq, dk, dv, column_sums, *weights = attend_back(
            queries,
            keys,
            values,
            soft_weights,
            con_grad,
            normed_t,
            place,
            narrow_count,
            call * span,
            span,
        )
        grads.append((dq, dk, dv))
        packed.append(narrow_part(weights))
        bias_sums.append(column_sums)
    early = jnp.concatenate(packed[:-1], axis=1)
    hid_grad = after(hid_grad, early)
    down_grad = lax.psum_scatter(after(down_sums, early, in_grad, column_sums), "narrow", scatter_dimension=0)
    grad_w_in, grad_w_down, grad_bias_in, grad_bias_down = unpack_expert(
        place, down_grad, in_grad, width // narrow_count
    )
    grad_tokens, norm_sums = close(grads, tokens, hid_grad, row(norm1_gain), w_query, w_key, w_value)
    block_out = block_output(
        returned.reshape(experts * capacity, width), columns, ids, logits, hidden
    )
    bias_sums = jnp.concatenate(bias_sums, axis=1)
    prob_row = jnp.pad(prob_sums.reshape(1, experts), ((0, 0), (0, width - experts)))
    small = jnp.concatenate([norm_sums[:2], bias_sums[:2], sums[:3], prob_row, router_grad], axis=0)
    small = axis_sum(small, "narrow")
    early = wide_part(after(early, returned))
    late = wide_part(after(packed[-1], early, small))
    small = axis_sum(small, "wide")
    early = wide_whole(after(early, late, small))
    late = wide_whole(after(late, early, grad_w_in, block_out))
    upper = is_upper("narrow", 1).astype(jnp.int32).reshape(1, 1)
    blocks = narrow_count // 2
    early = outer_whole(early)
    grad_w_out, *weights = unpack(upper, early, trade(early, "narrow", 1), blocks, width, 1)
    late = outer_whole(late)
    weights = unpack(upper, late, trade(late, "narrow", 1), blocks, width, 0, weights)
    balance_loss = experts * jnp.sum(fraction * (small[7, :experts] / total_tokens))
    return (
        block_out,
        balance_loss,
        grad_tokens,
        small[0],
        small[1],
        weights[0],
        small[2],
        weights[1],
        weights[2],
        small[3],
        grad_w_out,
        small[6],
        small[4],
        small[5],
        jnp.transpose(small[8:]),
        grad_w_in[None],
        grad_bias_in,
        grad_w_down[None],
        grad_bias_down,
    )


def solution(mesh):
    return jax.shard_map(
        per_device,
        mesh=mesh,
        in_specs=(
            P(("wide", "narrow"), None),
            P(("wide", "narrow"), None),
            P(("wide", "narrow"), None),
            P(),
            P(),
            P(),
            P(),
            P(),
            P(),
            P(),
            P(),
            P(),
            P(),
            P(),
            P(),
            P(),
            P(),
            P("wide", None, "narrow"),
            P("wide", "narrow"),
            P("wide", "narrow", None),
            P("wide", None),
        ),
        out_specs=(
            P(("wide", "narrow"), None),
            P(),
            P(("wide", "narrow"), None),
            P(),
            P(),
            P(),
            P(),
            P(),
            P(),
            P(),
            P(),
            P(),
            P(),
            P(),
            P(),
            P("wide", None, "narrow"),
            P("wide", "narrow"),
            P("wide", "narrow", None),
            P("wide", "narrow"),
        ),
        check_vma=False,
    )
```
